32 devices in a mesh: batch: 8 (over y, x, core), blk: 4 (over z).
Axes of the slice: x: 2, y: 2, z: 4, core: 2. Of those that a mesh axis runs over, the one named last changes fastest.
Arguments:
- hidden_in: bfloat16 [16, 1024, 1024], P('batch', 'blk'), may hold values from -6 to 6
- mask_index: int32 [16, 153], P('batch'), may hold values from 0 to 1023, as said below
- mask_count: int32 [16], P('batch'), may hold values from 76 to 153, as said below
- replacement: bfloat16 [16, 153, 1024], P('batch'), may hold values from -6 to 6
- out_grad: bfloat16 [16, 153, 1024], P('batch'), may hold values from -6 to 6
- w_qkv: bfloat16 [2, 1024, 3072], P(None, ('batch', 'blk')), may hold values from -0.1875 to 0.1875
- w_out: bfloat16 [2, 1024, 1024], P(None, ('batch', 'blk')), may hold values from -0.5 to 0.5
- w_up: bfloat16 [2, 1024, 4096], P(None, ('batch', 'blk')), may hold values from -0.1875 to 0.1875
- w_down: bfloat16 [2, 4096, 1024], P(None, ('batch', 'blk')), may hold values from -0.09375 to 0.09375
- biases: bfloat16 [2, 6, 1024], P(None, None, ('batch', 'blk')), may hold values from -1.1953125 to 1.1953125
- up_bias: bfloat16 [2, 4096], P(None, ('batch', 'blk')), may hold values from -1.1953125 to 1.1953125
- gains: bfloat16 [2, 2, 1024], P(None, None, ('batch', 'blk')), may hold values from 0.5 to 1.5
Outputs:
- output: bfloat16 [16, 1024, 1024], P('batch', 'blk')
- input_grad: float32 [16, 1024, 1024], P('batch', 'blk')
- grad_qkv: float32 [2, 1024, 3072], P(None, ('batch', 'blk'))
- grad_out: float32 [2, 1024, 1024], P(None, ('batch', 'blk'))
- grad_up: float32 [2, 1024, 4096], P(None, ('batch', 'blk'))
- grad_down: float32 [2, 4096, 1024], P(None, ('batch', 'blk'))
- grad_biases: float32 [2, 6, 1024], P(None, None, ('batch', 'blk'))
- grad_up_bias: float32 [2, 4096], P(None, ('batch', 'blk'))
- grad_gains: float32 [2, 2, 1024], P(None, None, ('batch', 'blk'))
The draws below stay inside these ranges and needn't reach their ends.
Inputs may be any that keep to these rules, and one draw needn't show every extreme that they name: `mask_index`: in each row the entries are distinct positions of the sequence; the first mask_count entries are the masked ones, the rest are padding, and the masked ones include a position in every aligned block of 256 positions. `mask_count`: some sequence has exactly 153.
All inputs are finite; a program needn't handle non-finite values.
Results may differ from the reference program's by a relative error of at most 0.029.
Values may be sent and summed in bfloat16 or wider, within the bound.
A program may use at most 448 MiB of HBM per device.

```python
import jax
import jax.numpy as jnp
from jax import lax

D = 1024
HEADS = 16
FF = 4096
LAYERS = 2
LENGTH = 1024
SEQUENCES = 16
BLOCK = 256
MASK_MAX = 153


def draw_mask_index(key, part):
    block_count = LENGTH // BLOCK

    def one_row(row_key):
        ranking = jax.random.permutation(row_key, LENGTH).astype(jnp.int32)
        block_rank = ranking.reshape(block_count, BLOCK)
        lowest = jnp.min(block_rank, axis=1, keepdims=True)
        adjusted = jnp.where(block_rank == lowest, block_rank - LENGTH, block_rank).reshape(LENGTH)
        picked = jnp.argsort(adjusted, stable=True)[:MASK_MAX]
        return picked.astype(jnp.int32)
    row_keys = jax.random.split(jax.random.fold_in(key, 11), SEQUENCES)
    return jax.vmap(one_row)(row_keys)


def draw_mask_count(key, part):
    lowest = max(MASK_MAX // 2, LENGTH // BLOCK)
    count_key = jax.random.fold_in(key, 23)
    top_key = jax.random.fold_in(key, 37)
    counts = jax.random.randint(count_key, (SEQUENCES,), lowest, MASK_MAX + 1).astype(jnp.int32)
    chosen = jax.random.randint(top_key, (), 0, SEQUENCES)
    return counts.at[chosen].set(MASK_MAX).astype(jnp.int32)


def level_of(key, extent, cuts, least, top_value):
    level = 1.0
    for axis_at, shards_of in cuts:
        steps = jax.random.uniform(jax.random.fold_in(jax.random.fold_in(key, 6), axis_at), (shards_of,), jnp.float32, least / len(cuts), top_value / len(cuts))
        level = level * jnp.repeat(jnp.exp(steps), extent[axis_at] // shards_of).reshape((-1,) + (1,) * (len(extent) - 1 - axis_at))
    return level


def scatter_about(stream_key, shape, scale, bound, shards=(), kind=jnp.bfloat16):
    drawn = scale * jax.random.normal(stream_key, shape, jnp.float32)
    if shards:
        drawn = drawn * level_of(stream_key, shape, shards, -0.22, 0.18)
    return jnp.clip(drawn, -bound, bound).astype(kind)


def setup_inputs(seed: int = 0) -> dict:
    key_list = jax.random.split(jax.random.key(seed), 13)
    return {
        "hidden_in": scatter_about(key_list[0], (SEQUENCES, LENGTH, D), 1.0, 6.0, ((0, 8), (1, 4))),
        "mask_index": draw_mask_index(jax.random.fold_in(key_list[12], 71), 0),
        "mask_count": draw_mask_count(jax.random.fold_in(key_list[12], 71), 0),
        "replacement": scatter_about(key_list[3], (SEQUENCES, MASK_MAX, D), 1.0, 6.0, ((0, 8),)),
        "out_grad": scatter_about(key_list[4], (SEQUENCES, MASK_MAX, D), 1.0, 6.0, ((0, 8),)),
        "w_qkv": scatter_about(key_list[5], (LAYERS, D, 3 * D), D ** -0.5, 0.1875, ((1, 32),)),
        "w_out": scatter_about(key_list[6], (LAYERS, D, D), (D // 8) ** -0.5, 0.5, ((1, 32),)),
        "w_up": scatter_about(key_list[7], (LAYERS, D, FF), D ** -0.5, 0.1875, ((1, 32),)),
        "w_down": scatter_about(key_list[8], (LAYERS, FF, D), FF ** -0.5, 0.09375, ((1, 32),)),
        "biases": scatter_about(key_list[9], (LAYERS, 6, D), 0.2, 1.1953125, ((2, 32),)),
        "up_bias": scatter_about(key_list[10], (LAYERS, FF), 0.2, 1.1953125, ((1, 32),)),
        "gains": jnp.clip(1.0 + 0.1 * jax.random.normal(key_list[11], (LAYERS, 2, D), jnp.float32), 0.5, 1.5).astype(jnp.bfloat16),
    }


NORM_EPS = 1e-12
SCORE_SCALE = 0.125

@jax.custom_vjp
def low(v):
    return lax.optimization_barrier(v.astype(jnp.bfloat16)).astype(jnp.float32)

@jax.custom_vjp
def low_back(v):
    return v

def low_keep(v):
    return (low(v), None)

def low_pass(kept, grad):
    return (grad,)

def back_keep(v):
    return (v, None)

def back_low(kept, grad):
    return (low(grad),)
low.defvjp(low_keep, low_pass)
low_back.defvjp(back_keep, back_low)

def dense(left, right):
    return jnp.dot(left, right, precision=lax.Precision.HIGHEST)

def layer_norm(values, gain, shift):
    center = values - lax.optimization_barrier(jnp.mean(values, -1, keepdims=True))
    spread = lax.optimization_barrier(jnp.mean(center * center, -1, keepdims=True))
    return center * lax.rsqrt(spread + NORM_EPS) * gain + shift

def gelu_exact(values):
    return 0.5 * values * (1.0 + jax.scipy.special.erf(values * 0.7071067811865476))

def attention(query, keys, values):
    row_block = min(512, LENGTH)

    def one_block(query_rows):
        scores = jnp.einsum('qhd,khd->hqk', query_rows, keys, precision=lax.Precision.HIGHEST)
        scores = low_back(scores * SCORE_SCALE)
        shifted = scores - lax.optimization_barrier(jnp.max(scores, -1, keepdims=True))
        expo = jnp.exp(shifted)
        probs = expo / lax.optimization_barrier(jnp.sum(expo, -1, keepdims=True))
        return jnp.einsum('hqk,khd->qhd', low(probs), values, precision=lax.Precision.HIGHEST)
    blocks = query.reshape(LENGTH // row_block, row_block, HEADS, D // HEADS)
    result = lax.map(jax.checkpoint(one_block), blocks)
    return result.reshape(LENGTH, D)

def one_layer(inputs, weights):
    qkv_weight, out_weight, up_weight, down_weight, bias_rows, up_shift, gain_rows = weights
    inputs_low = low(inputs)
    project = dense(inputs_low, qkv_weight)
    query = low(low_back(project[:, :D] + bias_rows[0]))
    keys = low(low_back(project[:, D:2 * D]))
    values = low(low_back(project[:, 2 * D:] + bias_rows[1]))
    shaped = (LENGTH, HEADS, D // HEADS)
    attended = attention(query.reshape(shaped), keys.reshape(shaped), values.reshape(shaped))
    attended = low(low_back(attended))
    mixed = inputs + low_back(dense(attended, out_weight) + bias_rows[2])
    normed = layer_norm(mixed, gain_rows[0], bias_rows[4])
    hidden = low_back(dense(low(normed), up_weight) + up_shift)
    active = low(gelu_exact(hidden))
    second = normed + low_back(dense(active, down_weight) + bias_rows[3])
    return layer_norm(second, gain_rows[1], bias_rows[5])

def network(inputs, weights):
    current = inputs
    for layer_idx in range(LAYERS):
        current = one_layer(current, tuple((item[layer_idx] for item in weights)))
    return current

def reference(hidden_in, mask_index, mask_count, replacement, out_grad, w_qkv, w_out, w_up, w_down, biases, up_bias, gains):
    weights = tuple((item.astype(jnp.float32) for item in (w_qkv, w_out, w_up, w_down, biases, up_bias, gains)))
    positions = jnp.arange(LENGTH, dtype=jnp.int32)
    slot_ids = jnp.arange(MASK_MAX, dtype=jnp.int32)

    def one_sequence(totals, item):
        hidden_seq, index_seq, count_seq, replace_seq, cotan_seq = item
        hit_table = ((index_seq[None, :] == positions[:, None]) & (slot_ids[None, :] < count_seq)).astype(jnp.float32)
        chosen = lax.optimization_barrier(jnp.sum(hit_table, -1, keepdims=True))
        placed = dense(hit_table, replace_seq.astype(jnp.float32))
        inputs = jnp.where(chosen > 0.5, placed, hidden_seq.astype(jnp.float32))
        result, pull = jax.vjp(network, inputs, weights)
        cotan_full = dense(hit_table, cotan_seq.astype(jnp.float32))
        inputs_grad, weight_grads = pull(cotan_full)
        totals = tuple((total + grad_part for total, grad_part in zip(totals, weight_grads)))
        return (totals, (result.astype(jnp.bfloat16), inputs_grad))
    start_totals = tuple((jnp.zeros(item.shape, jnp.float32) for item in weights))
    totals, (outputs, input_grads) = lax.scan(one_sequence, start_totals, (hidden_in, mask_index, mask_count, replacement, out_grad))
    return (outputs, input_grads, totals[0], totals[1], totals[2], totals[3], totals[4], totals[5], totals[6])
```

```python
import functools

import jax
import jax.numpy as jnp
from jax import lax
from jax.experimental import pallas as pl
from jax.experimental.pallas import tpu as pltpu
from jax.sharding import PartitionSpec as P

HEADS = 16


BOTH = ("batch", "blk")
NORM_EPS = 1e-12
SCORE_SCALE = 0.125


def norm_rows(values, gain, shift):
    center = values - jnp.mean(values, -1, keepdims=True)
    spread = jnp.mean(center * center, -1, keepdims=True)
    return center * lax.rsqrt(spread + NORM_EPS) * gain + shift


def gelu_exact(values):
    return 0.5 * values * (1.0 + jax.scipy.special.erf(values * 0.7071067811865476))


def forward_layer(inputs, fetched, head_shape):
    qkv_weight, out_weight, up_weight, down_weight, bias_rows, up_shift, gain_rows = fetched
    bias_rows = bias_rows.astype(jnp.float32)
    up_shift = up_shift.astype(jnp.float32)
    gain_rows = gain_rows.astype(jnp.float32)
    seq_count, block_len, head_count, head_dim = head_shape
    model_width = head_count * head_dim
    inputs_low = inputs.astype(jnp.bfloat16)
    project = jnp.einsum("sbd,de->sbe", inputs_low, qkv_weight, preferred_element_type=jnp.float32)
    query = (project[..., :model_width] + bias_rows[0]).astype(jnp.bfloat16).reshape(head_shape)
    keys = project[..., model_width : 2 * model_width].astype(jnp.bfloat16).reshape(head_shape)
    values = (
        (project[..., 2 * model_width :] + bias_rows[1]).astype(jnp.bfloat16).reshape(head_shape)
    )
    stat_shape = (seq_count, head_count, block_len)
    top_now = jnp.full(stat_shape, -1e30, jnp.float32)
    key_part = lax.all_gather(keys, "blk", axis=1, tiled=True)
    value_part = lax.all_gather(values, "blk", axis=1, tiled=True)
    scores = (
        jnp.einsum("sqhd,skhd->shqk", query, key_part, preferred_element_type=jnp.float32)
        * SCORE_SCALE
    )
    top_next = jnp.maximum(top_now, jnp.max(scores, -1))
    weights_now = jnp.exp(scores - top_next[..., None])
    total_next = jnp.sum(weights_now, -1)
    acc_next = jnp.einsum(
        "shqk,skhd->shqd",
        weights_now.astype(jnp.bfloat16),
        value_part,
        preferred_element_type=jnp.float32,
    )
    log_total = top_next + jnp.log(total_next)
    attended = (acc_next / total_next[..., None]).transpose(0, 2, 1, 3).reshape(inputs.shape)
    attended_low = attended.astype(jnp.bfloat16)
    mixed = (
        inputs
        + jnp.einsum("sbe,ed->sbd", attended_low, out_weight, preferred_element_type=jnp.float32)
        + bias_rows[2]
    )
    normed, first_pull = jax.vjp(norm_rows, mixed, gain_rows[0], bias_rows[4])
    normed_low = normed.astype(jnp.bfloat16)
    hidden = (
        jnp.einsum("sbd,df->sbf", normed_low, up_weight, preferred_element_type=jnp.float32)
        + up_shift
    )
    active, gelu_pull = jax.vjp(gelu_exact, hidden)
    active_low = active.astype(jnp.bfloat16)
    second = (
        normed
        + jnp.einsum("sbf,fd->sbd", active_low, down_weight, preferred_element_type=jnp.float32)
        + bias_rows[3]
    )
    result, second_pull = jax.vjp(norm_rows, second, gain_rows[1], bias_rows[5])
    kept = (
        inputs_low,
        query,
        keys,
        values,
        log_total,
        attended,
        attended_low,
        normed_low,
        active_low,
        first_pull,
        gelu_pull,
        second_pull,
    )
    return (result, kept)


def backward_layer(upstream, fetched, kept, head_shape):
    qkv_weight, out_weight, up_weight, down_weight = (
        fetched[0],
        fetched[1],
        fetched[2],
        fetched[3],
    )
    (
        inputs_low,
        query,
        keys,
        values,
        log_total,
        attended,
        attended_low,
        normed_low,
        active_low,
        first_pull,
        gelu_pull,
        second_pull,
    ) = kept
    seq_count, block_len, head_count, head_dim = head_shape
    row_axes = (0, 1)
    second_grad, gain_two, shift_two = second_pull(upstream)
    down_in = second_grad.astype(jnp.bfloat16)
    down_grad = jnp.einsum("sbf,sbd->fd", active_low, down_in, preferred_element_type=jnp.float32)
    down_shift = jnp.sum(down_in.astype(jnp.float32), row_axes)
    active_grad = jnp.einsum(
        "sbd,fd->sbf", down_in, down_weight, preferred_element_type=jnp.float32
    )
    hidden_grad = gelu_pull(active_grad)[0].astype(jnp.bfloat16)
    up_grad = jnp.einsum("sbd,sbf->df", normed_low, hidden_grad, preferred_element_type=jnp.float32)
    up_shift_grad = jnp.sum(hidden_grad.astype(jnp.float32), row_axes)
    normed_grad = second_grad + jnp.einsum(
        "sbf,df->sbd", hidden_grad, up_weight, preferred_element_type=jnp.float32
    )
    mixed_grad, gain_one, shift_one = first_pull(normed_grad)
    out_in = mixed_grad.astype(jnp.bfloat16)
    out_weight_grad = jnp.einsum(
        "sbe,sbd->ed", attended_low, out_in, preferred_element_type=jnp.float32
    )
    out_shift = jnp.sum(out_in.astype(jnp.float32), row_axes)
    attend_grad = (
        jnp.einsum("sbd,ed->sbe", out_in, out_weight, preferred_element_type=jnp.float32)
        .astype(jnp.bfloat16)
        .reshape(head_shape)
    )
    delta_rows = jnp.sum(attend_grad.astype(jnp.float32) * attended.reshape(head_shape), -1)
    lse_rows = log_total.transpose(0, 2, 1)
    lse_all, delta_all = (
        lax.all_gather(lse_rows, "blk", axis=1, tiled=True),
        lax.all_gather(delta_rows, "blk", axis=1, tiled=True),
    )
    delta_heads = delta_rows.transpose(0, 2, 1)
    key_part = lax.all_gather(keys, "blk", axis=1, tiled=True)
    value_part = lax.all_gather(values, "blk", axis=1, tiled=True)
    scores = (
        jnp.einsum("sqhd,skhd->shqk", query, key_part, preferred_element_type=jnp.float32)
        * SCORE_SCALE
    )
    probs = jnp.exp(scores - log_total[..., None])
    prob_grad = jnp.einsum(
        "sqhd,skhd->shqk", attend_grad, value_part, preferred_element_type=jnp.float32
    )
    score_grad = (probs * (prob_grad - delta_heads[..., None])).astype(jnp.bfloat16)
    query_grad = (
        jnp.einsum("shqk,skhd->sqhd", score_grad, key_part, preferred_element_type=jnp.float32)
        * SCORE_SCALE
    )
    query_part = lax.all_gather(query, "blk", axis=1, tiled=True)
    grad_part = lax.all_gather(attend_grad, "blk", axis=1, tiled=True)
    lse_part = lse_all.transpose(0, 2, 1)
    delta_part = delta_all.transpose(0, 2, 1)
    scores = (
        jnp.einsum("sqhd,skhd->shqk", query_part, keys, preferred_element_type=jnp.float32)
        * SCORE_SCALE
    )
    probs = jnp.exp(scores - lse_part[..., None])
    value_acc = jnp.einsum(
        "shqk,sqhd->skhd", probs.astype(jnp.bfloat16), grad_part, preferred_element_type=jnp.float32
    )
    prob_grad = jnp.einsum("sqhd,skhd->shqk", grad_part, values, preferred_element_type=jnp.float32)
    score_grad = (probs * (prob_grad - delta_part[..., None])).astype(jnp.bfloat16)
    key_acc = (
        jnp.einsum("shqk,sqhd->skhd", score_grad, query_part, preferred_element_type=jnp.float32)
        * SCORE_SCALE
    )
    flat_shape = (seq_count, block_len, head_count * head_dim)
    query_low = query_grad.reshape(flat_shape).astype(jnp.bfloat16)
    key_low = key_acc.reshape(flat_shape).astype(jnp.bfloat16)
    value_low = value_acc.reshape(flat_shape).astype(jnp.bfloat16)
    proj_grad = jnp.concatenate((query_low, key_low, value_low), -1)
    qkv_grad = jnp.einsum("sbd,sbe->de", inputs_low, proj_grad, preferred_element_type=jnp.float32)
    query_shift = jnp.sum(query_low.astype(jnp.float32), row_axes)
    value_shift = jnp.sum(value_low.astype(jnp.float32), row_axes)
    inputs_grad = mixed_grad + jnp.einsum(
        "sbe,de->sbd", proj_grad, qkv_weight, preferred_element_type=jnp.float32
    )
    shift_rows = jnp.stack((query_shift, value_shift, out_shift, down_shift, shift_one, shift_two))
    gain_grad = jnp.stack((gain_one, gain_two))
    return (
        inputs_grad,
        (qkv_grad, out_weight_grad, up_grad, down_grad, shift_rows, up_shift_grad, gain_grad),
    )


def general_shards(
    hidden_in,
    mask_index,
    mask_count,
    replacement,
    out_grad,
    w_qkv,
    w_out,
    w_up,
    w_down,
    biases,
    up_bias,
    gains,
):
    seq_count, block_len, model_width = hidden_in.shape
    layer_count = w_qkv.shape[0]
    head_shape = (seq_count, block_len, HEADS, model_width // HEADS)
    offset = lax.axis_index("blk") * block_len
    places = offset + jnp.arange(block_len, dtype=jnp.int32)
    slot_ids = jnp.arange(mask_index.shape[1], dtype=jnp.int32)
    hit_table = (mask_index[:, None, :] == places[None, :, None]) & (
        slot_ids[None, None, :] < mask_count[:, None, None]
    )
    hit_low = hit_table.astype(jnp.bfloat16)
    chosen = jnp.any(hit_table, -1, keepdims=True)
    placed = jnp.einsum("sbm,smd->sbd", hit_low, replacement, preferred_element_type=jnp.float32)
    current = jnp.where(chosen, placed, hidden_in.astype(jnp.float32))
    upstream = jnp.einsum("sbm,smd->sbd", hit_low, out_grad, preferred_element_type=jnp.float32)
    shard_shapes = (w_qkv.shape[1:], w_out.shape[1:], w_up.shape[1:], w_down.shape[1:])
    saved_weights = []
    saved_state = []
    for layer_idx in range(layer_count):
        fetched = (
            lax.all_gather(w_qkv[layer_idx], BOTH, axis=0, tiled=True),
            lax.all_gather(w_out[layer_idx], BOTH, axis=0, tiled=True),
            lax.all_gather(w_up[layer_idx], BOTH, axis=0, tiled=True),
            lax.all_gather(w_down[layer_idx], BOTH, axis=0, tiled=True),
            lax.all_gather(biases[layer_idx], BOTH, axis=1, tiled=True),
            lax.all_gather(up_bias[layer_idx], BOTH, axis=0, tiled=True),
            lax.all_gather(gains[layer_idx], BOTH, axis=1, tiled=True),
        )
        saved_weights.append(None)
        current, state = forward_layer(current, fetched, head_shape)
        saved_state.append(state)
    grad_now = upstream
    summed = [None] * layer_count
    for layer_idx in reversed(range(layer_count)):
        fetched = (
            lax.all_gather(w_qkv[layer_idx], BOTH, axis=0, tiled=True),
            lax.all_gather(w_out[layer_idx], BOTH, axis=0, tiled=True),
            lax.all_gather(w_up[layer_idx], BOTH, axis=0, tiled=True),
            lax.all_gather(w_down[layer_idx], BOTH, axis=0, tiled=True),
            lax.all_gather(biases[layer_idx], BOTH, axis=1, tiled=True),
            lax.all_gather(up_bias[layer_idx], BOTH, axis=0, tiled=True),
            lax.all_gather(gains[layer_idx], BOTH, axis=1, tiled=True),
        )
        grad_now, terms = backward_layer(grad_now, fetched, saved_state[layer_idx], head_shape)
        flat_terms = (
            terms[0].reshape(-1, 128),
            terms[1].reshape(-1, 128),
            terms[2].reshape(-1, 128),
            terms[3].reshape(-1, 128),
            terms[4],
            terms[5],
            terms[6],
        )
        reduced = (
            lax.psum_scatter(flat_terms[0], BOTH, scatter_dimension=0, tiled=True),
            lax.psum_scatter(flat_terms[1], BOTH, scatter_dimension=0, tiled=True),
            lax.psum_scatter(flat_terms[2], BOTH, scatter_dimension=0, tiled=True),
            lax.psum_scatter(flat_terms[3], BOTH, scatter_dimension=0, tiled=True),
            lax.psum_scatter(flat_terms[4], BOTH, scatter_dimension=1, tiled=True),
            lax.psum_scatter(flat_terms[5], BOTH, scatter_dimension=0, tiled=True),
            lax.psum_scatter(flat_terms[6], BOTH, scatter_dimension=1, tiled=True),
        )
        summed[layer_idx] = tuple(
            (reduced[member].reshape(shard_shapes[member]) for member in range(4))
        ) + tuple(reduced[4:])
    stacked = [jnp.stack([entry[member] for entry in summed]) for member in range(7)]
    return (
        current.astype(jnp.bfloat16),
        grad_now,
        stacked[0],
        stacked[1],
        stacked[2],
        stacked[3],
        stacked[4],
        stacked[5],
        stacked[6],
    )


NT = (((1,), (1,)), ((), ()))
TN = (((0,), (0,)), ((), ()))
F32 = jnp.float32
BF = jnp.bfloat16


def dot(a, b, dims):
    return lax.dot_general(a, b, dims, preferred_element_type=F32)


MESH = pl.DeviceIdType.MESH
UNITS = 12
TILE = 256
LAGS = (3, 2, 4, 5)
DIRECT = 8


def place_of():
    batch = lax.axis_index("batch")
    return batch, lax.axis_index("blk"), batch // 4, lax.rem(batch // 2, 2), lax.rem(batch, 2)


def columns(tile):
    return pl.ds(pl.multiple_of(tile * TILE, TILE), TILE)


def forward_kernel(
    first_ref,
    qkv_in,
    out_in,
    up_in,
    down_in,
    small_ref,
    w_ref,
    out_ref,
    rows_ref,
    lse_ref,
    low_ref,
    qkv_ref,
    kv_ref,
    mix_ref,
    nrm_ref,
    act_ref,
    slope_ref,
    unit_ref,
    scale_ref,
    cur,
    low,
    qkv,
    sib,
    mix,
    nrm,
    acc,
    act,
    slope,
    unit,
    scale,
    wbuf,
    shard,
    small_all,
    local_sems,
    own_sems,
    save_sems,
    send_sems,
    recv_sems,
    side_send,
    side_recv,
    turn_send,
    turn_recv,
    layers,
):
    batch, z, y, x, core = place_of()
    total = layers * UNITS
    yx = 2 * y + x
    column = 4 * y + 2 * x
    here = {"x": (batch ^ 2, z), "y": (batch ^ 4, z), "core": (batch ^ 1, z)}

    def remote(src, dst, send, recv, device):
        return pltpu.make_async_remote_copy(
            src_ref=src,
            dst_ref=dst,
            send_sem=send,
            recv_sem=recv,
            device_id=device,
            device_id_type=MESH,
        )

    flying = {}

    def launch(kind, unit_id, copies):
        flying[kind, unit_id] = copies
        for copy in copies:
            copy.start()

    def landed(kind, unit_id):
        for copy in flying[kind, unit_id]:
            copy.wait_recv()

    def hop(unit_id, slot, src, dst, device):
        return remote(src, dst, send_sems.at[unit_id, slot], recv_sems.at[unit_id, slot], device)

    own_rows = pl.ds(pl.multiple_of(z * 32, 32), 32)

    def straight(unit_id):
        return 1024 if unit_id < DIRECT else 1024 - 128

    def along(unit_id):
        cols = pl.ds(0, straight(unit_id))
        dst = w_ref.at[unit_id, yx, core, own_rows, cols]
        src = shard.at[unit_id, :, cols]
        copies = []
        if unit_id >= DIRECT:
            edge = pl.ds(1024 - 128, 128)
            piece, spot = shard.at[unit_id, :, edge], w_ref.at[unit_id, yx, core, own_rows, edge]
            copies += [hop(unit_id, 8, piece, spot, here["x"]), hop(unit_id, 9, piece, spot, here["y"])]
        for step in (1, 2, 3):
            copies.append(hop(unit_id, step - 1, src, dst, (batch, lax.rem(z + step, 4))))
        return copies

    def across(unit_id):
        line = w_ref.at[unit_id, yx, core, :, pl.ds(0, straight(unit_id))]
        copies = []
        if unit_id >= DIRECT:
            edge = pl.ds(1024 - 128, 128)
            if unit_id % 2:
                piece, to = w_ref.at[unit_id, 2 * y + 1 - x, core, own_rows, edge], here["y"]
            else:
                piece, to = w_ref.at[unit_id, 2 - 2 * y + x, core, own_rows, edge], here["x"]
            copies.append(hop(unit_id, 10, piece, piece, to))
        copies += [hop(unit_id, 3, line, line, here["x"]), hop(unit_id, 4, line, line, here["y"])]
        return copies

    def corner(unit_id):
        full = straight(unit_id)
        half = 384 if full < 1024 and unit_id % 2 else 512
        left = w_ref.at[unit_id, 2 * y + 1 - x, core, :, pl.ds(0, half)]
        right = w_ref.at[unit_id, 2 - 2 * y + x, core, :, pl.ds(half, full - half)]
        copies = []
        if unit_id >= DIRECT:
            block = w_ref.at[unit_id, :, core, own_rows, pl.ds(1024 - 128, 128)]
            for step in (1, 2, 3):
                to = (batch, lax.rem(z + step, 4))
                copies.append(hop(unit_id, 10 + step, block, block, to))
        copies += [hop(unit_id, 5, left, left, here["y"]), hop(unit_id, 6, right, right, here["x"])]
        return copies

    def inner(unit_id):
        block = w_ref.at[unit_id, :, core]
        return [hop(unit_id, 7, block, block, here["core"])]

    def side(slot, src, dst, device):
        return remote(src, dst, side_send.at[slot], side_recv.at[slot], device)

    def layout(layer):
        base = layer * UNITS
        for part in range(3):
            shard[base + part] = qkv_in[layer, :, part * 1024 : part * 1024 + 1024]
        shard[base + 3] = out_in[layer]
        lane = lax.broadcasted_iota(jnp.int32, (32, 128), 1) // 32
        for j in range(4):
            shard[base + 5 + 2 * j] = down_in[layer, j * 32 : j * 32 + 32]
            for block in range(8):
                made = None
                for part in range(4):
                    start = (4 * block + part) * 128
                    value = up_in[layer, :, start : start + 128].astype(F32)
                    if part != j:
                        value = pltpu.roll(value, ((part - j) * 32) % 128, 1)
                    made = value if made is None else jnp.where(lane == part, value, made)
                shard[base + 4 + 2 * j, :, block * 128 : block * 128 + 128] = made.astype(BF)

    owns = [
        pltpu.make_async_copy(
            shard.at[unit_id], w_ref.at[unit_id, yx, core, own_rows], own_sems.at[unit_id]
        )
        for unit_id in range(total)
    ]
    mine = small_all.at[y, x, core, z]
    mine[...] = small_ref[...]
    launch(
        "small",
        0,
        [side(step - 1, small_ref, mine, (batch, lax.rem(z + step, 4))) for step in (1, 2, 3)],
    )

    def turn(j, half):
        to = 2 * core + j
        block = lax.rem(to - z + 4, 4)
        src = first_ref.at[j, pl.ds(half * 128, 128)]
        dst = low.at[pl.ds(pl.multiple_of(block * 128, 128), 128)]
        send, recv = turn_send.at[2 * j + half], turn_recv.at[block]
        return (
            lambda: pltpu.make_async_copy(src, dst, local_sems.at[0]),
            lambda: remote(src, dst, send, recv, (column + half, to)),
            jnp.logical_and(to == z, core == half),
        )

    def turned(block):
        spot = low.at[pl.ds(block * 128, 128)]
        return remote(spot, spot, turn_send.at[0], turn_recv.at[block], here["core"])

    for layer in range(layers):
        layout(layer)
        if layer == 0:
            for unit_id in range(2):
                owns[unit_id].start()
                launch("along", unit_id, along(unit_id))
            for j in range(2):
                for half in range(2):
                    local, away, stays = turn(j, half)
                    pl.when(stays)(lambda: local().start())
                    pl.when(jnp.logical_not(stays))(lambda: away().start())
            for unit_id in range(2, LAGS[0]):
                owns[unit_id].start()
                launch("along", unit_id, along(unit_id))
    own_turn = core == z // 2

    def small_hop(number):
        landed("small", number - 1)
        if number == 1:
            line = small_all.at[y, x, core]
            launch("small", 1, [side(3, line, line, here["x"])])
        elif number == 2:
            plane = small_all.at[y, :, core]
            launch("small", 2, [side(4, plane, plane, here["y"])])
        elif number == 3:
            cube = small_all.at[:, :, core]
            launch("small", 3, [side(5, cube, cube, here["core"])])

    def begin():
        small_hop(4)
        for block in range(8):
            four = small_all[block // 4, (block // 2) % 2, block % 2]
            rows_ref[:, block * 128 : block * 128 + 128] = (four[0] + four[1]) + (four[2] + four[3])
        local = turn(0, 0)[0]
        pl.when(own_turn)(lambda: local().wait())
        pl.when(jnp.logical_not(own_turn))(lambda: turned(0).wait_recv())
        for block in range(1, 4):
            turned(block).wait_recv()

        def body(step, carry):
            rows = pl.ds(pl.multiple_of(step * 64, 64), 64)
            cur[rows] = low[rows].astype(F32)
            return carry

        lax.fori_loop(0, 8, body, 0)

    saves = {}

    def save(name, src, dst, slot):
        if name in saves:
            saves[name].wait()
        saves[name] = pltpu.make_async_copy(src, dst, save_sems.at[slot])
        saves[name].start()

    def settle(*names):
        for name in names:
            if name in saves:
                saves.pop(name).wait()

    def weight(tile):
        return wbuf[:, :, :, columns(tile)].reshape(1024, TILE)

    def norm(layer, which, gain_row, shift_row):
        gain = rows_ref[pl.ds(gain_row, 1)]
        shift_by = rows_ref[pl.ds(shift_row, 1)]

        def body(step, carry):
            rows = pl.ds(step * 64, 64)
            value = acc[rows]
            center = value - jnp.mean(value, -1, keepdims=True)
            spread = jnp.mean(center * center, -1, keepdims=True)
            root = lax.rsqrt(spread + NORM_EPS)
            normal = center * root
            unit[which, rows] = normal
            scale[which, rows] = jnp.broadcast_to(root, (64, 128))
            result = normal * gain + shift_by
            if which == 0:
                acc[rows] = result + rows_ref[pl.ds(layer * 12 + 3, 1)]
                nrm[rows] = result.astype(BF)
            else:
                cur[rows] = result
                low[rows] = result.astype(BF)
            return carry

        lax.fori_loop(0, 8, body, 0)
        save(("unit", which), unit.at[which], unit_ref.at[layer, which], 8 + which)
        save(("scale", which), scale.at[which], scale_ref.at[layer, which], 10 + which)

    def heads(layer, begin, end):
        def body(j, carry):
            lanes = pl.ds(pl.multiple_of(j * 128, 128), 128)
            k_lanes = pl.ds(pl.multiple_of(1024 + j * 128, 128), 128)
            v_lanes = pl.ds(pl.multiple_of(2048 + j * 128, 128), 128)
            q = qkv[:, lanes]
            lane = lax.broadcasted_iota(jnp.int32, q.shape, 1)
            outs = []
            for head in range(2):
                qh = jnp.where((lane // 64) == head, q, jnp.zeros_like(q))
                s_own = dot(qkv[:, k_lanes], qh, NT)
                s_sib = dot(sib[layer, 0, :, lanes], qh, NT)
                top = jnp.maximum(
                    jnp.max(s_own, 0, keepdims=True), jnp.max(s_sib, 0, keepdims=True)
                )
                p_own = jnp.exp(s_own - top)
                p_sib = jnp.exp(s_sib - top)
                mass = jnp.sum(p_own, 0, keepdims=True) + jnp.sum(p_sib, 0, keepdims=True)
                lse_ref[layer, j, pl.ds(head, 1)] = top + jnp.log(mass)
                o = dot(qkv[:, v_lanes], p_own.astype(BF), TN) + dot(
                    sib[layer, 1, :, lanes], p_sib.astype(BF), TN
                )
                outs.append(o[head * 64 : head * 64 + 64] / mass)
            mix[:, lanes] = jnp.transpose(jnp.concatenate(outs, 0)).astype(BF)
            return carry

        lax.fori_loop(begin, end, body, 0)

    def compute(unit_id):
        layer, kind = unit_id // UNITS, unit_id % UNITS
        base = layer * 12
        fetch = pltpu.make_async_copy(w_ref.at[unit_id], wbuf, local_sems.at[3])
        fetch.start()
        if kind == 0:
            save("low", low, low_ref.at[layer], 0)
        if kind == 3:
            heads(layer, 4, 8)
            save("mix", mix, mix_ref.at[layer], 3)
        fetch.wait()
        if kind < 3:
            bias = rows_ref[pl.ds(base + (0 if kind == 0 else 1), 1)]
            if kind == 0:
                settle("qkv")
            for copy in flying.pop(("kv", (layer - 1, kind)), ()):
                copy.wait_send()

            def body(tile, carry):
                value = jnp.dot(low[...], weight(tile), preferred_element_type=F32)
                cols = columns(tile)
                if kind != 1:
                    value = value + rows_ref[pl.ds(base + kind // 2, 1), cols]
                value = value.astype(BF)
                if kind == 0:
                    value = (value.astype(F32) * SCORE_SCALE).astype(BF)
                qkv[:, columns(tile + 4 * kind)] = value
                return carry

            lax.fori_loop(0, 4, body, 0)
            if kind:
                launch(
                    "kv",
                    (layer, kind),
                    [
                        side(
                            6 + 2 * layer + kind - 1,
                            qkv.at[:, pl.ds(1024 * kind, 1024)],
                            sib.at[layer, kind - 1],
                            here["core"],
                        )
                    ],
                )
            if kind == 2:
                save("qkv", qkv, qkv_ref.at[layer], 1)
                landed("kv", (layer, 1))
                landed("kv", (layer, 2))
                save("kv", sib.at[layer], kv_ref.at[layer], 2)
                settle("mix")
                heads(layer, 0, 4)
        elif kind == 3:
            settle("nrm", ("unit", 0), ("scale", 0))

            def body(tile, carry):
                cols = columns(tile)
                value = jnp.dot(mix[...], weight(tile), preferred_element_type=F32)
                acc[:, cols] = cur[:, cols] + value + rows_ref[pl.ds(base + 2, 1), cols]
                return carry

            lax.fori_loop(0, 4, body, 0)
            norm(layer, 0, base + 6, base + 4)
            save("nrm", nrm, nrm_ref.at[layer], 4)
        elif kind % 2 == 0:
            j = kind // 2 - 2
            settle(("act", j), ("slope", j))

            def body(tile, carry):
                cols = columns(tile)
                value = jnp.dot(nrm[...], weight(tile), preferred_element_type=F32)
                value = value + rows_ref[pl.ds(base + 8 + j, 1), cols]
                gate = 0.5 * (1.0 + lax.erf(value * 0.7071067811865476))
                act[j, :, cols] = (value * gate).astype(BF)
                bell = jnp.exp(-0.5 * value * value)
                slope[j, :, cols] = (gate + value * (0.3989422804014327 * bell)).astype(BF)
                return carry

            lax.fori_loop(0, 4, body, 0)
            save(("act", j), act.at[j], act_ref.at[layer, j], 12 + j)
            save(("slope", j), slope.at[j], slope_ref.at[layer, j], 16 + j)
        else:
            j = kind // 2 - 2

            def body(tile, carry):
                cols = columns(tile)
                acc[:, cols] += jnp.dot(act[j], weight(tile), preferred_element_type=F32)
                return carry

            lax.fori_loop(0, 4, body, 0)
            if j == 3:
                settle("low", ("unit", 1), ("scale", 1))
                norm(layer, 1, base + 7, base + 5)
                if layer == layers - 1:
                    save("low", low, out_ref, 0)

    ahead, corner_lag, inner_lag, use_lag = LAGS
    for step in range(total + use_lag):
        if step + ahead < total:
            owns[step + ahead].start()
            launch("along", step + ahead, along(step + ahead))
        if step < total:
            owns[step].wait()
            landed("along", step)
            launch("across", step, across(step))
        if 0 < step < 4:
            small_hop(step)
        if 0 <= step - corner_lag < total:
            landed("across", step - corner_lag)
            launch("corner", step - corner_lag, corner(step - corner_lag))
        if 0 <= step - inner_lag < total:
            landed("corner", step - inner_lag)
            launch("inner", step - inner_lag, inner(step - inner_lag))
        if step == use_lag:
            begin()
        if 0 <= step - use_lag < total:
            landed("inner", step - use_lag)
            compute(step - use_lag)
    for j in range(2):
        for half in range(2):
            local, away, stays = turn(j, half)
            pl.when(jnp.logical_not(stays))(lambda: away().wait_send())
    for copies in flying.values():
        for copy in copies:
            copy.wait_send()
    settle(*list(saves))


def forward_pass(first, w_qkv, w_out, w_up, w_down, small):
    layers = w_qkv.shape[0]
    width = first.shape[2]
    rows = first.shape[0] * first.shape[1]
    any_spec = pl.BlockSpec(memory_space=pl.ANY)
    vmem = pl.BlockSpec(memory_space=pltpu.VMEM)
    shape = jax.ShapeDtypeStruct
    total = layers * UNITS
    return pl.pallas_call(
        functools.partial(forward_kernel, layers=layers),
        in_specs=[vmem] * 6,
        out_specs=[any_spec, any_spec, vmem, vmem] + [any_spec] * 9,
        out_shape=[
            shape((total, 4, 2, 128, width), BF),
            shape((rows, width), BF),
            shape((layers * 12, width), F32),
            shape((layers, 8, 2, rows), F32),
            shape((layers, rows, width), BF),
            shape((layers, rows, 3 * width), BF),
            shape((layers, 2, rows, width), BF),
            shape((layers, rows, width), BF),
            shape((layers, rows, width), BF),
            shape((layers, 4, rows, width), BF),
            shape((layers, 4, rows, width), BF),
            shape((layers, 2, rows, width), F32),
            shape((layers, 2, rows, 128), F32),
        ],
        scratch_shapes=[
            pltpu.VMEM((rows, width), F32),
            pltpu.VMEM((rows, width), BF),
            pltpu.VMEM((rows, 3 * width), BF),
            pltpu.VMEM((layers, 2, rows, width), BF),
            pltpu.VMEM((rows, width), BF),
            pltpu.VMEM((rows, width), BF),
            pltpu.VMEM((rows, width), F32),
            pltpu.VMEM((4, rows, width), BF),
            pltpu.VMEM((4, rows, width), BF),
            pltpu.VMEM((2, rows, width), F32),
            pltpu.VMEM((2, rows, 128), F32),
            pltpu.VMEM((4, 2, 128, width), BF),
            pltpu.VMEM((total, 32, width), BF),
            pltpu.VMEM((2, 2, 2, 4, layers * 12, 128), F32),
            pltpu.SemaphoreType.DMA((4,)),
            pltpu.SemaphoreType.DMA((total,)),
            pltpu.SemaphoreType.DMA((20,)),
            pltpu.SemaphoreType.DMA((total, 14)),
            pltpu.SemaphoreType.DMA((total, 14)),
            pltpu.SemaphoreType.DMA((6 + 2 * layers,)),
            pltpu.SemaphoreType.DMA((6 + 2 * layers,)),
            pltpu.SemaphoreType.DMA((4,)),
            pltpu.SemaphoreType.DMA((4,)),
        ],
        compiler_params=pltpu.CompilerParams(
            has_side_effects=True, vmem_limit_bytes=60 << 20
        ),
        name="forward_pass",
    )(first, w_qkv, w_out, w_up, w_down, small)


def backward_kernel(
    top_ref,
    last_ref,
    w_ref,
    rows_ref,
    lse_ref,
    low_ref,
    qkv_ref,
    kv_ref,
    mix_ref,
    nrm_ref,
    act_ref,
    slope_ref,
    unit_ref,
    scale_ref,
    last_out,
    grad_out,
    qkv_out,
    out_out,
    up_out,
    down_out,
    bias_out,
    up_bias_out,
    gain_out,
    grad,
    edge,
    unit,
    scale,
    arena,
    span,
    feat,
    turned,
    wbuf,
    send,
    mine,
    land,
    wide,
    slim,
    ends,
    small_all,
    small_in,
    staged,
    up_all,
    load_sems,
    store_sems,
    send_sems,
    recv_sems,
    side_send,
    side_recv,
    turn_send,
    turn_recv,
    layers,
):
    batch, z, y, x, core = place_of()
    total = layers * UNITS
    here = {"x": (batch ^ 2, z), "y": (batch ^ 4, z), "core": (batch ^ 1, z)}
    slots = 6

    def remote(src, dst, send_sem, recv_sem, device):
        return pltpu.make_async_remote_copy(
            src_ref=src,
            dst_ref=dst,
            send_sem=send_sem,
            recv_sem=recv_sem,
            device_id=device,
            device_id_type=MESH,
        )

    incoming, outgoing = {}, {}

    def launch(kind, number, copies):
        incoming[kind, number] = copies
        outgoing[kind, number] = copies
        for copy in copies:
            copy.start()

    def landed(kind, number):
        for copy in incoming.pop((kind, number)):
            copy.wait_recv()

    def sent(kind, number):
        for copy in outgoing.pop((kind, number), ()):
            copy.wait_send()

    def hop(number, slot, src, dst, device):
        return remote(src, dst, send_sems.at[number, slot], recv_sems.at[number, slot], device)

    def side(slot, src, dst, device):
        return remote(src, dst, side_send.at[slot], side_recv.at[slot], device)

    loads = {}

    def fetch(name, src, dst, slot):
        loads[name] = pltpu.make_async_copy(src, dst, load_sems.at[slot])
        loads[name].start()

    def ready(name):
        loads.pop(name).wait()

    order = []
    for layer in reversed(range(layers)):
        for j in range(4):
            order += [layer * UNITS + 5 + 2 * j, layer * UNITS + 4 + 2 * j]
        order += [layer * UNITS + 3, layer * UNITS, layer * UNITS + 1, layer * UNITS + 2]

    def fetch_weight(number):
        if number < total:
            fetch(("w", number), w_ref.at[order[number]], wbuf.at[number % 2], number % 2)

    def rows_of(number, tile):
        return wbuf[number % 2, tile].reshape(TILE, 1024)

    def turn(slot, source):
        def body(block, carry):
            rows = pl.ds(pl.multiple_of(block * 128, 128), 128)
            for half, which in enumerate((core, 1 - core)):
                lanes = pl.ds(pl.multiple_of(block * 256 + which * 128, 128), 128)
                turned[slot, half, rows] = jnp.transpose(source[:, lanes])
            return carry

        lax.fori_loop(0, 4, body, 0)

    def produce(number, slot, upper):
        buffer = number % 2
        sent("core", number - 2)

        def body(tile, carry):
            cols = columns(tile)
            value = jnp.dot(turned[slot, 1], upper[:, cols], preferred_element_type=F32)
            send[buffer, :, :, cols] = value.astype(BF).reshape(4, 128, TILE)
            return carry

        lax.fori_loop(0, 4, body, 0)
        launch("core", number, [hop(number, 0, send.at[buffer], land.at[number % UNITS], here["core"])])

        def own(tile, carry):
            cols = columns(tile)
            value = jnp.dot(turned[slot, 0], upper[:, cols], preferred_element_type=F32)
            mine[number % slots, :, :, cols] = value.astype(BF).reshape(4, 128, TILE)
            return carry

        lax.fori_loop(0, 4, own, 0)

    left, right = pl.ds(0, 512), pl.ds(512, 512)

    def stage_core(number):
        part = land.at[number % UNITS]
        landed("core", number)

        def body(block, carry):
            part[block] = (part[block].astype(F32) + mine[number % slots, block].astype(F32)).astype(BF)
            return carry

        lax.fori_loop(0, 4, body, 0)
        spot = number % slots
        launch(
            "wide",
            number,
            [
                hop(number, 1, part.at[pl.ds(2 - 2 * y, 2), :, left], wide.at[spot, 0], here["y"]),
                hop(number, 2, part.at[pl.ds(1 - x, 1), :, right], wide.at[spot, 1, pl.ds(0, 1)], here["x"]),
                hop(number, 3, part.at[pl.ds(3 - x, 1), :, right], wide.at[spot, 1, pl.ds(1, 1)], here["x"]),
            ],
        )

    def stage_wide(number):
        part, spot = land.at[number % UNITS], number % slots
        landed("wide", number)
        for block in range(2):
            spot_y = 2 * y + block
            value = part[spot_y, :, left].astype(F32) + wide[spot, 0, block].astype(F32)
            part[spot_y, :, left] = value.astype(BF)
            spot_x = 2 * block + x
            value = part[spot_x, :, right].astype(F32) + wide[spot, 1, block].astype(F32)
            part[spot_x, :, right] = value.astype(BF)
        launch(
            "slim",
            number,
            [
                hop(number, 4, part.at[2 * y + 1 - x, :, left], slim.at[spot, 0], here["x"]),
                hop(number, 5, part.at[2 - 2 * y + x, :, right], slim.at[spot, 1], here["y"]),
            ],
        )

    def stage_slim(number):
        part, spot = land.at[number % UNITS, 2 * y + x], number % slots
        landed("slim", number)
        part[:, left] = (part[:, left].astype(F32) + slim[spot, 0].astype(F32)).astype(BF)
        part[:, right] = (part[:, right].astype(F32) + slim[spot, 1].astype(F32)).astype(BF)
        copies = []
        for step in (1, 2, 3):
            to = lax.rem(z + step, 4)
            src = part.at[pl.ds(pl.multiple_of(to * 32, 32), 32)]
            copies.append(hop(number, 5 + step, src, ends.at[spot, step - 1], (batch, to)))
        launch("ends", number, copies)

    def stage_ends(number):
        part, spot = land.at[number % UNITS, 2 * y + x], number % slots
        landed("ends", number)
        value = part[pl.ds(pl.multiple_of(z * 32, 32), 32)].astype(F32)
        for step in range(3):
            value = value + ends[spot, step].astype(F32)
        layer, kind = order[number] // UNITS, order[number] % UNITS
        j = kind // 2 - 2
        if kind > 3 and kind % 2 == 0:
            lane = lax.broadcasted_iota(jnp.int32, (32, 128), 1) // 32
            if j == 0 and 4 in stores:
                stores.pop(4).wait()
            for block in range(32):
                spot = pl.ds(block * 128, 128)
                piece = value[:, block // 4 * 128 : block // 4 * 128 + 128]
                if j != block % 4:
                    piece = pltpu.roll(piece, ((j - block % 4) * 32) % 128, 1)
                up_all[:, spot] = piece if j == 0 else jnp.where(lane == j, piece, up_all[:, spot])
            if j == 3:
                stores[4] = pltpu.make_async_copy(up_all, up_out.at[layer], store_sems.at[4])
                stores[4].start()
        else:
            slot = number % 4
            if slot in stores:
                stores.pop(slot).wait()
            staged[slot] = value
            if kind < 3:
                dst = qkv_out.at[layer, :, pl.ds(1024 * kind, 1024)]
            else:
                dst = out_out.at[layer] if kind == 3 else down_out.at[layer, j]
            stores[slot] = pltpu.make_async_copy(staged.at[slot], dst, store_sems.at[slot])
            stores[slot].start()
        for kind in ("wide", "slim", "ends"):
            sent(kind, number)

    ticks = [0]
    stores = {}
    wide_lag, slim_lag, ends_lag = BACK_LAGS

    def tick():
        step = ticks[0]
        ticks[0] += 1
        if step < total:
            stage_core(step)
        if 0 <= step - wide_lag < total:
            stage_wide(step - wide_lag)
        if 0 <= step - slim_lag < total:
            stage_slim(step - slim_lag)
        if 0 <= step - ends_lag < total:
            stage_ends(step - ends_lag)

    def norm(base, gain_row, shift_row, sum_row):
        gain = rows_ref[pl.ds(base + gain_row, 1)]

        def body(step, carry):
            gains, shifts, sums = carry
            rows = pl.ds(step * 64, 64)
            value = grad[rows]
            normal = unit[rows]
            scaled = value * gain
            inner = jnp.mean(scaled * normal, -1, keepdims=True)
            centre = jnp.mean(scaled, -1, keepdims=True)
            result = scale[rows][:, :1] * (scaled - centre - normal * inner)
            grad[rows] = result
            rounded = result.astype(BF)
            edge[rows] = rounded
            return (
                gains + jnp.sum(value * normal, 0, keepdims=True),
                shifts + jnp.sum(value, 0, keepdims=True),
                sums + jnp.sum(rounded.astype(F32), 0, keepdims=True),
            )

        zero = jnp.zeros((1, 1024), F32)
        gains, shifts, sums = lax.fori_loop(0, 8, body, (zero, zero, zero))
        put_row(base + gain_row, gains)
        put_row(base + shift_row, shifts)
        put_row(base + sum_row, sums)

    def put_row(row, value):
        for block in range(8):
            small_all[block // 2, block % 2, row : row + 1] = value[:, block * 128 : block * 128 + 128]

    def heads(layer, begin, end):
        def body(j, carry):
            lanes = pl.ds(pl.multiple_of(j * 128, 128), 128)
            q = arena[0, :, lanes]
            do = span[:, lanes]
            lane = lax.broadcasted_iota(jnp.int32, q.shape, 1)
            prod = jnp.transpose(do.astype(F32) * feat[1, :, lanes].astype(F32))
            dq = []
            sums = [[None, None], [None, None]]
            for head in range(2):
                pick = (lane // 64) == head
                qh = jnp.where(pick, q, jnp.zeros_like(q))
                dh = jnp.where(pick, do, jnp.zeros_like(do))
                delta = jnp.sum(prod[head * 64 : head * 64 + 64], 0, keepdims=True)
                lse = lse_ref[layer, j, pl.ds(head, 1)]
                dqh = None
                for half in range(2):
                    k = arena[1 + 2 * half, :, lanes]
                    v = arena[2 + 2 * half, :, lanes]
                    p = jnp.exp(dot(k, qh, NT) - lse)
                    ds = (p * (dot(v, dh, NT) - delta)).astype(BF)
                    dv = jnp.dot(p.astype(BF), dh, preferred_element_type=F32)
                    dk = jnp.dot(ds, qh, preferred_element_type=F32)
                    part = dot(ds, k, TN)
                    dqh = part if dqh is None else dqh + part
                    sums[half][0] = dk if head == 0 else sums[half][0] + dk
                    sums[half][1] = dv if head == 0 else sums[half][1] + dv
                dq.append(dqh)
            arena[5, :, lanes] = (jnp.where(lane < 64, dq[0], dq[1]) * SCORE_SCALE).astype(BF)
            arena[6, :, lanes] = sums[0][0].astype(BF)
            arena[7, :, lanes] = sums[0][1].astype(BF)
            arena[8, :, lanes] = sums[1][0].astype(BF)
            arena[9, :, lanes] = sums[1][1].astype(BF)
            return carry

        lax.fori_loop(begin, end, body, 0)

    def row_sum(row, slot):
        def body(step, carry):
            rows = pl.ds(pl.multiple_of(step * 64, 64), 64)
            return carry + jnp.sum(arena[slot, rows].astype(F32), 0, keepdims=True)

        put_row(row, lax.fori_loop(0, 8, body, jnp.zeros((1, 1024), F32)))

    def pull(number, upper):
        def body(tile, carry):
            cols = columns(tile)
            grad[:, cols] += dot(upper[...], rows_of(number, tile), NT)
            return carry

        ready(("w", number))
        lax.fori_loop(0, 4, body, 0)
        fetch_weight(number + 2)

    def load_attention(layer):
        for part in range(3):
            fetch(("qkv", part), qkv_ref.at[layer, :, pl.ds(1024 * part, 1024)], arena.at[part], 2 + part)
        for part in range(2):
            fetch(("kv", part), kv_ref.at[layer, part], arena.at[3 + part], 5 + part)

    column = 4 * y + 2 * x
    seat = 2 * lax.rem(z, 2) + core
    stays = core == z // 2

    def homeward(which, block, src, dst):
        rows = src.at[pl.ds(block * 128, 128)]
        spot = dst.at[lax.rem(z, 2), pl.ds(pl.multiple_of(core * 128, 128), 128)]
        to = (column + z // 2, lax.rem(z - block + 4, 4))
        return (
            lambda: pltpu.make_async_copy(rows, spot, load_sems.at[14 + which]),
            lambda: remote(rows, spot, turn_send.at[which, block], turn_recv.at[which, seat], to),
        )

    def turn_start(which, src, dst):
        for block in range(4):
            local, away = homeward(which, block, src, dst)
            if block:
                away().start()
            else:
                pl.when(stays)(lambda: local().start())
                pl.when(jnp.logical_not(stays))(lambda: away().start())

    def turn_end(which, src, dst):
        for block in range(4):
            local, away = homeward(which, block, src, dst)
            if block:
                away().wait_send()
            else:
                pl.when(stays)(lambda: local().wait())
                pl.when(jnp.logical_not(stays))(lambda: away().wait_send())
        for place in range(4):
            spot = dst.at[place // 2, pl.ds(place % 2 * 128, 128)]
            came = remote(spot, spot, turn_send.at[which, 0], turn_recv.at[which, place], here["core"])
            own = jnp.logical_and(2 * core + place // 2 == z, core == place % 2)
            pl.when(jnp.logical_not(own))(came.wait_recv)

    fetch("top", top_ref, grad, 7)
    turn_start(0, last_ref, last_out)
    first = True
    for layer in reversed(range(layers)):
        base = layer * 12
        start = (layers - 1 - layer) * UNITS
        if first:
            fetch("unit", unit_ref.at[layer, 1], unit, 8)
            fetch("scale", scale_ref.at[layer, 1], scale, 9)
            fetch_weight(0)
            fetch_weight(1)
            load_attention(layer)
            ready("top")
        fetch("act", act_ref.at[layer, 0], arena.at[8], 10)
        fetch("slope", slope_ref.at[layer, 0], arena.at[9], 11)
        fetch("nrm", nrm_ref.at[layer], feat.at[0], 12)
        fetch("mix", mix_ref.at[layer], feat.at[1], 13)
        first = False
        ready("unit")
        ready("scale")
        norm(base, 7, 5, 3)
        fetch("unit", unit_ref.at[layer, 0], unit, 8)
        fetch("scale", scale_ref.at[layer, 0], scale, 9)
        ready("nrm")
        turn(0, feat.at[0])
        fetch("low", low_ref.at[layer], feat.at[0], 12)
        for j in range(4):
            number = start + 2 * j
            ready("act")
            turn(1, arena.at[8])
            if j < 3:
                fetch("act", act_ref.at[layer, j + 1], arena.at[8], 10)
            produce(number, 1, edge)
            ready(("w", number))
            ready("slope")

            def body(tile, carry):
                cols = columns(tile)
                value = dot(edge[...], rows_of(number, tile), NT)
                value = (arena[9, :, cols].astype(F32) * value).astype(BF)
                span[:, cols] = value
                total_row = jnp.sum(value.astype(F32), 0, keepdims=True)
                for block in range(2):
                    small_all[tile, block, pl.ds(base + 8 + j, 1)] = total_row[
                        :, block * 128 : block * 128 + 128
                    ]
                return carry

            lax.fori_loop(0, 4, body, 0)
            fetch_weight(number + 2)
            if j < 3:
                fetch("slope", slope_ref.at[layer, j + 1], arena.at[9], 11)
            produce(number + 1, 0, span)
            pull(number + 1, span)
            tick()
        ready("unit")
        ready("scale")
        norm(base, 6, 4, 2)
        if layer:
            fetch("unit", unit_ref.at[layer - 1, 1], unit, 8)
            fetch("scale", scale_ref.at[layer - 1, 1], scale, 9)
        ready("mix")
        turn(1, feat.at[1])
        number = start + 8
        ready(("w", number))

        def body(tile, carry):
            span[:, columns(tile)] = dot(edge[...], rows_of(number, tile), NT).astype(BF)
            return carry

        lax.fori_loop(0, 4, body, 0)
        fetch_weight(number + 2)
        tick()
        produce(number, 1, edge)
        for part in range(3):
            ready(("qkv", part))
        for part in range(2):
            ready(("kv", part))
        for group in range(4):
            heads(layer, 2 * group, 2 * group + 2)
            tick()
        place = layers - 1 - layer
        for part in range(2):
            launch(
                "keys",
                2 * place + part,
                [side(2 * place + part, arena.at[8 + part], arena.at[10 + part], here["core"])],
            )
        if layer:
            load_attention(layer - 1)
        ready("low")
        turn(0, feat.at[0])
        for part in range(3):
            number = start + 9 + part
            if part:
                landed("keys", 2 * place + part - 1)

                def body(step, carry):
                    rows = pl.ds(pl.multiple_of(step * 64, 64), 64)
                    value = arena[5 + part, rows].astype(F32) + arena[9 + part, rows].astype(F32)
                    arena[5 + part, rows] = value.astype(BF)
                    return carry

                lax.fori_loop(0, 8, body, 0)
            if part != 1:
                row_sum(base + part // 2, 5 + part)
            produce(number, 0, arena.at[5 + part])
            pull(number, arena.at[5 + part])
            if part < 2:
                tick()
        sent("keys", 2 * place)
        sent("keys", 2 * place + 1)
        if layer == 0:

            def body(step, carry):
                rows = pl.ds(pl.multiple_of(step * 64, 64), 64)
                edge[rows] = grad[rows].astype(BF)
                return carry

            lax.fori_loop(0, 8, body, 0)
            turn_start(1, edge, grad_out)
        tick()
    base = 2 * layers

    def small_core():
        launch("small", 0, [side(base, small_all.at[:, 1 - core], small_in.at[pl.ds(0, 4)], here["core"])])

    def small_y():
        landed("small", 0)
        sent("small", 0)
        small_all[:, core] = small_all[:, core] + small_in[0:4]
        launch(
            "small",
            1,
            [side(base + 1, small_all.at[pl.ds(2 - 2 * y, 2), core], small_in.at[pl.ds(4, 2)], here["y"])],
        )

    def small_x():
        landed("small", 1)
        sent("small", 1)
        for block in range(2):
            small_all[2 * y + block, core] = small_all[2 * y + block, core] + small_in[4 + block]
        launch(
            "small",
            2,
            [side(base + 2, small_all.at[2 * y + 1 - x, core], small_in.at[6], here["x"])],
        )

    def small_z():
        landed("small", 2)
        sent("small", 2)
        own = small_all.at[2 * y + x, core]
        own[...] = own[...] + small_in[6]
        launch(
            "small",
            3,
            [
                side(base + 2 + step, own, small_in.at[6 + step], (batch, lax.rem(z + step, 4)))
                for step in (1, 2, 3)
            ],
        )

    def small_end():
        landed("small", 3)
        sent("small", 3)
        value = small_all[2 * y + x, core]
        for step in (1, 2, 3):
            value = value + small_in[6 + step]
        mine_row = value[:, 0:32]
        for place in range(1, 4):
            mine_row = jnp.where(z == place, value[:, place * 32 : place * 32 + 32], mine_row)
        for layer in range(layers):
            top = layer * 12
            bias_out[layer] = mine_row[top : top + 6]
            gain_out[layer] = mine_row[top + 6 : top + 8]
            for j in range(4):
                up_bias_out[layer : layer + 1, j * 32 : j * 32 + 32] = mine_row[top + 8 + j : top + 9 + j]

    queue = [small_core, small_y, small_x, small_z, small_end]
    while ticks[0] < total + ends_lag or queue:
        if queue:
            queue.pop(0)()
        if ticks[0] < total + ends_lag:
            tick()
    for kind, number in list(outgoing):
        sent(kind, number)
    for copy in stores.values():
        copy.wait()
    turn_end(0, last_ref, last_out)
    turn_end(1, edge, grad_out)


BACK_LAGS = (2, 4, 5)


def backward_pass(top, last, saved):
    w, rows, lse, low, qkv, kv, mix, nrm, act, slope, unit, scale = saved
    total = w.shape[0]
    layers = total // UNITS
    tokens, width = top.shape
    any_spec = pl.BlockSpec(memory_space=pl.ANY)
    vmem = pl.BlockSpec(memory_space=pltpu.VMEM)
    shape = jax.ShapeDtypeStruct
    return pl.pallas_call(
        functools.partial(backward_kernel, layers=layers),
        in_specs=[any_spec] * 3 + [vmem, vmem] + [any_spec] * 9,
        out_specs=[any_spec] * 6 + [vmem] * 3,
        out_shape=[
            shape((2, tokens // 2, width), BF),
            shape((2, tokens // 2, width), BF),
            shape((layers, 32, 3 * width), F32),
            shape((layers, 32, width), F32),
            shape((layers, 32, 4 * width), F32),
            shape((layers, 4, 32, width), F32),
            shape((layers, 6, 32), F32),
            shape((layers, 128), F32),
            shape((layers, 2, 32), F32),
        ],
        scratch_shapes=[
            pltpu.VMEM((tokens, width), F32),
            pltpu.VMEM((tokens, width), BF),
            pltpu.VMEM((tokens, width), F32),
            pltpu.VMEM((tokens, 128), F32),
            pltpu.VMEM((12, tokens, width), BF),
            pltpu.VMEM((tokens, width), BF),
            pltpu.VMEM((2, tokens, width), BF),
            pltpu.VMEM((2, 2, width // 2, tokens), BF),
            pltpu.VMEM((2, 4, 2, 128, width), BF),
            pltpu.VMEM((2, 4, 128, width), BF),
            pltpu.VMEM((6, 4, 128, width), BF),
            pltpu.VMEM((UNITS, 4, 128, width), BF),
            pltpu.VMEM((6, 2, 2, 128, width // 2), BF),
            pltpu.VMEM((6, 2, 128, width // 2), BF),
            pltpu.VMEM((6, 3, 32, width), BF),
            pltpu.VMEM((4, 2, layers * 12, 128), F32),
            pltpu.VMEM((10, layers * 12, 128), F32),
            pltpu.VMEM((4, 32, width), F32),
            pltpu.VMEM((32, 4 * width), F32),
            pltpu.SemaphoreType.DMA((16,)),
            pltpu.SemaphoreType.DMA((5,)),
            pltpu.SemaphoreType.DMA((total, 9)),
            pltpu.SemaphoreType.DMA((total, 9)),
            pltpu.SemaphoreType.DMA((2 * layers + 6,)),
            pltpu.SemaphoreType.DMA((2 * layers + 6,)),
            pltpu.SemaphoreType.DMA((2, 4)),
            pltpu.SemaphoreType.DMA((2, 4)),
        ],
        compiler_params=pltpu.CompilerParams(has_side_effects=True, vmem_limit_bytes=60 << 20),
        name="backward_pass",
    )(top, last, w, rows, lse, low, qkv, kv, mix, nrm, act, slope, unit, scale)


def swap(value, bit):
    return lax.ppermute(value, "batch", [(place, place ^ bit) for place in range(8)])


def take(value, index, axis):
    return lax.dynamic_index_in_dim(value, index, axis, keepdims=False)


def small_rows(biases, up_bias, gains):
    layers = biases.shape[0]
    rows = jnp.concatenate((biases, gains, up_bias.reshape(layers, 4, 32)), 1).astype(F32)
    wide = jnp.tile(rows.reshape(layers * 12, 32), (1, 4))
    lane = lax.broadcasted_iota(jnp.int32, wide.shape, 1)
    return jnp.where(lane // 32 == lax.axis_index("blk"), wide, 0.0)


def column_shards(
    hidden_in,
    mask_index,
    mask_count,
    replacement,
    out_grad,
    w_qkv,
    w_out,
    w_up,
    w_down,
    biases,
    up_bias,
    gains,
):
    batch = lax.axis_index("batch")
    z = lax.axis_index("blk")
    core = lax.rem(batch, 2)
    seq_count, block_len, width = hidden_in.shape
    layers = w_qkv.shape[0]
    slots = mask_index.shape[1]
    per = width // 32

    slot_ids = jnp.arange(slots, dtype=jnp.int32)
    used = slot_ids[None, :] < mask_count[:, None]
    slot_place = jnp.where(used, mask_index, -1)
    places = z * block_len + jnp.arange(block_len, dtype=jnp.int32)
    hits = slot_place[:, None, :] == places[None, :, None]
    placed = jnp.einsum("sbm,smd->sbd", hits.astype(BF), replacement, preferred_element_type=F32)
    first = jnp.where(jnp.any(hits, -1, keepdims=True), placed.astype(BF), hidden_in)

    mine = lax.rem(z, 2)
    came_grad = swap(take(out_grad, mine, 0), 1)
    came_place = swap(take(slot_place, mine, 0).astype(F32), 1)
    here = (z // 2) == core
    top_grad = jnp.where(here, take(out_grad, mine, 0), came_grad)
    top_place = jnp.where(here, take(slot_place, mine, 0), came_place.astype(jnp.int32))
    blocks = lax.rem(z - jnp.arange(4, dtype=jnp.int32) + 4, 4)
    token_place = (
        blocks[:, None] * block_len
        + core * (block_len // 2)
        + jnp.arange(block_len // 2, dtype=jnp.int32)[None, :]
    ).reshape(-1)
    top_hits = (token_place[:, None] == top_place[None, :]).astype(BF)
    upstream = jnp.dot(top_hits, top_grad, preferred_element_type=F32)

    results = forward_pass(first, w_qkv, w_out, w_up, w_down, small_rows(biases, up_bias, gains))
    last, grad, qkv, out, up, down, bias_rows, up_rows, gain_rows = backward_pass(
        upstream, results[1], (results[0],) + tuple(results[2:])
    )
    return (
        last,
        grad.astype(F32),
        qkv,
        out,
        up,
        down.reshape(layers, 4 * per, width),
        bias_rows,
        up_rows,
        gain_rows,
    )


def solution(mesh):
    fits = mesh.shape["batch"] == 8 and mesh.shape["blk"] == 4
    return jax.shard_map(
        column_shards if fits else general_shards,
        mesh=mesh,
        in_specs=(
            P(*BOTH, None),
            P("batch", None),
            P("batch"),
            P("batch", None, None),
            P("batch", None, None),
            P(None, BOTH, None),
            P(None, BOTH, None),
            P(None, BOTH, None),
            P(None, BOTH, None),
            P(None, None, BOTH),
            P(None, BOTH),
            P(None, None, BOTH),
        ),
        out_specs=(
            P(*BOTH, None),
            P(*BOTH, None),
            P(None, BOTH, None),
            P(None, BOTH, None),
            P(None, BOTH, None),
            P(None, BOTH, None),
            P(None, None, BOTH),
            P(None, BOTH),
            P(None, None, BOTH),
        ),
        check_vma=False,
    )
```

```python
import functools

import jax
import jax.numpy as jnp
from jax import lax
from jax.experimental import pallas as pl
from jax.experimental.pallas import tpu as pltpu
from jax.sharding import PartitionSpec as P

HEADS = 16


BOTH = ("batch", "blk")
NORM_EPS = 1e-12
SCORE_SCALE = 0.125


def norm_rows(values, gain, shift):
    center = values - jnp.mean(values, -1, keepdims=True)
    spread = jnp.mean(center * center, -1, keepdims=True)
    return center * lax.rsqrt(spread + NORM_EPS) * gain + shift


def gelu_exact(values):
    return 0.5 * values * (1.0 + jax.scipy.special.erf(values * 0.7071067811865476))


def forward_layer(inputs, fetched, head_shape):
    qkv_weight, out_weight, up_weight, down_weight, bias_rows, up_shift, gain_rows = fetched
    bias_rows = bias_rows.astype(jnp.float32)
    up_shift = up_shift.astype(jnp.float32)
    gain_rows = gain_rows.astype(jnp.float32)
    seq_count, block_len, head_count, head_dim = head_shape
    model_width = head_count * head_dim
    inputs_low = inputs.astype(jnp.bfloat16)
    project = jnp.einsum("sbd,de->sbe", inputs_low, qkv_weight, preferred_element_type=jnp.float32)
    query = (project[..., :model_width] + bias_rows[0]).astype(jnp.bfloat16).reshape(head_shape)
    keys = project[..., model_width : 2 * model_width].astype(jnp.bfloat16).reshape(head_shape)
    values = (
        (project[..., 2 * model_width :] + bias_rows[1]).astype(jnp.bfloat16).reshape(head_shape)
    )
    stat_shape = (seq_count, head_count, block_len)
    top_now = jnp.full(stat_shape, -1e30, jnp.float32)
    key_part = lax.all_gather(keys, "blk", axis=1, tiled=True)
    value_part = lax.all_gather(values, "blk", axis=1, tiled=True)
    scores = (
        jnp.einsum("sqhd,skhd->shqk", query, key_part, preferred_element_type=jnp.float32)
        * SCORE_SCALE
    )
    top_next = jnp.maximum(top_now, jnp.max(scores, -1))
    weights_now = jnp.exp(scores - top_next[..., None])
    total_next = jnp.sum(weights_now, -1)
    acc_next = jnp.einsum(
        "shqk,skhd->shqd",
        weights_now.astype(jnp.bfloat16),
        value_part,
        preferred_element_type=jnp.float32,
    )
    log_total = top_next + jnp.log(total_next)
    attended = (acc_next / total_next[..., None]).transpose(0, 2, 1, 3).reshape(inputs.shape)
    attended_low = attended.astype(jnp.bfloat16)
    mixed = (
        inputs
        + jnp.einsum("sbe,ed->sbd", attended_low, out_weight, preferred_element_type=jnp.float32)
        + bias_rows[2]
    )
    normed, first_pull = jax.vjp(norm_rows, mixed, gain_rows[0], bias_rows[4])
    normed_low = normed.astype(jnp.bfloat16)
    hidden = (
        jnp.einsum("sbd,df->sbf", normed_low, up_weight, preferred_element_type=jnp.float32)
        + up_shift
    )
    active, gelu_pull = jax.vjp(gelu_exact, hidden)
    active_low = active.astype(jnp.bfloat16)
    second = (
        normed
        + jnp.einsum("sbf,fd->sbd", active_low, down_weight, preferred_element_type=jnp.float32)
        + bias_rows[3]
    )
    result, second_pull = jax.vjp(norm_rows, second, gain_rows[1], bias_rows[5])
    kept = (
        inputs_low,
        query,
        keys,
        values,
        log_total,
        attended,
        attended_low,
        normed_low,
        active_low,
        first_pull,
        gelu_pull,
        second_pull,
    )
    return (result, kept)


def backward_layer(upstream, fetched, kept, head_shape):
    qkv_weight, out_weight, up_weight, down_weight = (
        fetched[0],
        fetched[1],
        fetched[2],
        fetched[3],
    )
    (
        inputs_low,
        query,
        keys,
        values,
        log_total,
        attended,
        attended_low,
        normed_low,
        active_low,
        first_pull,
        gelu_pull,
        second_pull,
    ) = kept
    seq_count, block_len, head_count, head_dim = head_shape
    row_axes = (0, 1)
    second_grad, gain_two, shift_two = second_pull(upstream)
    down_in = second_grad.astype(jnp.bfloat16)
    down_grad = jnp.einsum("sbf,sbd->fd", active_low, down_in, preferred_element_type=jnp.float32)
    down_shift = jnp.sum(down_in.astype(jnp.float32), row_axes)
    active_grad = jnp.einsum(
        "sbd,fd->sbf", down_in, down_weight, preferred_element_type=jnp.float32
    )
    hidden_grad = gelu_pull(active_grad)[0].astype(jnp.bfloat16)
    up_grad = jnp.einsum("sbd,sbf->df", normed_low, hidden_grad, preferred_element_type=jnp.float32)
    up_shift_grad = jnp.sum(hidden_grad.astype(jnp.float32), row_axes)
    normed_grad = second_grad + jnp.einsum(
        "sbf,df->sbd", hidden_grad, up_weight, preferred_element_type=jnp.float32
    )
    mixed_grad, gain_one, shift_one = first_pull(normed_grad)
    out_in = mixed_grad.astype(jnp.bfloat16)
    out_weight_grad = jnp.einsum(
        "sbe,sbd->ed", attended_low, out_in, preferred_element_type=jnp.float32
    )
    out_shift = jnp.sum(out_in.astype(jnp.float32), row_axes)
    attend_grad = (
        jnp.einsum("sbd,ed->sbe", out_in, out_weight, preferred_element_type=jnp.float32)
        .astype(jnp.bfloat16)
        .reshape(head_shape)
    )
    delta_rows = jnp.sum(attend_grad.astype(jnp.float32) * attended.reshape(head_shape), -1)
    lse_rows = log_total.transpose(0, 2, 1)
    lse_all, delta_all = (
        lax.all_gather(lse_rows, "blk", axis=1, tiled=True),
        lax.all_gather(delta_rows, "blk", axis=1, tiled=True),
    )
    delta_heads = delta_rows.transpose(0, 2, 1)
    key_part = lax.all_gather(keys, "blk", axis=1, tiled=True)
    value_part = lax.all_gather(values, "blk", axis=1, tiled=True)
    scores = (
        jnp.einsum("sqhd,skhd->shqk", query, key_part, preferred_element_type=jnp.float32)
        * SCORE_SCALE
    )
    probs = jnp.exp(scores - log_total[..., None])
    prob_grad = jnp.einsum(
        "sqhd,skhd->shqk", attend_grad, value_part, preferred_element_type=jnp.float32
    )
    score_grad = (probs * (prob_grad - delta_heads[..., None])).astype(jnp.bfloat16)
    query_grad = (
        jnp.einsum("shqk,skhd->sqhd", score_grad, key_part, preferred_element_type=jnp.float32)
        * SCORE_SCALE
    )
    query_part = lax.all_gather(query, "blk", axis=1, tiled=True)
    grad_part = lax.all_gather(attend_grad, "blk", axis=1, tiled=True)
    lse_part = lse_all.transpose(0, 2, 1)
    delta_part = delta_all.transpose(0, 2, 1)
    scores = (
        jnp.einsum("sqhd,skhd->shqk", query_part, keys, preferred_element_type=jnp.float32)
        * SCORE_SCALE
    )
    probs = jnp.exp(scores - lse_part[..., None])
    value_acc = jnp.einsum(
        "shqk,sqhd->skhd", probs.astype(jnp.bfloat16), grad_part, preferred_element_type=jnp.float32
    )
    prob_grad = jnp.einsum("sqhd,skhd->shqk", grad_part, values, preferred_element_type=jnp.float32)
    score_grad = (probs * (prob_grad - delta_part[..., None])).astype(jnp.bfloat16)
    key_acc = (
        jnp.einsum("shqk,sqhd->skhd", score_grad, query_part, preferred_element_type=jnp.float32)
        * SCORE_SCALE
    )
    flat_shape = (seq_count, block_len, head_count * head_dim)
    query_low = query_grad.reshape(flat_shape).astype(jnp.bfloat16)
    key_low = key_acc.reshape(flat_shape).astype(jnp.bfloat16)
    value_low = value_acc.reshape(flat_shape).astype(jnp.bfloat16)
    proj_grad = jnp.concatenate((query_low, key_low, value_low), -1)
    qkv_grad = jnp.einsum("sbd,sbe->de", inputs_low, proj_grad, preferred_element_type=jnp.float32)
    query_shift = jnp.sum(query_low.astype(jnp.float32), row_axes)
    value_shift = jnp.sum(value_low.astype(jnp.float32), row_axes)
    inputs_grad = mixed_grad + jnp.einsum(
        "sbe,de->sbd", proj_grad, qkv_weight, preferred_element_type=jnp.float32
    )
    shift_rows = jnp.stack((query_shift, value_shift, out_shift, down_shift, shift_one, shift_two))
    gain_grad = jnp.stack((gain_one, gain_two))
    return (
        inputs_grad,
        (qkv_grad, out_weight_grad, up_grad, down_grad, shift_rows, up_shift_grad, gain_grad),
    )


def general_shards(
    hidden_in,
    mask_index,
    mask_count,
    replacement,
    out_grad,
    w_qkv,
    w_out,
    w_up,
    w_down,
    biases,
    up_bias,
    gains,
):
    seq_count, block_len, model_width = hidden_in.shape
    layer_count = w_qkv.shape[0]
    head_shape = (seq_count, block_len, HEADS, model_width // HEADS)
    offset = lax.axis_index("blk") * block_len
    places = offset + jnp.arange(block_len, dtype=jnp.int32)
    slot_ids = jnp.arange(mask_index.shape[1], dtype=jnp.int32)
    hit_table = (mask_index[:, None, :] == places[None, :, None]) & (
        slot_ids[None, None, :] < mask_count[:, None, None]
    )
    hit_low = hit_table.astype(jnp.bfloat16)
    chosen = jnp.any(hit_table, -1, keepdims=True)
    placed = jnp.einsum("sbm,smd->sbd", hit_low, replacement, preferred_element_type=jnp.float32)
    current = jnp.where(chosen, placed, hidden_in.astype(jnp.float32))
    upstream = jnp.einsum("sbm,smd->sbd", hit_low, out_grad, preferred_element_type=jnp.float32)
    shard_shapes = (w_qkv.shape[1:], w_out.shape[1:], w_up.shape[1:], w_down.shape[1:])
    saved_weights = []
    saved_state = []
    for layer_idx in range(layer_count):
        fetched = (
            lax.all_gather(w_qkv[layer_idx], BOTH, axis=0, tiled=True),
            lax.all_gather(w_out[layer_idx], BOTH, axis=0, tiled=True),
            lax.all_gather(w_up[layer_idx], BOTH, axis=0, tiled=True),
            lax.all_gather(w_down[layer_idx], BOTH, axis=0, tiled=True),
            lax.all_gather(biases[layer_idx], BOTH, axis=1, tiled=True),
            lax.all_gather(up_bias[layer_idx], BOTH, axis=0, tiled=True),
            lax.all_gather(gains[layer_idx], BOTH, axis=1, tiled=True),
        )
        saved_weights.append(None)
        current, state = forward_layer(current, fetched, head_shape)
        saved_state.append(state)
    grad_now = upstream
    summed = [None] * layer_count
    for layer_idx in reversed(range(layer_count)):
        fetched = (
            lax.all_gather(w_qkv[layer_idx], BOTH, axis=0, tiled=True),
            lax.all_gather(w_out[layer_idx], BOTH, axis=0, tiled=True),
            lax.all_gather(w_up[layer_idx], BOTH, axis=0, tiled=True),
            lax.all_gather(w_down[layer_idx], BOTH, axis=0, tiled=True),
            lax.all_gather(biases[layer_idx], BOTH, axis=1, tiled=True),
            lax.all_gather(up_bias[layer_idx], BOTH, axis=0, tiled=True),
            lax.all_gather(gains[layer_idx], BOTH, axis=1, tiled=True),
        )
        grad_now, terms = backward_layer(grad_now, fetched, saved_state[layer_idx], head_shape)
        flat_terms = (
            terms[0].reshape(-1, 128),
            terms[1].reshape(-1, 128),
            terms[2].reshape(-1, 128),
            terms[3].reshape(-1, 128),
            terms[4],
            terms[5],
            terms[6],
        )
        reduced = (
            lax.psum_scatter(flat_terms[0], BOTH, scatter_dimension=0, tiled=True),
            lax.psum_scatter(flat_terms[1], BOTH, scatter_dimension=0, tiled=True),
            lax.psum_scatter(flat_terms[2], BOTH, scatter_dimension=0, tiled=True),
            lax.psum_scatter(flat_terms[3], BOTH, scatter_dimension=0, tiled=True),
            lax.psum_scatter(flat_terms[4], BOTH, scatter_dimension=1, tiled=True),
            lax.psum_scatter(flat_terms[5], BOTH, scatter_dimension=0, tiled=True),
            lax.psum_scatter(flat_terms[6], BOTH, scatter_dimension=1, tiled=True),
        )
        summed[layer_idx] = tuple(
            (reduced[member].reshape(shard_shapes[member]) for member in range(4))
        ) + tuple(reduced[4:])
    stacked = [jnp.stack([entry[member] for entry in summed]) for member in range(7)]
    return (
        current.astype(jnp.bfloat16),
        grad_now,
        stacked[0],
        stacked[1],
        stacked[2],
        stacked[3],
        stacked[4],
        stacked[5],
        stacked[6],
    )


NT = (((1,), (1,)), ((), ()))
TN = (((0,), (0,)), ((), ()))
F32 = jnp.float32
BF = jnp.bfloat16


def dot(a, b, dims):
    return lax.dot_general(a, b, dims, preferred_element_type=F32)


MESH = pl.DeviceIdType.MESH
UNITS = 12
TILE = 256
LAGS = (3, 1, 3, 4)
DIRECT = 8
TURN_STEPS = (0, 2, 4, 6)
BEGIN = 9
BUDGET = 4.5


def place_of():
    batch = lax.axis_index("batch")
    return batch, lax.axis_index("blk"), batch // 4, lax.rem(batch // 2, 2), lax.rem(batch, 2)


def columns(tile):
    return pl.ds(pl.multiple_of(tile * TILE, TILE), TILE)


def forward_kernel(
    first_ref,
    qkv_in,
    out_in,
    up_in,
    down_in,
    small_ref,
    w_ref,
    out_ref,
    rows_ref,
    lse_ref,
    qkv_ref,
    kv_ref,
    mix_ref,
    flip_ref,
    slope_ref,
    unit_ref,
    scale_ref,
    cur,
    low,
    qkv,
    sib,
    mix,
    nrm,
    acc,
    act,
    slope,
    unit,
    scale,
    wbuf,
    flipped,
    shard,
    small_all,
    local_sems,
    own_sems,
    save_sems,
    send_sems,
    recv_sems,
    side_send,
    side_recv,
    turn_send,
    turn_recv,
    layers,
):
    batch, z, y, x, core = place_of()
    total = layers * UNITS
    yx = 2 * y + x
    column = 4 * y + 2 * x
    here = {"x": (batch ^ 2, z), "y": (batch ^ 4, z), "core": (batch ^ 1, z)}

    def remote(src, dst, send, recv, device):
        return pltpu.make_async_remote_copy(
            src_ref=src,
            dst_ref=dst,
            send_sem=send,
            recv_sem=recv,
            device_id=device,
            device_id_type=MESH,
        )

    flying = {}

    def launch(kind, unit_id, copies):
        flying[kind, unit_id] = copies
        for copy in copies:
            copy.start()

    def landed(kind, unit_id):
        for copy in flying[kind, unit_id]:
            copy.wait_recv()

    def hop(unit_id, slot, src, dst, device):
        return remote(src, dst, send_sems.at[unit_id, slot], recv_sems.at[unit_id, slot], device)

    own_rows = pl.ds(pl.multiple_of(z * 32, 32), 32)

    def straight(unit_id):
        return 1024 if unit_id < DIRECT else 1024 - 128

    def along(unit_id):
        cols = pl.ds(0, straight(unit_id))
        dst = w_ref.at[unit_id, yx, core, own_rows, cols]
        src = shard.at[unit_id, :, cols]
        copies = []
        if unit_id >= DIRECT:
            edge = pl.ds(1024 - 128, 128)
            piece, spot = shard.at[unit_id, :, edge], w_ref.at[unit_id, yx, core, own_rows, edge]
            copies += [hop(unit_id, 8, piece, spot, here["x"]), hop(unit_id, 9, piece, spot, here["y"])]
        for step in (1, 2, 3):
            copies.append(hop(unit_id, step - 1, src, dst, (batch, lax.rem(z + step, 4))))
        return copies

    def across(unit_id):
        line = w_ref.at[unit_id, yx, core, :, pl.ds(0, straight(unit_id))]
        copies = []
        if unit_id >= DIRECT:
            edge = pl.ds(1024 - 128, 128)
            if unit_id % 2:
                piece, to = w_ref.at[unit_id, 2 * y + 1 - x, core, own_rows, edge], here["y"]
            else:
                piece, to = w_ref.at[unit_id, 2 - 2 * y + x, core, own_rows, edge], here["x"]
            copies.append(hop(unit_id, 10, piece, piece, to))
        copies += [hop(unit_id, 3, line, line, here["x"]), hop(unit_id, 4, line, line, here["y"])]
        return copies

    def corner(unit_id):
        full = straight(unit_id)
        half = 384 if full < 1024 and unit_id % 2 else 512
        left = w_ref.at[unit_id, 2 * y + 1 - x, core, :, pl.ds(0, half)]
        right = w_ref.at[unit_id, 2 - 2 * y + x, core, :, pl.ds(half, full - half)]
        copies = []
        if unit_id >= DIRECT:
            block = w_ref.at[unit_id, :, core, own_rows, pl.ds(1024 - 128, 128)]
            for step in (1, 2, 3):
                to = (batch, lax.rem(z + step, 4))
                copies.append(hop(unit_id, 10 + step, block, block, to))
        copies += [hop(unit_id, 5, left, left, here["y"]), hop(unit_id, 6, right, right, here["x"])]
        return copies

    def inner(unit_id):
        block = w_ref.at[unit_id, :, core]
        return [hop(unit_id, 7, block, block, here["core"])]

    def side(slot, src, dst, device):
        return remote(src, dst, side_send.at[slot], side_recv.at[slot], device)

    def layout(layer):
        base = layer * UNITS
        for part in range(3):
            shard[base + part] = qkv_in[layer, :, part * 1024 : part * 1024 + 1024]
        shard[base + 3] = out_in[layer]
        lane = lax.broadcasted_iota(jnp.int32, (32, 128), 1) // 32
        for j in range(4):
            shard[base + 5 + 2 * j] = down_in[layer, j * 32 : j * 32 + 32]
            for block in range(8):
                made = None
                for part in range(4):
                    start = (4 * block + part) * 128
                    value = up_in[layer, :, start : start + 128].astype(F32)
                    if part != j:
                        value = pltpu.roll(value, ((part - j) * 32) % 128, 1)
                    made = value if made is None else jnp.where(lane == part, value, made)
                shard[base + 4 + 2 * j, :, block * 128 : block * 128 + 128] = made.astype(BF)

    owns = [
        pltpu.make_async_copy(
            shard.at[unit_id], w_ref.at[unit_id, yx, core, own_rows], own_sems.at[unit_id]
        )
        for unit_id in range(total)
    ]
    mine = small_all.at[y, x, core, z]
    mine[...] = small_ref[...]
    launch(
        "small",
        0,
        [side(step - 1, small_ref, mine, (batch, lax.rem(z + step, 4))) for step in (1, 2, 3)],
    )

    def turn(j, half):
        to = 2 * core + j
        block = lax.rem(to - z + 4, 4)
        src = first_ref.at[j, pl.ds(half * 128, 128)]
        dst = low.at[pl.ds(pl.multiple_of(block * 128, 128), 128)]
        send, recv = turn_send.at[2 * j + half], turn_recv.at[block]
        return (
            lambda: pltpu.make_async_copy(src, dst, local_sems.at[0]),
            lambda: remote(src, dst, send, recv, (column + half, to)),
            jnp.logical_and(to == z, core == half),
        )

    def turned(block):
        spot = low.at[pl.ds(block * 128, 128)]
        return remote(spot, spot, turn_send.at[0], turn_recv.at[block], here["core"])

    for layer in range(layers):
        layout(layer)
        if layer == 0:
            for unit_id in range(1):
                owns[unit_id].start()
                launch("along", unit_id, along(unit_id))
            for unit_id in range(1, LAGS[0]):
                owns[unit_id].start()
                launch("along", unit_id, along(unit_id))
    own_turn = core == z // 2

    def turn_out(j, half):
        local, away, stays = turn(j, half)
        pl.when(stays)(lambda: local().start())
        pl.when(jnp.logical_not(stays))(lambda: away().start())


    def small_hop(number):
        landed("small", number - 1)
        if number == 1:
            line = small_all.at[y, x, core]
            launch("small", 1, [side(3, line, line, here["x"])])
        elif number == 2:
            plane = small_all.at[y, :, core]
            launch("small", 2, [side(4, plane, plane, here["y"])])
        elif number == 3:
            cube = small_all.at[:, :, core]
            launch("small", 3, [side(5, cube, cube, here["core"])])

    def begin():
        small_hop(4)
        for block in range(8):
            four = small_all[block // 4, (block // 2) % 2, block % 2]
            rows_ref[:, block * 128 : block * 128 + 128] = (four[0] + four[1]) + (four[2] + four[3])
        local = turn(0, 0)[0]
        pl.when(own_turn)(lambda: local().wait())
        pl.when(jnp.logical_not(own_turn))(lambda: turned(0).wait_recv())
        for block in range(1, 4):
            turned(block).wait_recv()

        def body(step, carry):
            rows = pl.ds(pl.multiple_of(step * 64, 64), 64)
            cur[rows] = low[rows].astype(F32)
            return carry

        lax.fori_loop(0, 8, body, 0)

    saves = {}

    def save(name, src, dst, slot):
        if name in saves:
            saves[name].wait()
        saves[name] = pltpu.make_async_copy(src, dst, save_sems.at[slot])
        saves[name].start()

    def settle(*names):
        for name in names:
            if name in saves:
                saves.pop(name).wait()

    def norm(layer, which, gain_row, shift_row):
        gain = rows_ref[pl.ds(gain_row, 1)]
        shift_by = rows_ref[pl.ds(shift_row, 1)]

        def body(step, carry):
            rows = pl.ds(step * 64, 64)
            value = acc[rows]
            center = value - jnp.mean(value, -1, keepdims=True)
            spread = jnp.mean(center * center, -1, keepdims=True)
            root = lax.rsqrt(spread + NORM_EPS)
            normal = center * root
            unit[which, rows] = normal
            scale[which, rows] = jnp.broadcast_to(root, (64, 128))
            result = normal * gain + shift_by
            if which == 0:
                acc[rows] = result + rows_ref[pl.ds(layer * 12 + 3, 1)]
                nrm[rows] = result.astype(BF)
            else:
                cur[rows] = result
                low[rows] = result.astype(BF)
            return carry

        lax.fori_loop(0, 8, body, 0)
        save(("unit", which), unit.at[which], unit_ref.at[layer, which], 8 + which)
        save(("scale", which), scale.at[which], scale_ref.at[layer, which], 10 + which)

    def heads(layer, begin, end):
        def body(j, carry):
            lanes = pl.ds(pl.multiple_of(j * 128, 128), 128)
            k_lanes = pl.ds(pl.multiple_of(1024 + j * 128, 128), 128)
            v_lanes = pl.ds(pl.multiple_of(2048 + j * 128, 128), 128)
            q = qkv[:, lanes]
            lane = lax.broadcasted_iota(jnp.int32, q.shape, 1)
            outs = []
            for head in range(2):
                qh = jnp.where((lane // 64) == head, q, jnp.zeros_like(q))
                s_own = dot(qkv[:, k_lanes], qh, NT)
                s_sib = dot(sib[layer, 0, :, lanes], qh, NT)
                top = jnp.maximum(
                    jnp.max(s_own, 0, keepdims=True), jnp.max(s_sib, 0, keepdims=True)
                )
                p_own = jnp.exp(s_own - top)
                p_sib = jnp.exp(s_sib - top)
                mass = jnp.sum(p_own, 0, keepdims=True) + jnp.sum(p_sib, 0, keepdims=True)
                lse_ref[layer, j, pl.ds(head, 1)] = top + jnp.log(mass)
                o = dot(qkv[:, v_lanes], p_own.astype(BF), TN) + dot(
                    sib[layer, 1, :, lanes], p_sib.astype(BF), TN
                )
                outs.append(o[head * 64 : head * 64 + 64] / mass)
            mix[:, lanes] = jnp.transpose(jnp.concatenate(outs, 0)).astype(BF)
            return carry

        lax.fori_loop(begin, end, body, 0)

    fetched = {}

    def fetch(unit_id):
        if unit_id < total and unit_id not in fetched:
            fetched[unit_id] = pltpu.make_async_copy(
                w_ref.at[unit_id], wbuf.at[unit_id % 2], local_sems.at[2 + unit_id % 2]
            )
            fetched[unit_id].start()

    def weight(unit_id, tile):
        return wbuf[unit_id % 2, :, :, :, columns(tile)].reshape(1024, TILE)

    def project(unit_id):
        layer, kind = unit_id // UNITS, unit_id % UNITS
        base = layer * 12
        if kind == 0:
            settle("qkv")
        for copy in flying.pop(("kv", (layer - 1, kind)), ()):
            copy.wait_send()

        def body(tile, carry):
            value = jnp.dot(low[...], weight(unit_id, tile), preferred_element_type=F32)
            cols = columns(tile)
            if kind != 1:
                value = value + rows_ref[pl.ds(base + kind // 2, 1), cols]
            value = value.astype(BF)
            if kind == 0:
                value = (value.astype(F32) * SCORE_SCALE).astype(BF)
            qkv[:, columns(tile + 4 * kind)] = value
            return carry

        lax.fori_loop(0, 4, body, 0)
        if kind:
            spot = 6 + 2 * layer + kind - 1
            src, dst = qkv.at[:, pl.ds(1024 * kind, 1024)], sib.at[layer, kind - 1]
            launch("kv", (layer, kind), [side(spot, src, dst, here["core"])])
        if kind == 2:
            save("qkv", qkv, qkv_ref.at[layer], 1)

    def attention(layer, group):
        if group == 0:
            landed("kv", (layer, 1))
            landed("kv", (layer, 2))
            save("kv", sib.at[layer], kv_ref.at[layer], 2)
            settle("mix")
        heads(layer, 2 * group, 2 * group + 2)
        if group == 3:
            save("mix", mix, mix_ref.at[layer], 3)

    def mixing(unit_id):
        layer = unit_id // UNITS
        base = layer * 12
        settle(("unit", 0), ("scale", 0))

        def body(tile, carry):
            cols = columns(tile)
            value = jnp.dot(mix[...], weight(unit_id, tile), preferred_element_type=F32)
            acc[:, cols] = cur[:, cols] + value + rows_ref[pl.ds(base + 2, 1), cols]
            return carry

        lax.fori_loop(0, 4, body, 0)
        norm(layer, 0, base + 6, base + 4)

    def widen(unit_id):
        layer, j = unit_id // UNITS, unit_id % UNITS // 2 - 2
        base = layer * 12
        settle(("slope", j))

        def body(tile, carry):
            cols = columns(tile)
            value = jnp.dot(nrm[...], weight(unit_id, tile), preferred_element_type=F32)
            value = value + rows_ref[pl.ds(base + 8 + j, 1), cols]
            gate = 0.5 * (1.0 + lax.erf(value * 0.7071067811865476))
            act[j, :, cols] = (value * gate).astype(BF)
            bell = jnp.exp(-0.5 * value * value)
            slope[j, :, cols] = (gate + value * (0.3989422804014327 * bell)).astype(BF)
            return carry

        lax.fori_loop(0, 4, body, 0)
        save(("slope", j), slope.at[j], slope_ref.at[layer, j], 16 + j)

    def narrow(unit_id):
        layer, j = unit_id // UNITS, unit_id % UNITS // 2 - 2
        base = layer * 12

        def body(tile, carry):
            cols = columns(tile)
            acc[:, cols] += jnp.dot(act[j], weight(unit_id, tile), preferred_element_type=F32)
            return carry

        lax.fori_loop(0, 4, body, 0)
        if j == 3:
            settle(("unit", 1), ("scale", 1))
            norm(layer, 1, base + 7, base + 5)
            if layer == layers - 1:
                save("low", low, out_ref, 0)

    turns = [0]

    def flip(source, layer, index):
        slot = turns[0] % 2
        turns[0] += 1
        settle(("flip", slot))

        def body(block, carry):
            for half in range(2):
                lanes = pl.ds(pl.multiple_of(block * 256 + half * 128, 128), 128)
                flipped[slot, half, block] = jnp.transpose(source[:, lanes])
            return carry

        lax.fori_loop(0, 4, body, 0)
        save(("flip", slot), flipped.at[slot], flip_ref.at[layer, index], 4 + slot)

    chunks = []

    def plan_flip(unit_id, source, index):
        part = functools.partial(flip, source, unit_id // UNITS, index)
        chunks.append((unit_id, part, 1.3))

    for unit_id in range(total):
        layer, kind = unit_id // UNITS, unit_id % UNITS
        if kind < 3:
            chunks.append((unit_id, project, 2.0))
            if kind == 0:
                plan_flip(unit_id, low, 0)
        elif kind == 3:
            for group in range(4):
                chunks.append((unit_id - 1, functools.partial(attention, layer, group), 4.5))
            plan_flip(unit_id - 1, mix, 2)
            chunks.append((unit_id, mixing, 4.5))
            plan_flip(unit_id, nrm, 1)
        elif kind % 2 == 0:
            chunks.append((unit_id, widen, 3.5))
            plan_flip(unit_id, act.at[kind // 2 - 2], 3 + kind // 2 - 2)
        else:
            chunks.append((unit_id, narrow, 5.0 if kind == 11 else 1.5))

    def advance(have, budget):
        spent = 0.0
        while chunks and chunks[0][0] <= have and (spent == 0.0 or spent + chunks[0][2] <= budget):
            unit_id, chunk, cost = chunks.pop(0)
            if isinstance(chunk, functools.partial):
                chunk()
            else:
                fetch(unit_id)
                fetched[unit_id].wait()
                chunk(unit_id)
                if unit_id + 2 <= have:
                    fetch(unit_id + 2)
            spent += cost

    ahead, corner_lag, inner_lag, use_lag = LAGS
    step, have = 0, -1
    while step < total + use_lag or chunks:
        if step + ahead < total:
            owns[step + ahead].start()
            launch("along", step + ahead, along(step + ahead))
        if step < total:
            owns[step].wait()
            landed("along", step)
            launch("across", step, across(step))
        if 0 < step < 4:
            small_hop(step)
        if step in TURN_STEPS:
            number = TURN_STEPS.index(step)
            turn_out(number // 2, number % 2)
        if step > BEGIN:
            advance(have, BUDGET)
        if 0 <= step - corner_lag < total:
            landed("across", step - corner_lag)
            launch("corner", step - corner_lag, corner(step - corner_lag))
        if 0 <= step - inner_lag < total:
            landed("corner", step - inner_lag)
            launch("inner", step - inner_lag, inner(step - inner_lag))
        if step == BEGIN:
            begin()
        if 0 <= step - use_lag < total:
            landed("inner", step - use_lag)
            have = step - use_lag
            if have < 2 or have - 2 in fetched and all(item[0] > have - 2 for item in chunks):
                fetch(have)
        if step >= BEGIN:
            advance(have, BUDGET)
        step += 1
    for j in range(2):
        for half in range(2):
            local, away, stays = turn(j, half)
            pl.when(jnp.logical_not(stays))(lambda: away().wait_send())
    for copies in flying.values():
        for copy in copies:
            copy.wait_send()
    settle(*list(saves))


def forward_pass(first, w_qkv, w_out, w_up, w_down, small):
    layers = w_qkv.shape[0]
    width = first.shape[2]
    rows = first.shape[0] * first.shape[1]
    any_spec = pl.BlockSpec(memory_space=pl.ANY)
    vmem = pl.BlockSpec(memory_space=pltpu.VMEM)
    shape = jax.ShapeDtypeStruct
    total = layers * UNITS
    return pl.pallas_call(
        functools.partial(forward_kernel, layers=layers),
        in_specs=[vmem] * 6,
        out_specs=[any_spec, any_spec, vmem, vmem] + [any_spec] * 7,
        out_shape=[
            shape((total, 4, 2, 128, width), BF),
            shape((rows, width), BF),
            shape((layers * 12, width), F32),
            shape((layers, 8, 2, rows), F32),
            shape((layers, rows, 3 * width), BF),
            shape((layers, 2, rows, width), BF),
            shape((layers, rows, width), BF),
            shape((layers, 7, 2, 4, 128, rows), BF),
            shape((layers, 4, rows, width), BF),
            shape((layers, 2, rows, width), F32),
            shape((layers, 2, rows, 128), F32),
        ],
        scratch_shapes=[
            pltpu.VMEM((rows, width), F32),
            pltpu.VMEM((rows, width), BF),
            pltpu.VMEM((rows, 3 * width), BF),
            pltpu.VMEM((layers, 2, rows, width), BF),
            pltpu.VMEM((rows, width), BF),
            pltpu.VMEM((rows, width), BF),
            pltpu.VMEM((rows, width), F32),
            pltpu.VMEM((4, rows, width), BF),
            pltpu.VMEM((4, rows, width), BF),
            pltpu.VMEM((2, rows, width), F32),
            pltpu.VMEM((2, rows, 128), F32),
            pltpu.VMEM((2, 4, 2, 128, width), BF),
            pltpu.VMEM((2, 2, 4, 128, rows), BF),
            pltpu.VMEM((total, 32, width), BF),
            pltpu.VMEM((2, 2, 2, 4, layers * 12, 128), F32),
            pltpu.SemaphoreType.DMA((4,)),
            pltpu.SemaphoreType.DMA((total,)),
            pltpu.SemaphoreType.DMA((20,)),
            pltpu.SemaphoreType.DMA((total, 14)),
            pltpu.SemaphoreType.DMA((total, 14)),
            pltpu.SemaphoreType.DMA((6 + 2 * layers,)),
            pltpu.SemaphoreType.DMA((6 + 2 * layers,)),
            pltpu.SemaphoreType.DMA((4,)),
            pltpu.SemaphoreType.DMA((4,)),
        ],
        compiler_params=pltpu.CompilerParams(
            has_side_effects=True, vmem_limit_bytes=60 << 20
        ),
        name="forward_pass",
    )(first, w_qkv, w_out, w_up, w_down, small)


def backward_kernel(
    top_ref,
    last_ref,
    w_ref,
    rows_ref,
    lse_ref,
    qkv_ref,
    kv_ref,
    mix_ref,
    flip_ref,
    slope_ref,
    unit_ref,
    scale_ref,
    last_out,
    grad_out,
    qkv_out,
    out_out,
    up_out,
    down_out,
    bias_out,
    up_bias_out,
    gain_out,
    grad,
    edge,
    unit,
    scale,
    arena,
    span,
    feat,
    turned,
    wbuf,
    send,
    mine,
    land,
    wide,
    slim,
    ends,
    small_all,
    small_in,
    staged,
    up_all,
    load_sems,
    store_sems,
    send_sems,
    recv_sems,
    side_send,
    side_recv,
    turn_send,
    turn_recv,
    layers,
):
    batch, z, y, x, core = place_of()
    total = layers * UNITS
    here = {"x": (batch ^ 2, z), "y": (batch ^ 4, z), "core": (batch ^ 1, z)}
    slots = 6

    def remote(src, dst, send_sem, recv_sem, device):
        return pltpu.make_async_remote_copy(
            src_ref=src,
            dst_ref=dst,
            send_sem=send_sem,
            recv_sem=recv_sem,
            device_id=device,
            device_id_type=MESH,
        )

    incoming, outgoing = {}, {}

    def launch(kind, number, copies):
        incoming[kind, number] = copies
        outgoing[kind, number] = copies
        for copy in copies:
            copy.start()

    def landed(kind, number):
        for copy in incoming.pop((kind, number)):
            copy.wait_recv()

    def sent(kind, number):
        for copy in outgoing.pop((kind, number), ()):
            copy.wait_send()

    def hop(number, slot, src, dst, device):
        return remote(src, dst, send_sems.at[number, slot], recv_sems.at[number, slot], device)

    def side(slot, src, dst, device):
        return remote(src, dst, side_send.at[slot], side_recv.at[slot], device)

    loads = {}

    def fetch(name, src, dst, slot):
        loads[name] = pltpu.make_async_copy(src, dst, load_sems.at[slot])
        loads[name].start()

    def ready(name):
        loads.pop(name).wait()

    order = []
    for layer in reversed(range(layers)):
        for j in range(4):
            order += [layer * UNITS + 5 + 2 * j, layer * UNITS + 4 + 2 * j]
        order += [layer * UNITS + 3, layer * UNITS, layer * UNITS + 1, layer * UNITS + 2]

    def fetch_weight(number):
        if number < total:
            fetch(("w", number), w_ref.at[order[number]], wbuf.at[number % 2], number % 2)

    def rows_of(number, tile):
        return wbuf[number % 2, tile].reshape(TILE, 1024)

    def fetch_turned(slot, layer, index):
        for half, which in enumerate((core, 1 - core)):
            fetch(
                (slot, half),
                flip_ref.at[layer, index, which],
                turned.at[slot, half],
                10 + 2 * slot + half,
            )

    def ready_turned(slot):
        ready((slot, 0))
        ready((slot, 1))

    def produce(number, slot, upper):
        buffer = number % 2
        sent("core", number - 2)

        def body(tile, carry):
            cols = columns(tile)
            value = jnp.dot(
                turned[slot, 1].reshape(512, 512), upper[:, cols], preferred_element_type=F32
            )
            send[buffer, :, :, cols] = value.astype(BF).reshape(4, 128, TILE)
            return carry

        lax.fori_loop(0, 4, body, 0)
        launch("core", number, [hop(number, 0, send.at[buffer], land.at[number % UNITS], here["core"])])

        def own(tile, carry):
            cols = columns(tile)
            value = jnp.dot(
                turned[slot, 0].reshape(512, 512), upper[:, cols], preferred_element_type=F32
            )
            mine[number % slots, :, :, cols] = value.astype(BF).reshape(4, 128, TILE)
            return carry

        lax.fori_loop(0, 4, own, 0)

    left, right = pl.ds(0, 512), pl.ds(512, 512)

    def stage_core(number):
        part = land.at[number % UNITS]
        landed("core", number)

        def body(block, carry):
            part[block] = part[block] + mine[number % slots, block]
            return carry

        lax.fori_loop(0, 4, body, 0)
        spot = number % slots
        launch(
            "wide",
            number,
            [
                hop(number, 1, part.at[pl.ds(2 - 2 * y, 2), :, left], wide.at[spot, 0], here["y"]),
                hop(number, 2, part.at[pl.ds(1 - x, 1), :, right], wide.at[spot, 1, pl.ds(0, 1)], here["x"]),
                hop(number, 3, part.at[pl.ds(3 - x, 1), :, right], wide.at[spot, 1, pl.ds(1, 1)], here["x"]),
            ],
        )

    def stage_wide(number):
        part, spot = land.at[number % UNITS], number % slots
        landed("wide", number)
        for block in range(2):
            spot_y = 2 * y + block
            part[spot_y, :, left] = part[spot_y, :, left] + wide[spot, 0, block]
            spot_x = 2 * block + x
            part[spot_x, :, right] = part[spot_x, :, right] + wide[spot, 1, block]
        launch(
            "slim",
            number,
            [
                hop(number, 4, part.at[2 * y + 1 - x, :, left], slim.at[spot, 0], here["x"]),
                hop(number, 5, part.at[2 - 2 * y + x, :, right], slim.at[spot, 1], here["y"]),
            ],
        )

    def stage_slim(number):
        part, spot = land.at[number % UNITS, 2 * y + x], number % slots
        landed("slim", number)
        part[:, left] = part[:, left] + slim[spot, 0]
        part[:, right] = part[:, right] + slim[spot, 1]
        copies = []
        for step in (1, 2, 3):
            to = lax.rem(z + step, 4)
            src = part.at[pl.ds(pl.multiple_of(to * 32, 32), 32)]
            copies.append(hop(number, 5 + step, src, ends.at[spot, step - 1], (batch, to)))
        launch("ends", number, copies)

    def stage_ends(number):
        part, spot = land.at[number % UNITS, 2 * y + x], number % slots
        landed("ends", number)
        value = part[pl.ds(pl.multiple_of(z * 32, 32), 32)].astype(F32)
        for step in range(3):
            value = value + ends[spot, step].astype(F32)
        layer, kind = order[number] // UNITS, order[number] % UNITS
        j = kind // 2 - 2
        if kind > 3 and kind % 2 == 0:
            lane = lax.broadcasted_iota(jnp.int32, (32, 128), 1) // 32
            if j == 0 and 4 in stores:
                stores.pop(4).wait()
            for block in range(32):
                spot = pl.ds(block * 128, 128)
                piece = value[:, block // 4 * 128 : block // 4 * 128 + 128]
                if j != block % 4:
                    piece = pltpu.roll(piece, ((j - block % 4) * 32) % 128, 1)
                up_all[:, spot] = piece if j == 0 else jnp.where(lane == j, piece, up_all[:, spot])
            if j == 3:
                stores[4] = pltpu.make_async_copy(up_all, up_out.at[layer], store_sems.at[4])
                stores[4].start()
        else:
            slot = number % 4
            if slot in stores:
                stores.pop(slot).wait()
            staged[slot] = value
            if kind < 3:
                dst = qkv_out.at[layer, :, pl.ds(1024 * kind, 1024)]
            else:
                dst = out_out.at[layer] if kind == 3 else down_out.at[layer, j]
            stores[slot] = pltpu.make_async_copy(staged.at[slot], dst, store_sems.at[slot])
            stores[slot].start()
        for kind in ("wide", "slim", "ends"):
            sent(kind, number)

    ticks = [0]
    stores = {}
    wide_lag, slim_lag, ends_lag = BACK_LAGS

    def first_half():
        step = ticks[0]
        if step < total:
            stage_core(step)
        if 0 <= step - wide_lag < total:
            stage_wide(step - wide_lag)

    def second_half():
        step = ticks[0]
        ticks[0] += 1
        if 0 <= step - slim_lag < total:
            stage_slim(step - slim_lag)
        if 0 <= step - ends_lag < total:
            stage_ends(step - ends_lag)

    def tick():
        first_half()
        second_half()

    def norm(base, gain_row, shift_row, sum_row):
        gain = rows_ref[pl.ds(base + gain_row, 1)]

        def body(step, carry):
            gains, shifts, sums = carry
            rows = pl.ds(step * 64, 64)
            value = grad[rows]
            normal = unit[rows]
            scaled = value * gain
            inner = jnp.mean(scaled * normal, -1, keepdims=True)
            centre = jnp.mean(scaled, -1, keepdims=True)
            result = scale[rows][:, :1] * (scaled - centre - normal * inner)
            grad[rows] = result
            rounded = result.astype(BF)
            edge[rows] = rounded
            return (
                gains + jnp.sum(value * normal, 0, keepdims=True),
                shifts + jnp.sum(value, 0, keepdims=True),
                sums + jnp.sum(rounded.astype(F32), 0, keepdims=True),
            )

        zero = jnp.zeros((1, 1024), F32)
        gains, shifts, sums = lax.fori_loop(0, 8, body, (zero, zero, zero))
        put_row(base + gain_row, gains)
        put_row(base + shift_row, shifts)
        put_row(base + sum_row, sums)

    def put_row(row, value):
        for block in range(8):
            small_all[block // 2, block % 2, row : row + 1] = value[:, block * 128 : block * 128 + 128]

    def heads(layer, begin, end):
        def body(j, carry):
            lanes = pl.ds(pl.multiple_of(j * 128, 128), 128)
            q = arena[0, :, lanes]
            do = span[:, lanes]
            lane = lax.broadcasted_iota(jnp.int32, q.shape, 1)
            prod = jnp.transpose(do.astype(F32) * feat[:, lanes].astype(F32))
            dq = []
            sums = [[None, None], [None, None]]
            for head in range(2):
                pick = (lane // 64) == head
                qh = jnp.where(pick, q, jnp.zeros_like(q))
                dh = jnp.where(pick, do, jnp.zeros_like(do))
                delta = jnp.sum(prod[head * 64 : head * 64 + 64], 0, keepdims=True)
                lse = lse_ref[layer, j, pl.ds(head, 1)]
                dqh = None
                for half in range(2):
                    k = arena[1 + 2 * half, :, lanes]
                    v = arena[2 + 2 * half, :, lanes]
                    p = jnp.exp(dot(k, qh, NT) - lse)
                    ds = (p * (dot(v, dh, NT) - delta)).astype(BF)
                    dv = jnp.dot(p.astype(BF), dh, preferred_element_type=F32)
                    dk = jnp.dot(ds, qh, preferred_element_type=F32)
                    part = dot(ds, k, TN)
                    dqh = part if dqh is None else dqh + part
                    sums[half][0] = dk if head == 0 else sums[half][0] + dk
                    sums[half][1] = dv if head == 0 else sums[half][1] + dv
                dq.append(dqh)
            arena[5, :, lanes] = (jnp.where(lane < 64, dq[0], dq[1]) * SCORE_SCALE).astype(BF)
            arena[6, :, lanes] = sums[0][0].astype(BF)
            arena[7, :, lanes] = sums[0][1].astype(BF)
            arena[8, :, lanes] = sums[1][0].astype(BF)
            arena[9, :, lanes] = sums[1][1].astype(BF)
            return carry

        lax.fori_loop(begin, end, body, 0)

    def row_sum(row, slot):
        def body(step, carry):
            rows = pl.ds(pl.multiple_of(step * 64, 64), 64)
            return carry + jnp.sum(arena[slot, rows].astype(F32), 0, keepdims=True)

        put_row(row, lax.fori_loop(0, 8, body, jnp.zeros((1, 1024), F32)))

    def pull(number, upper):
        def body(tile, carry):
            cols = columns(tile)
            grad[:, cols] += dot(upper[...], rows_of(number, tile), NT)
            return carry

        ready(("w", number))
        lax.fori_loop(0, 4, body, 0)
        fetch_weight(number + 2)

    def load_attention(layer):
        for part in range(3):
            fetch(("qkv", part), qkv_ref.at[layer, :, pl.ds(1024 * part, 1024)], arena.at[part], 2 + part)
        for part in range(2):
            fetch(("kv", part), kv_ref.at[layer, part], arena.at[3 + part], 5 + part)

    column = 4 * y + 2 * x
    seat = 2 * lax.rem(z, 2) + core
    stays = core == z // 2

    def homeward(which, block, src, dst):
        rows = src.at[pl.ds(block * 128, 128)]
        spot = dst.at[lax.rem(z, 2), pl.ds(pl.multiple_of(core * 128, 128), 128)]
        to = (column + z // 2, lax.rem(z - block + 4, 4))
        return (
            lambda: pltpu.make_async_copy(rows, spot, load_sems.at[14 + which]),
            lambda: remote(rows, spot, turn_send.at[which, block], turn_recv.at[which, seat], to),
        )

    def turn_start(which, src, dst):
        for block in range(4):
            local, away = homeward(which, block, src, dst)
            if block:
                away().start()
            else:
                pl.when(stays)(lambda: local().start())
                pl.when(jnp.logical_not(stays))(lambda: away().start())

    def turn_end(which, src, dst):
        for block in range(4):
            local, away = homeward(which, block, src, dst)
            if block:
                away().wait_send()
            else:
                pl.when(stays)(lambda: local().wait())
                pl.when(jnp.logical_not(stays))(lambda: away().wait_send())
        for place in range(4):
            spot = dst.at[place // 2, pl.ds(place % 2 * 128, 128)]
            came = remote(spot, spot, turn_send.at[which, 0], turn_recv.at[which, place], here["core"])
            own = jnp.logical_and(2 * core + place // 2 == z, core == place % 2)
            pl.when(jnp.logical_not(own))(came.wait_recv)

    fetch("top", top_ref, grad, 7)
    turn_start(0, last_ref, last_out)
    first = True
    for layer in reversed(range(layers)):
        base = layer * 12
        start = (layers - 1 - layer) * UNITS
        if first:
            fetch("unit", unit_ref.at[layer, 1], unit, 8)
            fetch("scale", scale_ref.at[layer, 1], scale, 9)
            fetch_weight(0)
            fetch_weight(1)
            load_attention(layer)
            ready("top")
            fetch_turned(0, layer, 1)
            fetch_turned(1, layer, 3)
        fetch("slope", slope_ref.at[layer, 0], arena.at[9], 16)
        fetch("mix", mix_ref.at[layer], feat, 17)
        first = False
        ready("unit")
        ready("scale")
        norm(base, 7, 5, 3)
        fetch("unit", unit_ref.at[layer, 0], unit, 8)
        fetch("scale", scale_ref.at[layer, 0], scale, 9)
        ready_turned(0)
        for j in range(4):
            number = start + 2 * j
            ready_turned(1)
            produce(number, 1, edge)
            fetch_turned(1, layer, 4 + j if j < 3 else 2)
            ready(("w", number))
            ready("slope")

            def body(tile, carry):
                cols = columns(tile)
                value = dot(edge[...], rows_of(number, tile), NT)
                value = (arena[9, :, cols].astype(F32) * value).astype(BF)
                span[:, cols] = value
                total_row = jnp.sum(value.astype(F32), 0, keepdims=True)
                for block in range(2):
                    small_all[tile, block, pl.ds(base + 8 + j, 1)] = total_row[
                        :, block * 128 : block * 128 + 128
                    ]
                return carry

            lax.fori_loop(0, 4, body, 0)
            fetch_weight(number + 2)
            if j < 3:
                fetch("slope", slope_ref.at[layer, j + 1], arena.at[9], 16)
            first_half()
            produce(number + 1, 0, span)
            pull(number + 1, span)
            second_half()
        ready("unit")
        ready("scale")
        norm(base, 6, 4, 2)
        if layer:
            fetch("unit", unit_ref.at[layer - 1, 1], unit, 8)
            fetch("scale", scale_ref.at[layer - 1, 1], scale, 9)
        fetch_turned(0, layer, 0)
        ready("mix")
        ready_turned(1)
        number = start + 8
        ready(("w", number))

        def body(tile, carry):
            span[:, columns(tile)] = dot(edge[...], rows_of(number, tile), NT).astype(BF)
            return carry

        lax.fori_loop(0, 4, body, 0)
        fetch_weight(number + 2)
        tick()
        produce(number, 1, edge)
        if layer:
            fetch_turned(1, layer - 1, 3)
        for part in range(3):
            ready(("qkv", part))
        for part in range(2):
            ready(("kv", part))
        for group in range(4):
            heads(layer, 2 * group, 2 * group + 2)
            tick()
        place = layers - 1 - layer
        for part in range(2):
            launch(
                "keys",
                2 * place + part,
                [side(2 * place + part, arena.at[8 + part], arena.at[10 + part], here["core"])],
            )
        if layer:
            load_attention(layer - 1)
        ready_turned(0)
        for part in range(3):
            number = start + 9 + part
            if part:
                landed("keys", 2 * place + part - 1)

                def body(step, carry):
                    rows = pl.ds(pl.multiple_of(step * 64, 64), 64)
                    arena[5 + part, rows] = arena[5 + part, rows] + arena[9 + part, rows]
                    return carry

                lax.fori_loop(0, 8, body, 0)
            if part != 1:
                row_sum(base + part // 2, 5 + part)
            produce(number, 0, arena.at[5 + part])
            pull(number, arena.at[5 + part])
            if part < 2:
                tick()
            elif layer:
                fetch_turned(0, layer - 1, 1)
        sent("keys", 2 * place)
        sent("keys", 2 * place + 1)
        if layer == 0:

            def body(step, carry):
                rows = pl.ds(pl.multiple_of(step * 64, 64), 64)
                edge[rows] = grad[rows].astype(BF)
                return carry

            lax.fori_loop(0, 8, body, 0)
            turn_start(1, edge, grad_out)
        tick()
    base = 2 * layers

    def small_core():
        launch("small", 0, [side(base, small_all.at[:, 1 - core], small_in.at[pl.ds(0, 4)], here["core"])])

    def small_y():
        landed("small", 0)
        sent("small", 0)
        small_all[:, core] = small_all[:, core] + small_in[0:4]
        launch(
            "small",
            1,
            [side(base + 1, small_all.at[pl.ds(2 - 2 * y, 2), core], small_in.at[pl.ds(4, 2)], here["y"])],
        )

    def small_x():
        landed("small", 1)
        sent("small", 1)
        for block in range(2):
            small_all[2 * y + block, core] = small_all[2 * y + block, core] + small_in[4 + block]
        launch(
            "small",
            2,
            [side(base + 2, small_all.at[2 * y + 1 - x, core], small_in.at[6], here["x"])],
        )

    def small_z():
        landed("small", 2)
        sent("small", 2)
        own = small_all.at[2 * y + x, core]
        own[...] = own[...] + small_in[6]
        launch(
            "small",
            3,
            [
                side(base + 2 + step, own, small_in.at[6 + step], (batch, lax.rem(z + step, 4)))
                for step in (1, 2, 3)
            ],
        )

    def small_end():
        landed("small", 3)
        sent("small", 3)
        value = small_all[2 * y + x, core]
        for step in (1, 2, 3):
            value = value + small_in[6 + step]
        mine_row = value[:, 0:32]
        for place in range(1, 4):
            mine_row = jnp.where(z == place, value[:, place * 32 : place * 32 + 32], mine_row)
        for layer in range(layers):
            top = layer * 12
            bias_out[layer] = mine_row[top : top + 6]
            gain_out[layer] = mine_row[top + 6 : top + 8]
            for j in range(4):
                up_bias_out[layer : layer + 1, j * 32 : j * 32 + 32] = mine_row[top + 8 + j : top + 9 + j]

    queue = [small_core, small_y, small_x, small_z, small_end]
    while ticks[0] < total + ends_lag or queue:
        if queue:
            queue.pop(0)()
        if ticks[0] < total + ends_lag:
            tick()
    for kind, number in list(outgoing):
        sent(kind, number)
    for copy in stores.values():
        copy.wait()
    turn_end(0, last_ref, last_out)
    turn_end(1, edge, grad_out)


BACK_LAGS = (2, 4, 5)


def backward_pass(top, last, saved):
    w, rows, lse, qkv, kv, mix, flip, slope, unit, scale = saved
    total = w.shape[0]
    layers = total // UNITS
    tokens, width = top.shape
    any_spec = pl.BlockSpec(memory_space=pl.ANY)
    vmem = pl.BlockSpec(memory_space=pltpu.VMEM)
    shape = jax.ShapeDtypeStruct
    return pl.pallas_call(
        functools.partial(backward_kernel, layers=layers),
        in_specs=[any_spec] * 3 + [vmem, vmem] + [any_spec] * 7,
        out_specs=[any_spec] * 6 + [vmem] * 3,
        out_shape=[
            shape((2, tokens // 2, width), BF),
            shape((2, tokens // 2, width), BF),
            shape((layers, 32, 3 * width), F32),
            shape((layers, 32, width), F32),
            shape((layers, 32, 4 * width), F32),
            shape((layers, 4, 32, width), F32),
            shape((layers, 6, 32), F32),
            shape((layers, 128), F32),
            shape((layers, 2, 32), F32),
        ],
        scratch_shapes=[
            pltpu.VMEM((tokens, width), F32),
            pltpu.VMEM((tokens, width), BF),
            pltpu.VMEM((tokens, width), F32),
            pltpu.VMEM((tokens, 128), F32),
            pltpu.VMEM((12, tokens, width), BF),
            pltpu.VMEM((tokens, width), BF),
            pltpu.VMEM((tokens, width), BF),
            pltpu.VMEM((2, 2, 4, 128, tokens), BF),
            pltpu.VMEM((2, 4, 2, 128, width), BF),
            pltpu.VMEM((2, 4, 128, width), BF),
            pltpu.VMEM((6, 4, 128, width), BF),
            pltpu.VMEM((UNITS, 4, 128, width), BF),
            pltpu.VMEM((6, 2, 2, 128, width // 2), BF),
            pltpu.VMEM((6, 2, 128, width // 2), BF),
            pltpu.VMEM((6, 3, 32, width), BF),
            pltpu.VMEM((4, 2, layers * 12, 128), F32),
            pltpu.VMEM((10, layers * 12, 128), F32),
            pltpu.VMEM((4, 32, width), F32),
            pltpu.VMEM((32, 4 * width), F32),
            pltpu.SemaphoreType.DMA((18,)),
            pltpu.SemaphoreType.DMA((5,)),
            pltpu.SemaphoreType.DMA((total, 9)),
            pltpu.SemaphoreType.DMA((total, 9)),
            pltpu.SemaphoreType.DMA((2 * layers + 6,)),
            pltpu.SemaphoreType.DMA((2 * layers + 6,)),
            pltpu.SemaphoreType.DMA((2, 4)),
            pltpu.SemaphoreType.DMA((2, 4)),
        ],
        compiler_params=pltpu.CompilerParams(has_side_effects=True, vmem_limit_bytes=60 << 20),
        name="backward_pass",
    )(top, last, w, rows, lse, qkv, kv, mix, flip, slope, unit, scale)


def swap(value, bit):
    return lax.ppermute(value, "batch", [(place, place ^ bit) for place in range(8)])


def take(value, index, axis):
    return lax.dynamic_index_in_dim(value, index, axis, keepdims=False)


def small_rows(biases, up_bias, gains):
    layers = biases.shape[0]
    rows = jnp.concatenate((biases, gains, up_bias.reshape(layers, 4, 32)), 1).astype(F32)
    wide = jnp.tile(rows.reshape(layers * 12, 32), (1, 4))
    lane = lax.broadcasted_iota(jnp.int32, wide.shape, 1)
    return jnp.where(lane // 32 == lax.axis_index("blk"), wide, 0.0)


def column_shards(
    hidden_in,
    mask_index,
    mask_count,
    replacement,
    out_grad,
    w_qkv,
    w_out,
    w_up,
    w_down,
    biases,
    up_bias,
    gains,
):
    batch = lax.axis_index("batch")
    z = lax.axis_index("blk")
    core = lax.rem(batch, 2)
    seq_count, block_len, width = hidden_in.shape
    layers = w_qkv.shape[0]
    slots = mask_index.shape[1]
    per = width // 32

    slot_ids = jnp.arange(slots, dtype=jnp.int32)
    used = slot_ids[None, :] < mask_count[:, None]
    slot_place = jnp.where(used, mask_index, -1)
    places = z * block_len + jnp.arange(block_len, dtype=jnp.int32)
    hits = slot_place[:, None, :] == places[None, :, None]
    placed = jnp.einsum("sbm,smd->sbd", hits.astype(BF), replacement, preferred_element_type=F32)
    first = jnp.where(jnp.any(hits, -1, keepdims=True), placed.astype(BF), hidden_in)

    mine = lax.rem(z, 2)
    came_grad = swap(take(out_grad, mine, 0), 1)
    came_place = swap(take(slot_place, mine, 0).astype(F32), 1)
    here = (z // 2) == core
    top_grad = jnp.where(here, take(out_grad, mine, 0), came_grad)
    top_place = jnp.where(here, take(slot_place, mine, 0), came_place.astype(jnp.int32))
    blocks = lax.rem(z - jnp.arange(4, dtype=jnp.int32) + 4, 4)
    token_place = (
        blocks[:, None] * block_len
        + core * (block_len // 2)
        + jnp.arange(block_len // 2, dtype=jnp.int32)[None, :]
    ).reshape(-1)
    top_hits = (token_place[:, None] == top_place[None, :]).astype(BF)
    upstream = jnp.dot(top_hits, top_grad, preferred_element_type=F32)

    results = forward_pass(first, w_qkv, w_out, w_up, w_down, small_rows(biases, up_bias, gains))
    last, grad, qkv, out, up, down, bias_rows, up_rows, gain_rows = backward_pass(
        upstream, results[1], (results[0],) + tuple(results[2:])
    )
    return (
        last,
        grad.astype(F32),
        qkv,
        out,
        up,
        down.reshape(layers, 4 * per, width),
        bias_rows,
        up_rows,
        gain_rows,
    )


def solution(mesh):
    fits = mesh.shape["batch"] == 8 and mesh.shape["blk"] == 4
    return jax.shard_map(
        column_shards if fits else general_shards,
        mesh=mesh,
        in_specs=(
            P(*BOTH, None),
            P("batch", None),
            P("batch"),
            P("batch", None, None),
            P("batch", None, None),
            P(None, BOTH, None),
            P(None, BOTH, None),
            P(None, BOTH, None),
            P(None, BOTH, None),
            P(None, None, BOTH),
            P(None, BOTH),
            P(None, None, BOTH),
        ),
        out_specs=(
            P(*BOTH, None),
            P(*BOTH, None),
            P(None, BOTH, None),
            P(None, BOTH, None),
            P(None, BOTH, None),
            P(None, BOTH, None),
            P(None, None, BOTH),
            P(None, BOTH),
            P(None, None, BOTH),
        ),
        check_vma=False,
    )
```

```python
import functools

import jax
import jax.numpy as jnp
from jax import lax
from jax.experimental import pallas as pl
from jax.experimental.pallas import tpu as pltpu
from jax.sharding import PartitionSpec as P

HEADS = 16


BOTH = ("batch", "blk")
NORM_EPS = 1e-12
SCORE_SCALE = 0.125


def norm_rows(values, gain, shift):
    center = values - jnp.mean(values, -1, keepdims=True)
    spread = jnp.mean(center * center, -1, keepdims=True)
    return center * lax.rsqrt(spread + NORM_EPS) * gain + shift


def gelu_exact(values):
    return 0.5 * values * (1.0 + jax.scipy.special.erf(values * 0.7071067811865476))


def forward_layer(inputs, fetched, head_shape):
    qkv_weight, out_weight, up_weight, down_weight, bias_rows, up_shift, gain_rows = fetched
    bias_rows = bias_rows.astype(jnp.float32)
    up_shift = up_shift.astype(jnp.float32)
    gain_rows = gain_rows.astype(jnp.float32)
    seq_count, block_len, head_count, head_dim = head_shape
    model_width = head_count * head_dim
    inputs_low = inputs.astype(jnp.bfloat16)
    project = jnp.einsum("sbd,de->sbe", inputs_low, qkv_weight, preferred_element_type=jnp.float32)
    query = (project[..., :model_width] + bias_rows[0]).astype(jnp.bfloat16).reshape(head_shape)
    keys = project[..., model_width : 2 * model_width].astype(jnp.bfloat16).reshape(head_shape)
    values = (
        (project[..., 2 * model_width :] + bias_rows[1]).astype(jnp.bfloat16).reshape(head_shape)
    )
    stat_shape = (seq_count, head_count, block_len)
    top_now = jnp.full(stat_shape, -1e30, jnp.float32)
    key_part = lax.all_gather(keys, "blk", axis=1, tiled=True)
    value_part = lax.all_gather(values, "blk", axis=1, tiled=True)
    scores = (
        jnp.einsum("sqhd,skhd->shqk", query, key_part, preferred_element_type=jnp.float32)
        * SCORE_SCALE
    )
    top_next = jnp.maximum(top_now, jnp.max(scores, -1))
    weights_now = jnp.exp(scores - top_next[..., None])
    total_next = jnp.sum(weights_now, -1)
    acc_next = jnp.einsum(
        "shqk,skhd->shqd",
        weights_now.astype(jnp.bfloat16),
        value_part,
        preferred_element_type=jnp.float32,
    )
    log_total = top_next + jnp.log(total_next)
    attended = (acc_next / total_next[..., None]).transpose(0, 2, 1, 3).reshape(inputs.shape)
    attended_low = attended.astype(jnp.bfloat16)
    mixed = (
        inputs
        + jnp.einsum("sbe,ed->sbd", attended_low, out_weight, preferred_element_type=jnp.float32)
        + bias_rows[2]
    )
    normed, first_pull = jax.vjp(norm_rows, mixed, gain_rows[0], bias_rows[4])
    normed_low = normed.astype(jnp.bfloat16)
    hidden = (
        jnp.einsum("sbd,df->sbf", normed_low, up_weight, preferred_element_type=jnp.float32)
        + up_shift
    )
    active, gelu_pull = jax.vjp(gelu_exact, hidden)
    active_low = active.astype(jnp.bfloat16)
    second = (
        normed
        + jnp.einsum("sbf,fd->sbd", active_low, down_weight, preferred_element_type=jnp.float32)
        + bias_rows[3]
    )
    result, second_pull = jax.vjp(norm_rows, second, gain_rows[1], bias_rows[5])
    kept = (
        inputs_low,
        query,
        keys,
        values,
        log_total,
        attended,
        attended_low,
        normed_low,
        active_low,
        first_pull,
        gelu_pull,
        second_pull,
    )
    return (result, kept)


def backward_layer(upstream, fetched, kept, head_shape):
    qkv_weight, out_weight, up_weight, down_weight = (
        fetched[0],
        fetched[1],
        fetched[2],
        fetched[3],
    )
    (
        inputs_low,
        query,
        keys,
        values,
        log_total,
        attended,
        attended_low,
        normed_low,
        active_low,
        first_pull,
        gelu_pull,
        second_pull,
    ) = kept
    seq_count, block_len, head_count, head_dim = head_shape
    row_axes = (0, 1)
    second_grad, gain_two, shift_two = second_pull(upstream)
    down_in = second_grad.astype(jnp.bfloat16)
    down_grad = jnp.einsum("sbf,sbd->fd", active_low, down_in, preferred_element_type=jnp.float32)
    down_shift = jnp.sum(down_in.astype(jnp.float32), row_axes)
    active_grad = jnp.einsum(
        "sbd,fd->sbf", down_in, down_weight, preferred_element_type=jnp.float32
    )
    hidden_grad = gelu_pull(active_grad)[0].astype(jnp.bfloat16)
    up_grad = jnp.einsum("sbd,sbf->df", normed_low, hidden_grad, preferred_element_type=jnp.float32)
    up_shift_grad = jnp.sum(hidden_grad.astype(jnp.float32), row_axes)
    normed_grad = second_grad + jnp.einsum(
        "sbf,df->sbd", hidden_grad, up_weight, preferred_element_type=jnp.float32
    )
    mixed_grad, gain_one, shift_one = first_pull(normed_grad)
    out_in = mixed_grad.astype(jnp.bfloat16)
    out_weight_grad = jnp.einsum(
        "sbe,sbd->ed", attended_low, out_in, preferred_element_type=jnp.float32
    )
    out_shift = jnp.sum(out_in.astype(jnp.float32), row_axes)
    attend_grad = (
        jnp.einsum("sbd,ed->sbe", out_in, out_weight, preferred_element_type=jnp.float32)
        .astype(jnp.bfloat16)
        .reshape(head_shape)
    )
    delta_rows = jnp.sum(attend_grad.astype(jnp.float32) * attended.reshape(head_shape), -1)
    lse_rows = log_total.transpose(0, 2, 1)
    lse_all, delta_all = (
        lax.all_gather(lse_rows, "blk", axis=1, tiled=True),
        lax.all_gather(delta_rows, "blk", axis=1, tiled=True),
    )
    delta_heads = delta_rows.transpose(0, 2, 1)
    key_part = lax.all_gather(keys, "blk", axis=1, tiled=True)
    value_part = lax.all_gather(values, "blk", axis=1, tiled=True)
    scores = (
        jnp.einsum("sqhd,skhd->shqk", query, key_part, preferred_element_type=jnp.float32)
        * SCORE_SCALE
    )
    probs = jnp.exp(scores - log_total[..., None])
    prob_grad = jnp.einsum(
        "sqhd,skhd->shqk", attend_grad, value_part, preferred_element_type=jnp.float32
    )
    score_grad = (probs * (prob_grad - delta_heads[..., None])).astype(jnp.bfloat16)
    query_grad = (
        jnp.einsum("shqk,skhd->sqhd", score_grad, key_part, preferred_element_type=jnp.float32)
        * SCORE_SCALE
    )
    query_part = lax.all_gather(query, "blk", axis=1, tiled=True)
    grad_part = lax.all_gather(attend_grad, "blk", axis=1, tiled=True)
    lse_part = lse_all.transpose(0, 2, 1)
    delta_part = delta_all.transpose(0, 2, 1)
    scores = (
        jnp.einsum("sqhd,skhd->shqk", query_part, keys, preferred_element_type=jnp.float32)
        * SCORE_SCALE
    )
    probs = jnp.exp(scores - lse_part[..., None])
    value_acc = jnp.einsum(
        "shqk,sqhd->skhd", probs.astype(jnp.bfloat16), grad_part, preferred_element_type=jnp.float32
    )
    prob_grad = jnp.einsum("sqhd,skhd->shqk", grad_part, values, preferred_element_type=jnp.float32)
    score_grad = (probs * (prob_grad - delta_part[..., None])).astype(jnp.bfloat16)
    key_acc = (
        jnp.einsum("shqk,sqhd->skhd", score_grad, query_part, preferred_element_type=jnp.float32)
        * SCORE_SCALE
    )
    flat_shape = (seq_count, block_len, head_count * head_dim)
    query_low = query_grad.reshape(flat_shape).astype(jnp.bfloat16)
    key_low = key_acc.reshape(flat_shape).astype(jnp.bfloat16)
    value_low = value_acc.reshape(flat_shape).astype(jnp.bfloat16)
    proj_grad = jnp.concatenate((query_low, key_low, value_low), -1)
    qkv_grad = jnp.einsum("sbd,sbe->de", inputs_low, proj_grad, preferred_element_type=jnp.float32)
    query_shift = jnp.sum(query_low.astype(jnp.float32), row_axes)
    value_shift = jnp.sum(value_low.astype(jnp.float32), row_axes)
    inputs_grad = mixed_grad + jnp.einsum(
        "sbe,de->sbd", proj_grad, qkv_weight, preferred_element_type=jnp.float32
    )
    shift_rows = jnp.stack((query_shift, value_shift, out_shift, down_shift, shift_one, shift_two))
    gain_grad = jnp.stack((gain_one, gain_two))
    return (
        inputs_grad,
        (qkv_grad, out_weight_grad, up_grad, down_grad, shift_rows, up_shift_grad, gain_grad),
    )


def general_shards(
    hidden_in,
    mask_index,
    mask_count,
    replacement,
    out_grad,
    w_qkv,
    w_out,
    w_up,
    w_down,
    biases,
    up_bias,
    gains,
):
    seq_count, block_len, model_width = hidden_in.shape
    layer_count = w_qkv.shape[0]
    head_shape = (seq_count, block_len, HEADS, model_width // HEADS)
    offset = lax.axis_index("blk") * block_len
    places = offset + jnp.arange(block_len, dtype=jnp.int32)
    slot_ids = jnp.arange(mask_index.shape[1], dtype=jnp.int32)
    hit_table = (mask_index[:, None, :] == places[None, :, None]) & (
        slot_ids[None, None, :] < mask_count[:, None, None]
    )
    hit_low = hit_table.astype(jnp.bfloat16)
    chosen = jnp.any(hit_table, -1, keepdims=True)
    placed = jnp.einsum("sbm,smd->sbd", hit_low, replacement, preferred_element_type=jnp.float32)
    current = jnp.where(chosen, placed, hidden_in.astype(jnp.float32))
    upstream = jnp.einsum("sbm,smd->sbd", hit_low, out_grad, preferred_element_type=jnp.float32)
    shard_shapes = (w_qkv.shape[1:], w_out.shape[1:], w_up.shape[1:], w_down.shape[1:])
    saved_weights = []
    saved_state = []
    for layer_idx in range(layer_count):
        fetched = (
            lax.all_gather(w_qkv[layer_idx], BOTH, axis=0, tiled=True),
            lax.all_gather(w_out[layer_idx], BOTH, axis=0, tiled=True),
            lax.all_gather(w_up[layer_idx], BOTH, axis=0, tiled=True),
            lax.all_gather(w_down[layer_idx], BOTH, axis=0, tiled=True),
            lax.all_gather(biases[layer_idx], BOTH, axis=1, tiled=True),
            lax.all_gather(up_bias[layer_idx], BOTH, axis=0, tiled=True),
            lax.all_gather(gains[layer_idx], BOTH, axis=1, tiled=True),
        )
        saved_weights.append(None)
        current, state = forward_layer(current, fetched, head_shape)
        saved_state.append(state)
    grad_now = upstream
    summed = [None] * layer_count
    for layer_idx in reversed(range(layer_count)):
        fetched = (
            lax.all_gather(w_qkv[layer_idx], BOTH, axis=0, tiled=True),
            lax.all_gather(w_out[layer_idx], BOTH, axis=0, tiled=True),
            lax.all_gather(w_up[layer_idx], BOTH, axis=0, tiled=True),
            lax.all_gather(w_down[layer_idx], BOTH, axis=0, tiled=True),
            lax.all_gather(biases[layer_idx], BOTH, axis=1, tiled=True),
            lax.all_gather(up_bias[layer_idx], BOTH, axis=0, tiled=True),
            lax.all_gather(gains[layer_idx], BOTH, axis=1, tiled=True),
        )
        grad_now, terms = backward_layer(grad_now, fetched, saved_state[layer_idx], head_shape)
        flat_terms = (
            terms[0].reshape(-1, 128),
            terms[1].reshape(-1, 128),
            terms[2].reshape(-1, 128),
            terms[3].reshape(-1, 128),
            terms[4],
            terms[5],
            terms[6],
        )
        reduced = (
            lax.psum_scatter(flat_terms[0], BOTH, scatter_dimension=0, tiled=True),
            lax.psum_scatter(flat_terms[1], BOTH, scatter_dimension=0, tiled=True),
            lax.psum_scatter(flat_terms[2], BOTH, scatter_dimension=0, tiled=True),
            lax.psum_scatter(flat_terms[3], BOTH, scatter_dimension=0, tiled=True),
            lax.psum_scatter(flat_terms[4], BOTH, scatter_dimension=1, tiled=True),
            lax.psum_scatter(flat_terms[5], BOTH, scatter_dimension=0, tiled=True),
            lax.psum_scatter(flat_terms[6], BOTH, scatter_dimension=1, tiled=True),
        )
        summed[layer_idx] = tuple(
            (reduced[member].reshape(shard_shapes[member]) for member in range(4))
        ) + tuple(reduced[4:])
    stacked = [jnp.stack([entry[member] for entry in summed]) for member in range(7)]
    return (
        current.astype(jnp.bfloat16),
        grad_now,
        stacked[0],
        stacked[1],
        stacked[2],
        stacked[3],
        stacked[4],
        stacked[5],
        stacked[6],
    )


NT = (((1,), (1,)), ((), ()))
TN = (((0,), (0,)), ((), ()))
F32 = jnp.float32
BF = jnp.bfloat16


def dot(a, b, dims):
    return lax.dot_general(a, b, dims, preferred_element_type=F32)


MESH = pl.DeviceIdType.MESH
UNITS = 12
TILE = 256
LAGS = (3, 1, 3, 4)
DIRECT = 8
TURN_STEPS = (0, 2, 4, 6)
BEGIN = 9
BUDGET = 4.5


def place_of():
    batch = lax.axis_index("batch")
    return batch, lax.axis_index("blk"), batch // 4, lax.rem(batch // 2, 2), lax.rem(batch, 2)


def columns(tile):
    return pl.ds(pl.multiple_of(tile * TILE, TILE), TILE)


def forward_kernel(
    first_ref,
    qkv_in,
    out_in,
    up_in,
    down_in,
    small_ref,
    w_ref,
    out_ref,
    rows_ref,
    lse_ref,
    qkv_ref,
    kv_ref,
    mix_ref,
    flip_ref,
    slope_ref,
    unit_ref,
    scale_ref,
    cur,
    low,
    qkv,
    sib,
    mix,
    nrm,
    acc,
    act,
    slope,
    unit,
    scale,
    wbuf,
    flipped,
    shard,
    small_all,
    local_sems,
    own_sems,
    save_sems,
    send_sems,
    recv_sems,
    side_send,
    side_recv,
    turn_send,
    turn_recv,
    layers,
):
    batch, z, y, x, core = place_of()
    total = layers * UNITS
    yx = 2 * y + x
    column = 4 * y + 2 * x
    here = {"x": (batch ^ 2, z), "y": (batch ^ 4, z), "core": (batch ^ 1, z)}

    def remote(src, dst, send, recv, device):
        return pltpu.make_async_remote_copy(
            src_ref=src,
            dst_ref=dst,
            send_sem=send,
            recv_sem=recv,
            device_id=device,
            device_id_type=MESH,
        )

    flying = {}

    def launch(kind, unit_id, copies):
        flying[kind, unit_id] = copies
        for copy in copies:
            copy.start()

    def landed(kind, unit_id):
        for copy in flying[kind, unit_id]:
            copy.wait_recv()

    def hop(unit_id, slot, src, dst, device):
        return remote(src, dst, send_sems.at[unit_id, slot], recv_sems.at[unit_id, slot], device)

    own_rows = pl.ds(pl.multiple_of(z * 32, 32), 32)

    def straight(unit_id):
        return 1024 if unit_id < DIRECT else 1024 - 128

    def along(unit_id):
        cols = pl.ds(0, straight(unit_id))
        dst = w_ref.at[unit_id, yx, core, own_rows, cols]
        src = shard.at[unit_id, :, cols]
        copies = []
        if unit_id >= DIRECT:
            edge = pl.ds(1024 - 128, 128)
            piece, spot = shard.at[unit_id, :, edge], w_ref.at[unit_id, yx, core, own_rows, edge]
            copies += [hop(unit_id, 8, piece, spot, here["x"]), hop(unit_id, 9, piece, spot, here["y"])]
        for step in (1, 2, 3):
            copies.append(hop(unit_id, step - 1, src, dst, (batch, lax.rem(z + step, 4))))
        return copies

    def across(unit_id):
        line = w_ref.at[unit_id, yx, core, :, pl.ds(0, straight(unit_id))]
        copies = []
        if unit_id >= DIRECT:
            edge = pl.ds(1024 - 128, 128)
            if unit_id % 2:
                piece, to = w_ref.at[unit_id, 2 * y + 1 - x, core, own_rows, edge], here["y"]
            else:
                piece, to = w_ref.at[unit_id, 2 - 2 * y + x, core, own_rows, edge], here["x"]
            copies.append(hop(unit_id, 10, piece, piece, to))
        copies += [hop(unit_id, 3, line, line, here["x"]), hop(unit_id, 4, line, line, here["y"])]
        return copies

    def corner(unit_id):
        full = straight(unit_id)
        half = 384 if full < 1024 and unit_id % 2 else 512
        left = w_ref.at[unit_id, 2 * y + 1 - x, core, :, pl.ds(0, half)]
        right = w_ref.at[unit_id, 2 - 2 * y + x, core, :, pl.ds(half, full - half)]
        copies = []
        if unit_id >= DIRECT:
            block = w_ref.at[unit_id, :, core, own_rows, pl.ds(1024 - 128, 128)]
            for step in (1, 2, 3):
                to = (batch, lax.rem(z + step, 4))
                copies.append(hop(unit_id, 10 + step, block, block, to))
        copies += [hop(unit_id, 5, left, left, here["y"]), hop(unit_id, 6, right, right, here["x"])]
        return copies

    def inner(unit_id):
        block = w_ref.at[unit_id, :, core]
        return [hop(unit_id, 7, block, block, here["core"])]

    def side(slot, src, dst, device):
        return remote(src, dst, side_send.at[slot], side_recv.at[slot], device)

    def layout(layer):
        base = layer * UNITS
        for part in range(3):
            shard[base + part] = qkv_in[layer, :, part * 1024 : part * 1024 + 1024]
        shard[base + 3] = out_in[layer]
        lane = lax.broadcasted_iota(jnp.int32, (32, 128), 1) // 32
        for j in range(4):
            shard[base + 5 + 2 * j] = down_in[layer, j * 32 : j * 32 + 32]
            for block in range(8):
                made = None
                for part in range(4):
                    start = (4 * block + part) * 128
                    value = up_in[layer, :, start : start + 128].astype(F32)
                    if part != j:
                        value = pltpu.roll(value, ((part - j) * 32) % 128, 1)
                    made = value if made is None else jnp.where(lane == part, value, made)
                shard[base + 4 + 2 * j, :, block * 128 : block * 128 + 128] = made.astype(BF)

    owns = [
        pltpu.make_async_copy(
            shard.at[unit_id], w_ref.at[unit_id, yx, core, own_rows], own_sems.at[unit_id]
        )
        for unit_id in range(total)
    ]
    mine = small_all.at[y, x, core, z]
    mine[...] = small_ref[...]
    launch(
        "small",
        0,
        [side(step - 1, small_ref, mine, (batch, lax.rem(z + step, 4))) for step in (1, 2, 3)],
    )

    def turn(j, half):
        to = 2 * core + j
        block = lax.rem(to - z + 4, 4)
        src = first_ref.at[j, pl.ds(half * 128, 128)]
        dst = low.at[pl.ds(pl.multiple_of(block * 128, 128), 128)]
        send, recv = turn_send.at[2 * j + half], turn_recv.at[block]
        return (
            lambda: pltpu.make_async_copy(src, dst, local_sems.at[0]),
            lambda: remote(src, dst, send, recv, (column + half, to)),
            jnp.logical_and(to == z, core == half),
        )

    def turned(block):
        spot = low.at[pl.ds(block * 128, 128)]
        return remote(spot, spot, turn_send.at[0], turn_recv.at[block], here["core"])

    for layer in range(layers):
        layout(layer)
        if layer == 0:
            for unit_id in range(1):
                owns[unit_id].start()
                launch("along", unit_id, along(unit_id))
            for unit_id in range(1, LAGS[0]):
                owns[unit_id].start()
                launch("along", unit_id, along(unit_id))
    own_turn = core == z // 2

    def turn_out(j, half):
        local, away, stays = turn(j, half)
        pl.when(stays)(lambda: local().start())
        pl.when(jnp.logical_not(stays))(lambda: away().start())


    def small_hop(number):
        landed("small", number - 1)
        if number == 1:
            line = small_all.at[y, x, core]
            launch("small", 1, [side(3, line, line, here["x"])])
        elif number == 2:
            plane = small_all.at[y, :, core]
            launch("small", 2, [side(4, plane, plane, here["y"])])
        elif number == 3:
            cube = small_all.at[:, :, core]
            launch("small", 3, [side(5, cube, cube, here["core"])])

    def begin():
        small_hop(4)
        for block in range(8):
            four = small_all[block // 4, (block // 2) % 2, block % 2]
            rows_ref[:, block * 128 : block * 128 + 128] = (four[0] + four[1]) + (four[2] + four[3])
        local = turn(0, 0)[0]
        pl.when(own_turn)(lambda: local().wait())
        pl.when(jnp.logical_not(own_turn))(lambda: turned(0).wait_recv())
        for block in range(1, 4):
            turned(block).wait_recv()

        def body(step, carry):
            rows = pl.ds(pl.multiple_of(step * 64, 64), 64)
            cur[rows] = low[rows].astype(F32)
            return carry

        lax.fori_loop(0, 8, body, 0)

    saves = {}

    def save(name, src, dst, slot):
        if name in saves:
            saves[name].wait()
        saves[name] = pltpu.make_async_copy(src, dst, save_sems.at[slot])
        saves[name].start()

    def settle(*names):
        for name in names:
            if name in saves:
                saves.pop(name).wait()

    def norm(layer, which, gain_row, shift_row):
        gain = rows_ref[pl.ds(gain_row, 1)]
        shift_by = rows_ref[pl.ds(shift_row, 1)]

        def body(step, carry):
            rows = pl.ds(step * 64, 64)
            value = acc[rows]
            center = value - jnp.mean(value, -1, keepdims=True)
            spread = jnp.mean(center * center, -1, keepdims=True)
            root = lax.rsqrt(spread + NORM_EPS)
            normal = center * root
            unit[which, rows] = normal
            scale[which, rows] = jnp.broadcast_to(root, (64, 128))
            result = normal * gain + shift_by
            if which == 0:
                acc[rows] = result + rows_ref[pl.ds(layer * 12 + 3, 1)]
                nrm[rows] = result.astype(BF)
            else:
                cur[rows] = result
                low[rows] = result.astype(BF)
            return carry

        lax.fori_loop(0, 8, body, 0)
        save(("unit", which), unit.at[which], unit_ref.at[layer, which], 8 + which)
        save(("scale", which), scale.at[which], scale_ref.at[layer, which], 10 + which)

    def heads(layer, begin, end):
        def body(j, carry):
            lanes = pl.ds(pl.multiple_of(j * 128, 128), 128)
            k_lanes = pl.ds(pl.multiple_of(1024 + j * 128, 128), 128)
            v_lanes = pl.ds(pl.multiple_of(2048 + j * 128, 128), 128)
            q = qkv[:, lanes]
            lane = lax.broadcasted_iota(jnp.int32, q.shape, 1)
            outs = []
            for head in range(2):
                qh = jnp.where((lane // 64) == head, q, jnp.zeros_like(q))
                s_own = dot(qkv[:, k_lanes], qh, NT)
                s_sib = dot(sib[layer, 0, :, lanes], qh, NT)
                top = jnp.maximum(
                    jnp.max(s_own, 0, keepdims=True), jnp.max(s_sib, 0, keepdims=True)
                )
                p_own = jnp.exp(s_own - top)
                p_sib = jnp.exp(s_sib - top)
                mass = jnp.sum(p_own, 0, keepdims=True) + jnp.sum(p_sib, 0, keepdims=True)
                lse_ref[layer, j, pl.ds(head, 1)] = top + jnp.log(mass)
                o = dot(qkv[:, v_lanes], p_own.astype(BF), TN) + dot(
                    sib[layer, 1, :, lanes], p_sib.astype(BF), TN
                )
                outs.append(o[head * 64 : head * 64 + 64] / mass)
            mix[:, lanes] = jnp.transpose(jnp.concatenate(outs, 0)).astype(BF)
            return carry

        lax.fori_loop(begin, end, body, 0)

    fetched = {}

    def fetch(unit_id):
        if unit_id < total and unit_id not in fetched:
            fetched[unit_id] = pltpu.make_async_copy(
                w_ref.at[unit_id], wbuf.at[unit_id % 2], local_sems.at[2 + unit_id % 2]
            )
            fetched[unit_id].start()

    def weight(unit_id, tile):
        return wbuf[unit_id % 2, :, :, :, columns(tile)].reshape(1024, TILE)

    def project(unit_id):
        layer, kind = unit_id // UNITS, unit_id % UNITS
        base = layer * 12
        if kind == 0:
            settle("qkv")
        for copy in flying.pop(("kv", (layer - 1, kind)), ()):
            copy.wait_send()

        def body(tile, carry):
            value = jnp.dot(low[...], weight(unit_id, tile), preferred_element_type=F32)
            cols = columns(tile)
            if kind != 1:
                value = value + rows_ref[pl.ds(base + kind // 2, 1), cols]
            value = value.astype(BF)
            if kind == 0:
                value = (value.astype(F32) * SCORE_SCALE).astype(BF)
            qkv[:, columns(tile + 4 * kind)] = value
            return carry

        lax.fori_loop(0, 4, body, 0)
        if kind:
            spot = 6 + 2 * layer + kind - 1
            src, dst = qkv.at[:, pl.ds(1024 * kind, 1024)], sib.at[layer, kind - 1]
            launch("kv", (layer, kind), [side(spot, src, dst, here["core"])])
        if kind == 2:
            save("qkv", qkv, qkv_ref.at[layer], 1)

    def attention(layer, group):
        if group == 0:
            landed("kv", (layer, 1))
            landed("kv", (layer, 2))
            save("kv", sib.at[layer], kv_ref.at[layer], 2)
            settle("mix")
        heads(layer, 2 * group, 2 * group + 2)
        if group == 3:
            save("mix", mix, mix_ref.at[layer], 3)

    def mixing(unit_id):
        layer = unit_id // UNITS
        base = layer * 12
        settle(("unit", 0), ("scale", 0))

        def body(tile, carry):
            cols = columns(tile)
            value = jnp.dot(mix[...], weight(unit_id, tile), preferred_element_type=F32)
            acc[:, cols] = cur[:, cols] + value + rows_ref[pl.ds(base + 2, 1), cols]
            return carry

        lax.fori_loop(0, 4, body, 0)
        norm(layer, 0, base + 6, base + 4)

    def widen(unit_id):
        layer, j = unit_id // UNITS, unit_id % UNITS // 2 - 2
        base = layer * 12
        settle(("slope", j))

        def body(tile, carry):
            cols = columns(tile)
            value = jnp.dot(nrm[...], weight(unit_id, tile), preferred_element_type=F32)
            value = value + rows_ref[pl.ds(base + 8 + j, 1), cols]
            gate = 0.5 * (1.0 + lax.erf(value * 0.7071067811865476))
            act[j, :, cols] = (value * gate).astype(BF)
            bell = jnp.exp(-0.5 * value * value)
            slope[j, :, cols] = (gate + value * (0.3989422804014327 * bell)).astype(BF)
            return carry

        lax.fori_loop(0, 4, body, 0)
        save(("slope", j), slope.at[j], slope_ref.at[layer, j], 16 + j)

    def narrow(unit_id):
        layer, j = unit_id // UNITS, unit_id % UNITS // 2 - 2
        base = layer * 12

        def body(tile, carry):
            cols = columns(tile)
            acc[:, cols] += jnp.dot(act[j], weight(unit_id, tile), preferred_element_type=F32)
            return carry

        lax.fori_loop(0, 4, body, 0)
        if j == 3:
            settle(("unit", 1), ("scale", 1))
            norm(layer, 1, base + 7, base + 5)
            if layer == layers - 1:
                save("low", low, out_ref, 0)

    turns = [0]

    def flip(source, layer, index):
        slot = turns[0] % 2
        turns[0] += 1
        settle(("flip", slot))

        def body(block, carry):
            for half in range(2):
                lanes = pl.ds(pl.multiple_of(block * 256 + half * 128, 128), 128)
                flipped[slot, half, block] = jnp.transpose(source[:, lanes])
            return carry

        lax.fori_loop(0, 4, body, 0)
        save(("flip", slot), flipped.at[slot], flip_ref.at[layer, index], 4 + slot)

    chunks = []

    def plan_flip(unit_id, source, index):
        part = functools.partial(flip, source, unit_id // UNITS, index)
        chunks.append((unit_id, part, 1.3))

    for unit_id in range(total):
        layer, kind = unit_id // UNITS, unit_id % UNITS
        if kind < 3:
            chunks.append((unit_id, project, 2.0))
            if kind == 0:
                plan_flip(unit_id, low, 0)
        elif kind == 3:
            for group in range(4):
                chunks.append((unit_id - 1, functools.partial(attention, layer, group), 4.5))
            plan_flip(unit_id - 1, mix, 2)
            chunks.append((unit_id, mixing, 4.5))
            plan_flip(unit_id, nrm, 1)
        elif kind % 2 == 0:
            chunks.append((unit_id, widen, 3.5))
            plan_flip(unit_id, act.at[kind // 2 - 2], 3 + kind // 2 - 2)
        else:
            chunks.append((unit_id, narrow, 5.0 if kind == 11 else 1.5))

    def advance(have, budget):
        spent = 0.0
        while chunks and chunks[0][0] <= have and (spent == 0.0 or spent + chunks[0][2] <= budget):
            unit_id, chunk, cost = chunks.pop(0)
            if isinstance(chunk, functools.partial):
                chunk()
            else:
                fetch(unit_id)
                fetched[unit_id].wait()
                chunk(unit_id)
                if unit_id + 2 <= have:
                    fetch(unit_id + 2)
            spent += cost

    ahead, corner_lag, inner_lag, use_lag = LAGS
    step, have = 0, -1
    while step < total + use_lag or chunks:
        if step + ahead < total:
            owns[step + ahead].start()
            launch("along", step + ahead, along(step + ahead))
        if step < total:
            owns[step].wait()
            landed("along", step)
            launch("across", step, across(step))
        if 0 < step < 4:
            small_hop(step)
        if step in TURN_STEPS:
            number = TURN_STEPS.index(step)
            turn_out(number // 2, number % 2)
        if step > BEGIN:
            advance(have, BUDGET)
        if 0 <= step - corner_lag < total:
            landed("across", step - corner_lag)
            launch("corner", step - corner_lag, corner(step - corner_lag))
        if 0 <= step - inner_lag < total:
            landed("corner", step - inner_lag)
            launch("inner", step - inner_lag, inner(step - inner_lag))
        if step == BEGIN:
            begin()
        if 0 <= step - use_lag < total:
            landed("inner", step - use_lag)
            have = step - use_lag
            if have < 2 or have - 2 in fetched and all(item[0] > have - 2 for item in chunks):
                fetch(have)
        if step >= BEGIN:
            advance(have, BUDGET)
        step += 1
    for j in range(2):
        for half in range(2):
            local, away, stays = turn(j, half)
            pl.when(jnp.logical_not(stays))(lambda: away().wait_send())
    for copies in flying.values():
        for copy in copies:
            copy.wait_send()
    settle(*list(saves))


def forward_pass(first, w_qkv, w_out, w_up, w_down, small):
    layers = w_qkv.shape[0]
    width = first.shape[2]
    rows = first.shape[0] * first.shape[1]
    any_spec = pl.BlockSpec(memory_space=pl.ANY)
    vmem = pl.BlockSpec(memory_space=pltpu.VMEM)
    shape = jax.ShapeDtypeStruct
    total = layers * UNITS
    return pl.pallas_call(
        functools.partial(forward_kernel, layers=layers),
        in_specs=[vmem] * 6,
        out_specs=[any_spec, any_spec, vmem, vmem] + [any_spec] * 7,
        out_shape=[
            shape((total, 4, 2, 128, width), BF),
            shape((rows, width), BF),
            shape((layers * 12, width), F32),
            shape((layers, 8, 2, rows), F32),
            shape((layers, rows, 3 * width), BF),
            shape((layers, 2, rows, width), BF),
            shape((layers, rows, width), BF),
            shape((layers, 7, 2, 4, 128, rows), BF),
            shape((layers, 4, rows, width), BF),
            shape((layers, 2, rows, width), F32),
            shape((layers, 2, rows, 128), F32),
        ],
        scratch_shapes=[
            pltpu.VMEM((rows, width), F32),
            pltpu.VMEM((rows, width), BF),
            pltpu.VMEM((rows, 3 * width), BF),
            pltpu.VMEM((layers, 2, rows, width), BF),
            pltpu.VMEM((rows, width), BF),
            pltpu.VMEM((rows, width), BF),
            pltpu.VMEM((rows, width), F32),
            pltpu.VMEM((4, rows, width), BF),
            pltpu.VMEM((4, rows, width), BF),
            pltpu.VMEM((2, rows, width), F32),
            pltpu.VMEM((2, rows, 128), F32),
            pltpu.VMEM((2, 4, 2, 128, width), BF),
            pltpu.VMEM((2, 2, 4, 128, rows), BF),
            pltpu.VMEM((total, 32, width), BF),
            pltpu.VMEM((2, 2, 2, 4, layers * 12, 128), F32),
            pltpu.SemaphoreType.DMA((4,)),
            pltpu.SemaphoreType.DMA((total,)),
            pltpu.SemaphoreType.DMA((20,)),
            pltpu.SemaphoreType.DMA((total, 14)),
            pltpu.SemaphoreType.DMA((total, 14)),
            pltpu.SemaphoreType.DMA((6 + 2 * layers,)),
            pltpu.SemaphoreType.DMA((6 + 2 * layers,)),
            pltpu.SemaphoreType.DMA((4,)),
            pltpu.SemaphoreType.DMA((4,)),
        ],
        compiler_params=pltpu.CompilerParams(
            has_side_effects=True, vmem_limit_bytes=60 << 20
        ),
        name="forward_pass",
    )(first, w_qkv, w_out, w_up, w_down, small)


def backward_kernel(
    top_ref,
    last_ref,
    w_ref,
    rows_ref,
    lse_ref,
    qkv_ref,
    kv_ref,
    mix_ref,
    flip_ref,
    slope_ref,
    unit_ref,
    scale_ref,
    last_out,
    grad_out,
    qkv_out,
    out_out,
    up_out,
    down_out,
    bias_out,
    up_bias_out,
    gain_out,
    grad,
    edge,
    unit,
    scale,
    arena,
    span,
    feat,
    turned,
    wbuf,
    send,
    mine,
    land,
    wide,
    slim,
    ends,
    small_all,
    small_in,
    staged,
    up_all,
    load_sems,
    store_sems,
    send_sems,
    recv_sems,
    side_send,
    side_recv,
    turn_send,
    turn_recv,
    layers,
):
    batch, z, y, x, core = place_of()
    total = layers * UNITS
    here = {"x": (batch ^ 2, z), "y": (batch ^ 4, z), "core": (batch ^ 1, z)}
    slots = 6

    def remote(src, dst, send_sem, recv_sem, device):
        return pltpu.make_async_remote_copy(
            src_ref=src,
            dst_ref=dst,
            send_sem=send_sem,
            recv_sem=recv_sem,
            device_id=device,
            device_id_type=MESH,
        )

    incoming, outgoing = {}, {}

    def launch(kind, number, copies):
        incoming[kind, number] = copies
        outgoing[kind, number] = copies
        for copy in copies:
            copy.start()

    def landed(kind, number):
        for copy in incoming.pop((kind, number)):
            copy.wait_recv()

    def sent(kind, number):
        for copy in outgoing.pop((kind, number), ()):
            copy.wait_send()

    def hop(number, slot, src, dst, device):
        return remote(src, dst, send_sems.at[number, slot], recv_sems.at[number, slot], device)

    def side(slot, src, dst, device):
        return remote(src, dst, side_send.at[slot], side_recv.at[slot], device)

    loads = {}

    def fetch(name, src, dst, slot):
        loads[name] = pltpu.make_async_copy(src, dst, load_sems.at[slot])
        loads[name].start()

    def ready(name):
        loads.pop(name).wait()

    order = []
    for layer in reversed(range(layers)):
        for j in range(4):
            order += [layer * UNITS + 5 + 2 * j, layer * UNITS + 4 + 2 * j]
        order += [layer * UNITS + 3, layer * UNITS, layer * UNITS + 1, layer * UNITS + 2]

    def fetch_weight(number):
        if number < total:
            fetch(("w", number), w_ref.at[order[number]], wbuf.at[number % 2], number % 2)

    def rows_of(number, tile):
        return wbuf[number % 2, tile].reshape(TILE, 1024)

    def fetch_turned(slot, layer, index):
        for half, which in enumerate((core, 1 - core)):
            fetch(
                (slot, half),
                flip_ref.at[layer, index, which],
                turned.at[slot, half],
                10 + 2 * slot + half,
            )

    def ready_turned(slot):
        ready((slot, 0))
        ready((slot, 1))

    def produce(number, slot, upper):
        buffer = number % 2
        sent("core", number - 2)

        def body(tile, carry):
            cols = columns(tile)
            value = jnp.dot(
                turned[slot, 1].reshape(512, 512), upper[:, cols], preferred_element_type=F32
            )
            send[buffer, :, :, cols] = value.astype(BF).reshape(4, 128, TILE)
            return carry

        lax.fori_loop(0, 4, body, 0)
        launch("core", number, [hop(number, 0, send.at[buffer], land.at[number % PLACES], here["core"])])

        def own(tile, carry):
            cols = columns(tile)
            value = jnp.dot(
                turned[slot, 0].reshape(512, 512), upper[:, cols], preferred_element_type=F32
            )
            mine[number % slots, :, :, cols] = value.astype(BF).reshape(4, 128, TILE)
            return carry

        lax.fori_loop(0, 4, own, 0)

    left, right = pl.ds(0, 512), pl.ds(512, 512)

    def chunk_rows(chunk):
        return pl.ds(pl.multiple_of(chunk * 32, 32), 32)

    def stage_core(number):
        part = land.at[number % PLACES]
        landed("core", number)

        def body(block, carry):
            part[block] = part[block] + mine[number % slots, block]
            return carry

        lax.fori_loop(0, 4, body, 0)
        spot = number % slots
        launch(
            "wide",
            number,
            [
                hop(number, 1, part.at[pl.ds(2 - 2 * y, 2), :, left], wide.at[spot, 0], here["y"]),
                hop(number, 2, part.at[pl.ds(1 - x, 1), :, right], wide.at[spot, 1, pl.ds(0, 1)], here["x"]),
                hop(number, 3, part.at[pl.ds(3 - x, 1), :, right], wide.at[spot, 1, pl.ds(1, 1)], here["x"]),
            ],
        )

    def stage_wide(number):
        part, spot = land.at[number % PLACES], number % slots
        landed("wide", number)
        for block in range(2):
            spot_y = 2 * y + block
            part[spot_y, :, left] = part[spot_y, :, left] + wide[spot, 0, block]
            spot_x = 2 * block + x
            part[spot_x, :, right] = part[spot_x, :, right] + wide[spot, 1, block]
        launch(
            "slim",
            number,
            [
                hop(number, 4, part.at[2 * y + 1 - x, :, left], slim.at[spot, 0], here["x"]),
                hop(number, 5, part.at[2 - 2 * y + x, :, right], slim.at[spot, 1], here["y"]),
            ],
        )

    def stage_slim(number):
        part, spot = land.at[number % PLACES, 2 * y + x], number % slots
        landed("slim", number)
        part[:, left] = part[:, left] + slim[spot, 0]
        part[:, right] = part[:, right] + slim[spot, 1]
        copies = []
        for step, chunk in enumerate((z ^ 1, z ^ 3)):
            copies.append(hop(number, 6 + step, part.at[chunk_rows(chunk)], ends.at[spot, step], (batch, z ^ 1)))
        launch("pair", number, copies)

    def stage_pair(number):
        part, spot = land.at[number % PLACES, 2 * y + x], number % slots
        landed("pair", number)
        for step, chunk in enumerate((z, z ^ 2)):
            rows = chunk_rows(chunk)
            part[rows] = part[rows] + ends[spot, step]
        src = part.at[chunk_rows(z ^ 2)]
        launch("ends", number, [hop(number, 8, src, ends.at[spot, 2], (batch, z ^ 2))])

    def stage_ends(number):
        part, spot = land.at[number % PLACES, 2 * y + x], number % slots
        landed("ends", number)
        value = part[chunk_rows(z)].astype(F32) + ends[spot, 2].astype(F32)
        layer, kind = order[number] // UNITS, order[number] % UNITS
        j = kind // 2 - 2
        if kind > 3 and kind % 2 == 0:
            lane = lax.broadcasted_iota(jnp.int32, (32, 128), 1) // 32
            if j == 0 and 4 in stores:
                stores.pop(4).wait()
            for block in range(32):
                spot = pl.ds(block * 128, 128)
                piece = value[:, block // 4 * 128 : block // 4 * 128 + 128]
                if j != block % 4:
                    piece = pltpu.roll(piece, ((j - block % 4) * 32) % 128, 1)
                up_all[:, spot] = piece if j == 0 else jnp.where(lane == j, piece, up_all[:, spot])
            if j == 3:
                stores[4] = pltpu.make_async_copy(up_all, up_out.at[layer], store_sems.at[4])
                stores[4].start()
        else:
            slot = number % 4
            if slot in stores:
                stores.pop(slot).wait()
            staged[slot] = value
            if kind < 3:
                dst = qkv_out.at[layer, :, pl.ds(1024 * kind, 1024)]
            else:
                dst = out_out.at[layer] if kind == 3 else down_out.at[layer, j]
            stores[slot] = pltpu.make_async_copy(staged.at[slot], dst, store_sems.at[slot])
            stores[slot].start()
        for kind in ("wide", "slim", "pair", "ends"):
            sent(kind, number)

    ticks = [0]
    stores = {}
    wide_lag, slim_lag, pair_lag, ends_lag = BACK_LAGS

    def first_half():
        step = ticks[0]
        if step < total:
            stage_core(step)
        if 0 <= step - wide_lag < total:
            stage_wide(step - wide_lag)

    def second_half():
        step = ticks[0]
        ticks[0] += 1
        if 0 <= step - slim_lag < total:
            stage_slim(step - slim_lag)
        if 0 <= step - pair_lag < total:
            stage_pair(step - pair_lag)
        if 0 <= step - ends_lag < total:
            stage_ends(step - ends_lag)

    def tick():
        first_half()
        second_half()

    def norm(base, gain_row, shift_row, sum_row):
        gain = rows_ref[pl.ds(base + gain_row, 1)]

        def body(step, carry):
            gains, shifts, sums = carry
            rows = pl.ds(step * 64, 64)
            value = grad[rows]
            normal = unit[rows]
            scaled = value * gain
            inner = jnp.mean(scaled * normal, -1, keepdims=True)
            centre = jnp.mean(scaled, -1, keepdims=True)
            result = scale[rows][:, :1] * (scaled - centre - normal * inner)
            grad[rows] = result
            rounded = result.astype(BF)
            edge[rows] = rounded
            return (
                gains + jnp.sum(value * normal, 0, keepdims=True),
                shifts + jnp.sum(value, 0, keepdims=True),
                sums + jnp.sum(rounded.astype(F32), 0, keepdims=True),
            )

        zero = jnp.zeros((1, 1024), F32)
        gains, shifts, sums = lax.fori_loop(0, 8, body, (zero, zero, zero))
        put_row(base + gain_row, gains)
        put_row(base + shift_row, shifts)
        put_row(base + sum_row, sums)

    def put_row(row, value):
        for block in range(8):
            small_all[block // 2, block % 2, row : row + 1] = value[:, block * 128 : block * 128 + 128]

    def heads(layer, begin, end):
        def body(j, carry):
            lanes = pl.ds(pl.multiple_of(j * 128, 128), 128)
            q = arena[0, :, lanes]
            do = span[:, lanes]
            lane = lax.broadcasted_iota(jnp.int32, q.shape, 1)
            prod = jnp.transpose(do.astype(F32) * feat[:, lanes].astype(F32))
            dq = []
            sums = [[None, None], [None, None]]
            for head in range(2):
                pick = (lane // 64) == head
                qh = jnp.where(pick, q, jnp.zeros_like(q))
                dh = jnp.where(pick, do, jnp.zeros_like(do))
                delta = jnp.sum(prod[head * 64 : head * 64 + 64], 0, keepdims=True)
                lse = lse_ref[layer, j, pl.ds(head, 1)]
                dqh = None
                for half in range(2):
                    k = arena[1 + 2 * half, :, lanes]
                    v = arena[2 + 2 * half, :, lanes]
                    p = jnp.exp(dot(k, qh, NT) - lse)
                    ds = (p * (dot(v, dh, NT) - delta)).astype(BF)
                    dv = jnp.dot(p.astype(BF), dh, preferred_element_type=F32)
                    dk = jnp.dot(ds, qh, preferred_element_type=F32)
                    part = dot(ds, k, TN)
                    dqh = part if dqh is None else dqh + part
                    sums[half][0] = dk if head == 0 else sums[half][0] + dk
                    sums[half][1] = dv if head == 0 else sums[half][1] + dv
                dq.append(dqh)
            arena[5, :, lanes] = (jnp.where(lane < 64, dq[0], dq[1]) * SCORE_SCALE).astype(BF)
            arena[6, :, lanes] = sums[0][0].astype(BF)
            arena[7, :, lanes] = sums[0][1].astype(BF)
            arena[8, :, lanes] = sums[1][0].astype(BF)
            arena[9, :, lanes] = sums[1][1].astype(BF)
            return carry

        lax.fori_loop(begin, end, body, 0)

    def row_sum(row, slot):
        def body(step, carry):
            rows = pl.ds(pl.multiple_of(step * 64, 64), 64)
            return carry + jnp.sum(arena[slot, rows].astype(F32), 0, keepdims=True)

        put_row(row, lax.fori_loop(0, 8, body, jnp.zeros((1, 1024), F32)))

    def pull(number, upper):
        def body(tile, carry):
            cols = columns(tile)
            grad[:, cols] += dot(upper[...], rows_of(number, tile), NT)
            return carry

        ready(("w", number))
        lax.fori_loop(0, 4, body, 0)
        fetch_weight(number + 2)

    def load_attention(layer):
        for part in range(3):
            fetch(("qkv", part), qkv_ref.at[layer, :, pl.ds(1024 * part, 1024)], arena.at[part], 2 + part)
        for part in range(2):
            fetch(("kv", part), kv_ref.at[layer, part], arena.at[3 + part], 5 + part)

    column = 4 * y + 2 * x
    seat = 2 * lax.rem(z, 2) + core
    stays = core == z // 2

    def homeward(which, block, src, dst):
        rows = src.at[pl.ds(block * 128, 128)]
        spot = dst.at[lax.rem(z, 2), pl.ds(pl.multiple_of(core * 128, 128), 128)]
        to = (column + z // 2, lax.rem(z - block + 4, 4))
        return (
            lambda: pltpu.make_async_copy(rows, spot, load_sems.at[14 + which]),
            lambda: remote(rows, spot, turn_send.at[which, block], turn_recv.at[which, seat], to),
        )

    def turn_start(which, src, dst):
        for block in range(4):
            local, away = homeward(which, block, src, dst)
            if block:
                away().start()
            else:
                pl.when(stays)(lambda: local().start())
                pl.when(jnp.logical_not(stays))(lambda: away().start())

    def turn_end(which, src, dst):
        for block in range(4):
            local, away = homeward(which, block, src, dst)
            if block:
                away().wait_send()
            else:
                pl.when(stays)(lambda: local().wait())
                pl.when(jnp.logical_not(stays))(lambda: away().wait_send())
        for place in range(4):
            spot = dst.at[place // 2, pl.ds(place % 2 * 128, 128)]
            came = remote(spot, spot, turn_send.at[which, 0], turn_recv.at[which, place], here["core"])
            own = jnp.logical_and(2 * core + place // 2 == z, core == place % 2)
            pl.when(jnp.logical_not(own))(came.wait_recv)

    fetch("top", top_ref, grad, 7)
    turn_start(0, last_ref, last_out)
    first = True
    for layer in reversed(range(layers)):
        base = layer * 12
        start = (layers - 1 - layer) * UNITS
        if first:
            fetch("unit", unit_ref.at[layer, 1], unit, 8)
            fetch("scale", scale_ref.at[layer, 1], scale, 9)
            fetch_weight(0)
            fetch_weight(1)
            load_attention(layer)
            ready("top")
            fetch_turned(0, layer, 1)
            fetch_turned(1, layer, 3)
        fetch("slope", slope_ref.at[layer, 0], arena.at[9], 16)
        fetch("mix", mix_ref.at[layer], feat, 17)
        first = False
        ready("unit")
        ready("scale")
        norm(base, 7, 5, 3)
        fetch("unit", unit_ref.at[layer, 0], unit, 8)
        fetch("scale", scale_ref.at[layer, 0], scale, 9)
        ready_turned(0)
        for j in range(4):
            number = start + 2 * j
            ready_turned(1)
            produce(number, 1, edge)
            fetch_turned(1, layer, 4 + j if j < 3 else 2)
            ready(("w", number))
            ready("slope")

            def body(tile, carry):
                cols = columns(tile)
                value = dot(edge[...], rows_of(number, tile), NT)
                value = (arena[9, :, cols].astype(F32) * value).astype(BF)
                span[:, cols] = value
                total_row = jnp.sum(value.astype(F32), 0, keepdims=True)
                for block in range(2):
                    small_all[tile, block, pl.ds(base + 8 + j, 1)] = total_row[
                        :, block * 128 : block * 128 + 128
                    ]
                return carry

            lax.fori_loop(0, 4, body, 0)
            fetch_weight(number + 2)
            if j < 3:
                fetch("slope", slope_ref.at[layer, j + 1], arena.at[9], 16)
            first_half()
            produce(number + 1, 0, span)
            pull(number + 1, span)
            second_half()
        ready("unit")
        ready("scale")
        norm(base, 6, 4, 2)
        if layer:
            fetch("unit", unit_ref.at[layer - 1, 1], unit, 8)
            fetch("scale", scale_ref.at[layer - 1, 1], scale, 9)
        fetch_turned(0, layer, 0)
        ready("mix")
        ready_turned(1)
        number = start + 8
        ready(("w", number))

        def body(tile, carry):
            span[:, columns(tile)] = dot(edge[...], rows_of(number, tile), NT).astype(BF)
            return carry

        lax.fori_loop(0, 4, body, 0)
        fetch_weight(number + 2)
        tick()
        produce(number, 1, edge)
        if layer:
            fetch_turned(1, layer - 1, 3)
        for part in range(3):
            ready(("qkv", part))
        for part in range(2):
            ready(("kv", part))
        for group in range(4):
            heads(layer, 2 * group, 2 * group + 2)
            tick()
        place = layers - 1 - layer
        for part in range(2):
            launch(
                "keys",
                2 * place + part,
                [side(2 * place + part, arena.at[8 + part], arena.at[10 + part], here["core"])],
            )
        if layer:
            load_attention(layer - 1)
        ready_turned(0)
        for part in range(3):
            number = start + 9 + part
            if part:
                landed("keys", 2 * place + part - 1)

                def body(step, carry):
                    rows = pl.ds(pl.multiple_of(step * 64, 64), 64)
                    arena[5 + part, rows] = arena[5 + part, rows] + arena[9 + part, rows]
                    return carry

                lax.fori_loop(0, 8, body, 0)
            if part != 1:
                row_sum(base + part // 2, 5 + part)
            produce(number, 0, arena.at[5 + part])
            pull(number, arena.at[5 + part])
            if part < 2:
                tick()
            elif layer:
                fetch_turned(0, layer - 1, 1)
        sent("keys", 2 * place)
        sent("keys", 2 * place + 1)
        if layer == 0:

            def body(step, carry):
                rows = pl.ds(pl.multiple_of(step * 64, 64), 64)
                edge[rows] = grad[rows].astype(BF)
                return carry

            lax.fori_loop(0, 8, body, 0)
            turn_start(1, edge, grad_out)
        tick()
    base = 2 * layers

    def small_core():
        launch("small", 0, [side(base, small_all.at[:, 1 - core], small_in.at[pl.ds(0, 4)], here["core"])])

    def small_y():
        landed("small", 0)
        sent("small", 0)
        small_all[:, core] = small_all[:, core] + small_in[0:4]
        launch(
            "small",
            1,
            [side(base + 1, small_all.at[pl.ds(2 - 2 * y, 2), core], small_in.at[pl.ds(4, 2)], here["y"])],
        )

    def small_x():
        landed("small", 1)
        sent("small", 1)
        for block in range(2):
            small_all[2 * y + block, core] = small_all[2 * y + block, core] + small_in[4 + block]
        launch(
            "small",
            2,
            [side(base + 2, small_all.at[2 * y + 1 - x, core], small_in.at[6], here["x"])],
        )

    def small_z():
        landed("small", 2)
        sent("small", 2)
        own = small_all.at[2 * y + x, core]
        own[...] = own[...] + small_in[6]
        launch(
            "small",
            3,
            [
                side(base + 2 + step, own, small_in.at[6 + step], (batch, lax.rem(z + step, 4)))
                for step in (1, 2, 3)
            ],
        )

    def small_end():
        landed("small", 3)
        sent("small", 3)
        value = small_all[2 * y + x, core]
        for step in (1, 2, 3):
            value = value + small_in[6 + step]
        mine_row = value[:, 0:32]
        for place in range(1, 4):
            mine_row = jnp.where(z == place, value[:, place * 32 : place * 32 + 32], mine_row)
        for layer in range(layers):
            top = layer * 12
            bias_out[layer] = mine_row[top : top + 6]
            gain_out[layer] = mine_row[top + 6 : top + 8]
            for j in range(4):
                up_bias_out[layer : layer + 1, j * 32 : j * 32 + 32] = mine_row[top + 8 + j : top + 9 + j]

    queue = [small_core, small_y, small_x, small_z, small_end]
    while ticks[0] < total + ends_lag or queue:
        if queue:
            queue.pop(0)()
        if ticks[0] < total + ends_lag:
            tick()
    for kind, number in list(outgoing):
        sent(kind, number)
    for copy in stores.values():
        copy.wait()
    turn_end(0, last_ref, last_out)
    turn_end(1, edge, grad_out)


BACK_LAGS = (2, 4, 5, 6)
PLACES = 13


def backward_pass(top, last, saved):
    w, rows, lse, qkv, kv, mix, flip, slope, unit, scale = saved
    total = w.shape[0]
    layers = total // UNITS
    tokens, width = top.shape
    any_spec = pl.BlockSpec(memory_space=pl.ANY)
    vmem = pl.BlockSpec(memory_space=pltpu.VMEM)
    shape = jax.ShapeDtypeStruct
    return pl.pallas_call(
        functools.partial(backward_kernel, layers=layers),
        in_specs=[any_spec] * 3 + [vmem, vmem] + [any_spec] * 7,
        out_specs=[any_spec] * 6 + [vmem] * 3,
        out_shape=[
            shape((2, tokens // 2, width), BF),
            shape((2, tokens // 2, width), BF),
            shape((layers, 32, 3 * width), F32),
            shape((layers, 32, width), F32),
            shape((layers, 32, 4 * width), F32),
            shape((layers, 4, 32, width), F32),
            shape((layers, 6, 32), F32),
            shape((layers, 128), F32),
            shape((layers, 2, 32), F32),
        ],
        scratch_shapes=[
            pltpu.VMEM((tokens, width), F32),
            pltpu.VMEM((tokens, width), BF),
            pltpu.VMEM((tokens, width), F32),
            pltpu.VMEM((tokens, 128), F32),
            pltpu.VMEM((12, tokens, width), BF),
            pltpu.VMEM((tokens, width), BF),
            pltpu.VMEM((tokens, width), BF),
            pltpu.VMEM((2, 2, 4, 128, tokens), BF),
            pltpu.VMEM((2, 4, 2, 128, width), BF),
            pltpu.VMEM((2, 4, 128, width), BF),
            pltpu.VMEM((6, 4, 128, width), BF),
            pltpu.VMEM((PLACES, 4, 128, width), BF),
            pltpu.VMEM((6, 2, 2, 128, width // 2), BF),
            pltpu.VMEM((6, 2, 128, width // 2), BF),
            pltpu.VMEM((6, 3, 32, width), BF),
            pltpu.VMEM((4, 2, layers * 12, 128), F32),
            pltpu.VMEM((10, layers * 12, 128), F32),
            pltpu.VMEM((4, 32, width), F32),
            pltpu.VMEM((32, 4 * width), F32),
            pltpu.SemaphoreType.DMA((18,)),
            pltpu.SemaphoreType.DMA((5,)),
            pltpu.SemaphoreType.DMA((total, 9)),
            pltpu.SemaphoreType.DMA((total, 9)),
            pltpu.SemaphoreType.DMA((2 * layers + 6,)),
            pltpu.SemaphoreType.DMA((2 * layers + 6,)),
            pltpu.SemaphoreType.DMA((2, 4)),
            pltpu.SemaphoreType.DMA((2, 4)),
        ],
        compiler_params=pltpu.CompilerParams(has_side_effects=True, vmem_limit_bytes=60 << 20),
        name="backward_pass",
    )(top, last, w, rows, lse, qkv, kv, mix, flip, slope, unit, scale)


def swap(value, bit):
    return lax.ppermute(value, "batch", [(place, place ^ bit) for place in range(8)])


def take(value, index, axis):
    return lax.dynamic_index_in_dim(value, index, axis, keepdims=False)


def small_rows(biases, up_bias, gains):
    layers = biases.shape[0]
    rows = jnp.concatenate((biases, gains, up_bias.reshape(layers, 4, 32)), 1).astype(F32)
    wide = jnp.tile(rows.reshape(layers * 12, 32), (1, 4))
    lane = lax.broadcasted_iota(jnp.int32, wide.shape, 1)
    return jnp.where(lane // 32 == lax.axis_index("blk"), wide, 0.0)


def column_shards(
    hidden_in,
    mask_index,
    mask_count,
    replacement,
    out_grad,
    w_qkv,
    w_out,
    w_up,
    w_down,
    biases,
    up_bias,
    gains,
):
    batch = lax.axis_index("batch")
    z = lax.axis_index("blk")
    core = lax.rem(batch, 2)
    seq_count, block_len, width = hidden_in.shape
    layers = w_qkv.shape[0]
    slots = mask_index.shape[1]
    per = width // 32

    slot_ids = jnp.arange(slots, dtype=jnp.int32)
    used = slot_ids[None, :] < mask_count[:, None]
    slot_place = jnp.where(used, mask_index, -1)
    places = z * block_len + jnp.arange(block_len, dtype=jnp.int32)
    hits = slot_place[:, None, :] == places[None, :, None]
    placed = jnp.einsum("sbm,smd->sbd", hits.astype(BF), replacement, preferred_element_type=F32)
    first = jnp.where(jnp.any(hits, -1, keepdims=True), placed.astype(BF), hidden_in)

    mine = lax.rem(z, 2)
    came_grad = swap(take(out_grad, mine, 0), 1)
    came_place = swap(take(slot_place, mine, 0).astype(F32), 1)
    here = (z // 2) == core
    top_grad = jnp.where(here, take(out_grad, mine, 0), came_grad)
    top_place = jnp.where(here, take(slot_place, mine, 0), came_place.astype(jnp.int32))
    blocks = lax.rem(z - jnp.arange(4, dtype=jnp.int32) + 4, 4)
    token_place = (
        blocks[:, None] * block_len
        + core * (block_len // 2)
        + jnp.arange(block_len // 2, dtype=jnp.int32)[None, :]
    ).reshape(-1)
    top_hits = (token_place[:, None] == top_place[None, :]).astype(BF)
    upstream = jnp.dot(top_hits, top_grad, preferred_element_type=F32)

    results = forward_pass(first, w_qkv, w_out, w_up, w_down, small_rows(biases, up_bias, gains))
    last, grad, qkv, out, up, down, bias_rows, up_rows, gain_rows = backward_pass(
        upstream, results[1], (results[0],) + tuple(results[2:])
    )
    return (
        last,
        grad.astype(F32),
        qkv,
        out,
        up,
        down.reshape(layers, 4 * per, width),
        bias_rows,
        up_rows,
        gain_rows,
    )


def solution(mesh):
    fits = mesh.shape["batch"] == 8 and mesh.shape["blk"] == 4
    return jax.shard_map(
        column_shards if fits else general_shards,
        mesh=mesh,
        in_specs=(
            P(*BOTH, None),
            P("batch", None),
            P("batch"),
            P("batch", None, None),
            P("batch", None, None),
            P(None, BOTH, None),
            P(None, BOTH, None),
            P(None, BOTH, None),
            P(None, BOTH, None),
            P(None, None, BOTH),
            P(None, BOTH),
            P(None, None, BOTH),
        ),
        out_specs=(
            P(*BOTH, None),
            P(*BOTH, None),
            P(None, BOTH, None),
            P(None, BOTH, None),
            P(None, BOTH, None),
            P(None, BOTH, None),
            P(None, None, BOTH),
            P(None, BOTH),
            P(None, None, BOTH),
        ),
        check_vma=False,
    )
```

```python
import functools

import jax
import jax.numpy as jnp
from jax import lax
from jax.experimental import pallas as pl
from jax.experimental.pallas import tpu as pltpu
from jax.sharding import PartitionSpec as P

HEADS = 16


BOTH = ("batch", "blk")
NORM_EPS = 1e-12
SCORE_SCALE = 0.125


def norm_rows(values, gain, shift):
    center = values - jnp.mean(values, -1, keepdims=True)
    spread = jnp.mean(center * center, -1, keepdims=True)
    return center * lax.rsqrt(spread + NORM_EPS) * gain + shift


def gelu_exact(values):
    return 0.5 * values * (1.0 + jax.scipy.special.erf(values * 0.7071067811865476))


def forward_layer(inputs, fetched, head_shape):
    qkv_weight, out_weight, up_weight, down_weight, bias_rows, up_shift, gain_rows = fetched
    bias_rows = bias_rows.astype(jnp.float32)
    up_shift = up_shift.astype(jnp.float32)
    gain_rows = gain_rows.astype(jnp.float32)
    seq_count, block_len, head_count, head_dim = head_shape
    model_width = head_count * head_dim
    inputs_low = inputs.astype(jnp.bfloat16)
    project = jnp.einsum("sbd,de->sbe", inputs_low, qkv_weight, preferred_element_type=jnp.float32)
    query = (project[..., :model_width] + bias_rows[0]).astype(jnp.bfloat16).reshape(head_shape)
    keys = project[..., model_width : 2 * model_width].astype(jnp.bfloat16).reshape(head_shape)
    values = (
        (project[..., 2 * model_width :] + bias_rows[1]).astype(jnp.bfloat16).reshape(head_shape)
    )
    stat_shape = (seq_count, head_count, block_len)
    top_now = jnp.full(stat_shape, -1e30, jnp.float32)
    key_part = lax.all_gather(keys, "blk", axis=1, tiled=True)
    value_part = lax.all_gather(values, "blk", axis=1, tiled=True)
    scores = (
        jnp.einsum("sqhd,skhd->shqk", query, key_part, preferred_element_type=jnp.float32)
        * SCORE_SCALE
    )
    top_next = jnp.maximum(top_now, jnp.max(scores, -1))
    weights_now = jnp.exp(scores - top_next[..., None])
    total_next = jnp.sum(weights_now, -1)
    acc_next = jnp.einsum(
        "shqk,skhd->shqd",
        weights_now.astype(jnp.bfloat16),
        value_part,
        preferred_element_type=jnp.float32,
    )
    log_total = top_next + jnp.log(total_next)
    attended = (acc_next / total_next[..., None]).transpose(0, 2, 1, 3).reshape(inputs.shape)
    attended_low = attended.astype(jnp.bfloat16)
    mixed = (
        inputs
        + jnp.einsum("sbe,ed->sbd", attended_low, out_weight, preferred_element_type=jnp.float32)
        + bias_rows[2]
    )
    normed, first_pull = jax.vjp(norm_rows, mixed, gain_rows[0], bias_rows[4])
    normed_low = normed.astype(jnp.bfloat16)
    hidden = (
        jnp.einsum("sbd,df->sbf", normed_low, up_weight, preferred_element_type=jnp.float32)
        + up_shift
    )
    active, gelu_pull = jax.vjp(gelu_exact, hidden)
    active_low = active.astype(jnp.bfloat16)
    second = (
        normed
        + jnp.einsum("sbf,fd->sbd", active_low, down_weight, preferred_element_type=jnp.float32)
        + bias_rows[3]
    )
    result, second_pull = jax.vjp(norm_rows, second, gain_rows[1], bias_rows[5])
    kept = (
        inputs_low,
        query,
        keys,
        values,
        log_total,
        attended,
        attended_low,
        normed_low,
        active_low,
        first_pull,
        gelu_pull,
        second_pull,
    )
    return (result, kept)


def backward_layer(upstream, fetched, kept, head_shape):
    qkv_weight, out_weight, up_weight, down_weight = (
        fetched[0],
        fetched[1],
        fetched[2],
        fetched[3],
    )
    (
        inputs_low,
        query,
        keys,
        values,
        log_total,
        attended,
        attended_low,
        normed_low,
        active_low,
        first_pull,
        gelu_pull,
        second_pull,
    ) = kept
    seq_count, block_len, head_count, head_dim = head_shape
    row_axes = (0, 1)
    second_grad, gain_two, shift_two = second_pull(upstream)
    down_in = second_grad.astype(jnp.bfloat16)
    down_grad = jnp.einsum("sbf,sbd->fd", active_low, down_in, preferred_element_type=jnp.float32)
    down_shift = jnp.sum(down_in.astype(jnp.float32), row_axes)
    active_grad = jnp.einsum(
        "sbd,fd->sbf", down_in, down_weight, preferred_element_type=jnp.float32
    )
    hidden_grad = gelu_pull(active_grad)[0].astype(jnp.bfloat16)
    up_grad = jnp.einsum("sbd,sbf->df", normed_low, hidden_grad, preferred_element_type=jnp.float32)
    up_shift_grad = jnp.sum(hidden_grad.astype(jnp.float32), row_axes)
    normed_grad = second_grad + jnp.einsum(
        "sbf,df->sbd", hidden_grad, up_weight, preferred_element_type=jnp.float32
    )
    mixed_grad, gain_one, shift_one = first_pull(normed_grad)
    out_in = mixed_grad.astype(jnp.bfloat16)
    out_weight_grad = jnp.einsum(
        "sbe,sbd->ed", attended_low, out_in, preferred_element_type=jnp.float32
    )
    out_shift = jnp.sum(out_in.astype(jnp.float32), row_axes)
    attend_grad = (
        jnp.einsum("sbd,ed->sbe", out_in, out_weight, preferred_element_type=jnp.float32)
        .astype(jnp.bfloat16)
        .reshape(head_shape)
    )
    delta_rows = jnp.sum(attend_grad.astype(jnp.float32) * attended.reshape(head_shape), -1)
    lse_rows = log_total.transpose(0, 2, 1)
    lse_all, delta_all = (
        lax.all_gather(lse_rows, "blk", axis=1, tiled=True),
        lax.all_gather(delta_rows, "blk", axis=1, tiled=True),
    )
    delta_heads = delta_rows.transpose(0, 2, 1)
    key_part = lax.all_gather(keys, "blk", axis=1, tiled=True)
    value_part = lax.all_gather(values, "blk", axis=1, tiled=True)
    scores = (
        jnp.einsum("sqhd,skhd->shqk", query, key_part, preferred_element_type=jnp.float32)
        * SCORE_SCALE
    )
    probs = jnp.exp(scores - log_total[..., None])
    prob_grad = jnp.einsum(
        "sqhd,skhd->shqk", attend_grad, value_part, preferred_element_type=jnp.float32
    )
    score_grad = (probs * (prob_grad - delta_heads[..., None])).astype(jnp.bfloat16)
    query_grad = (
        jnp.einsum("shqk,skhd->sqhd", score_grad, key_part, preferred_element_type=jnp.float32)
        * SCORE_SCALE
    )
    query_part = lax.all_gather(query, "blk", axis=1, tiled=True)
    grad_part = lax.all_gather(attend_grad, "blk", axis=1, tiled=True)
    lse_part = lse_all.transpose(0, 2, 1)
    delta_part = delta_all.transpose(0, 2, 1)
    scores = (
        jnp.einsum("sqhd,skhd->shqk", query_part, keys, preferred_element_type=jnp.float32)
        * SCORE_SCALE
    )
    probs = jnp.exp(scores - lse_part[..., None])
    value_acc = jnp.einsum(
        "shqk,sqhd->skhd", probs.astype(jnp.bfloat16), grad_part, preferred_element_type=jnp.float32
    )
    prob_grad = jnp.einsum("sqhd,skhd->shqk", grad_part, values, preferred_element_type=jnp.float32)
    score_grad = (probs * (prob_grad - delta_part[..., None])).astype(jnp.bfloat16)
    key_acc = (
        jnp.einsum("shqk,sqhd->skhd", score_grad, query_part, preferred_element_type=jnp.float32)
        * SCORE_SCALE
    )
    flat_shape = (seq_count, block_len, head_count * head_dim)
    query_low = query_grad.reshape(flat_shape).astype(jnp.bfloat16)
    key_low = key_acc.reshape(flat_shape).astype(jnp.bfloat16)
    value_low = value_acc.reshape(flat_shape).astype(jnp.bfloat16)
    proj_grad = jnp.concatenate((query_low, key_low, value_low), -1)
    qkv_grad = jnp.einsum("sbd,sbe->de", inputs_low, proj_grad, preferred_element_type=jnp.float32)
    query_shift = jnp.sum(query_low.astype(jnp.float32), row_axes)
    value_shift = jnp.sum(value_low.astype(jnp.float32), row_axes)
    inputs_grad = mixed_grad + jnp.einsum(
        "sbe,de->sbd", proj_grad, qkv_weight, preferred_element_type=jnp.float32
    )
    shift_rows = jnp.stack((query_shift, value_shift, out_shift, down_shift, shift_one, shift_two))
    gain_grad = jnp.stack((gain_one, gain_two))
    return (
        inputs_grad,
        (qkv_grad, out_weight_grad, up_grad, down_grad, shift_rows, up_shift_grad, gain_grad),
    )


def general_shards(
    hidden_in,
    mask_index,
    mask_count,
    replacement,
    out_grad,
    w_qkv,
    w_out,
    w_up,
    w_down,
    biases,
    up_bias,
    gains,
):
    seq_count, block_len, model_width = hidden_in.shape
    layer_count = w_qkv.shape[0]
    head_shape = (seq_count, block_len, HEADS, model_width // HEADS)
    offset = lax.axis_index("blk") * block_len
    places = offset + jnp.arange(block_len, dtype=jnp.int32)
    slot_ids = jnp.arange(mask_index.shape[1], dtype=jnp.int32)
    hit_table = (mask_index[:, None, :] == places[None, :, None]) & (
        slot_ids[None, None, :] < mask_count[:, None, None]
    )
    hit_low = hit_table.astype(jnp.bfloat16)
    chosen = jnp.any(hit_table, -1, keepdims=True)
    placed = jnp.einsum("sbm,smd->sbd", hit_low, replacement, preferred_element_type=jnp.float32)
    current = jnp.where(chosen, placed, hidden_in.astype(jnp.float32))
    upstream = jnp.einsum("sbm,smd->sbd", hit_low, out_grad, preferred_element_type=jnp.float32)
    shard_shapes = (w_qkv.shape[1:], w_out.shape[1:], w_up.shape[1:], w_down.shape[1:])
    saved_weights = []
    saved_state = []
    for layer_idx in range(layer_count):
        fetched = (
            lax.all_gather(w_qkv[layer_idx], BOTH, axis=0, tiled=True),
            lax.all_gather(w_out[layer_idx], BOTH, axis=0, tiled=True),
            lax.all_gather(w_up[layer_idx], BOTH, axis=0, tiled=True),
            lax.all_gather(w_down[layer_idx], BOTH, axis=0, tiled=True),
            lax.all_gather(biases[layer_idx], BOTH, axis=1, tiled=True),
            lax.all_gather(up_bias[layer_idx], BOTH, axis=0, tiled=True),
            lax.all_gather(gains[layer_idx], BOTH, axis=1, tiled=True),
        )
        saved_weights.append(None)
        current, state = forward_layer(current, fetched, head_shape)
        saved_state.append(state)
    grad_now = upstream
    summed = [None] * layer_count
    for layer_idx in reversed(range(layer_count)):
        fetched = (
            lax.all_gather(w_qkv[layer_idx], BOTH, axis=0, tiled=True),
            lax.all_gather(w_out[layer_idx], BOTH, axis=0, tiled=True),
            lax.all_gather(w_up[layer_idx], BOTH, axis=0, tiled=True),
            lax.all_gather(w_down[layer_idx], BOTH, axis=0, tiled=True),
            lax.all_gather(biases[layer_idx], BOTH, axis=1, tiled=True),
            lax.all_gather(up_bias[layer_idx], BOTH, axis=0, tiled=True),
            lax.all_gather(gains[layer_idx], BOTH, axis=1, tiled=True),
        )
        grad_now, terms = backward_layer(grad_now, fetched, saved_state[layer_idx], head_shape)
        flat_terms = (
            terms[0].reshape(-1, 128),
            terms[1].reshape(-1, 128),
            terms[2].reshape(-1, 128),
            terms[3].reshape(-1, 128),
            terms[4],
            terms[5],
            terms[6],
        )
        reduced = (
            lax.psum_scatter(flat_terms[0], BOTH, scatter_dimension=0, tiled=True),
            lax.psum_scatter(flat_terms[1], BOTH, scatter_dimension=0, tiled=True),
            lax.psum_scatter(flat_terms[2], BOTH, scatter_dimension=0, tiled=True),
            lax.psum_scatter(flat_terms[3], BOTH, scatter_dimension=0, tiled=True),
            lax.psum_scatter(flat_terms[4], BOTH, scatter_dimension=1, tiled=True),
            lax.psum_scatter(flat_terms[5], BOTH, scatter_dimension=0, tiled=True),
            lax.psum_scatter(flat_terms[6], BOTH, scatter_dimension=1, tiled=True),
        )
        summed[layer_idx] = tuple(
            (reduced[member].reshape(shard_shapes[member]) for member in range(4))
        ) + tuple(reduced[4:])
    stacked = [jnp.stack([entry[member] for entry in summed]) for member in range(7)]
    return (
        current.astype(jnp.bfloat16),
        grad_now,
        stacked[0],
        stacked[1],
        stacked[2],
        stacked[3],
        stacked[4],
        stacked[5],
        stacked[6],
    )


NT = (((1,), (1,)), ((), ()))
TN = (((0,), (0,)), ((), ()))
F32 = jnp.float32
BF = jnp.bfloat16


def dot(a, b, dims):
    return lax.dot_general(a, b, dims, preferred_element_type=F32)


MESH = pl.DeviceIdType.MESH
UNITS = 12
TILE = 256
LAGS = (3, 1, 3, 4)
DIRECT = 8
TURN_STEPS = (0, 2, 4, 6)
BEGIN = 9
BUDGET = 4.5


def place_of():
    batch = lax.axis_index("batch")
    return batch, lax.axis_index("blk"), batch // 4, lax.rem(batch // 2, 2), lax.rem(batch, 2)


def columns(tile):
    return pl.ds(pl.multiple_of(tile * TILE, TILE), TILE)


def forward_kernel(
    first_ref,
    qkv_in,
    out_in,
    up_in,
    down_in,
    small_ref,
    w_ref,
    out_ref,
    rows_ref,
    lse_ref,
    qkv_ref,
    kv_ref,
    mix_ref,
    flip_ref,
    slope_ref,
    unit_ref,
    scale_ref,
    cur,
    low,
    qkv,
    sib,
    mix,
    nrm,
    acc,
    act,
    slope,
    unit,
    scale,
    wbuf,
    flipped,
    shard,
    small_all,
    local_sems,
    own_sems,
    save_sems,
    send_sems,
    recv_sems,
    side_send,
    side_recv,
    turn_send,
    turn_recv,
    layers,
):
    batch, z, y, x, core = place_of()
    total = layers * UNITS
    yx = 2 * y + x
    column = 4 * y + 2 * x
    here = {"x": (batch ^ 2, z), "y": (batch ^ 4, z), "core": (batch ^ 1, z)}

    def remote(src, dst, send, recv, device):
        return pltpu.make_async_remote_copy(
            src_ref=src,
            dst_ref=dst,
            send_sem=send,
            recv_sem=recv,
            device_id=device,
            device_id_type=MESH,
        )

    flying = {}

    def launch(kind, unit_id, copies):
        flying[kind, unit_id] = copies
        for copy in copies:
            copy.start()

    def landed(kind, unit_id):
        for copy in flying[kind, unit_id]:
            copy.wait_recv()

    def hop(unit_id, slot, src, dst, device):
        return remote(src, dst, send_sems.at[unit_id, slot], recv_sems.at[unit_id, slot], device)

    own_rows = pl.ds(pl.multiple_of(z * 32, 32), 32)

    def straight(unit_id):
        return 1024 if unit_id < DIRECT else 1024 - 128

    def along(unit_id):
        cols = pl.ds(0, straight(unit_id))
        dst = w_ref.at[unit_id, yx, core, own_rows, cols]
        src = shard.at[unit_id, :, cols]
        copies = []
        if unit_id >= DIRECT:
            edge = pl.ds(1024 - 128, 128)
            piece, spot = shard.at[unit_id, :, edge], w_ref.at[unit_id, yx, core, own_rows, edge]
            copies += [hop(unit_id, 8, piece, spot, here["x"]), hop(unit_id, 9, piece, spot, here["y"])]
        for step in (1, 2, 3):
            copies.append(hop(unit_id, step - 1, src, dst, (batch, lax.rem(z + step, 4))))
        return copies

    def across(unit_id):
        line = w_ref.at[unit_id, yx, core, :, pl.ds(0, straight(unit_id))]
        copies = []
        if unit_id >= DIRECT:
            edge = pl.ds(1024 - 128, 128)
            if unit_id % 2:
                piece, to = w_ref.at[unit_id, 2 * y + 1 - x, core, own_rows, edge], here["y"]
            else:
                piece, to = w_ref.at[unit_id, 2 - 2 * y + x, core, own_rows, edge], here["x"]
            copies.append(hop(unit_id, 10, piece, piece, to))
        copies += [hop(unit_id, 3, line, line, here["x"]), hop(unit_id, 4, line, line, here["y"])]
        return copies

    def corner(unit_id):
        full = straight(unit_id)
        half = 384 if full < 1024 and unit_id % 2 else 512
        left = w_ref.at[unit_id, 2 * y + 1 - x, core, :, pl.ds(0, half)]
        right = w_ref.at[unit_id, 2 - 2 * y + x, core, :, pl.ds(half, full - half)]
        copies = []
        if unit_id >= DIRECT:
            block = w_ref.at[unit_id, :, core, own_rows, pl.ds(1024 - 128, 128)]
            for step in (1, 2, 3):
                to = (batch, lax.rem(z + step, 4))
                copies.append(hop(unit_id, 10 + step, block, block, to))
        copies += [hop(unit_id, 5, left, left, here["y"]), hop(unit_id, 6, right, right, here["x"])]
        return copies

    def inner(unit_id):
        block = w_ref.at[unit_id, :, core]
        return [hop(unit_id, 7, block, block, here["core"])]

    def side(slot, src, dst, device):
        return remote(src, dst, side_send.at[slot], side_recv.at[slot], device)

    def layout(layer):
        base = layer * UNITS
        for part in range(3):
            shard[base + part] = qkv_in[layer, :, part * 1024 : part * 1024 + 1024]
        shard[base + 3] = out_in[layer]
        lane = lax.broadcasted_iota(jnp.int32, (32, 128), 1) // 32
        for j in range(4):
            shard[base + 5 + 2 * j] = down_in[layer, j * 32 : j * 32 + 32]
            for block in range(8):
                made = None
                for part in range(4):
                    start = (4 * block + part) * 128
                    value = up_in[layer, :, start : start + 128].astype(F32)
                    if part != j:
                        value = pltpu.roll(value, ((part - j) * 32) % 128, 1)
                    made = value if made is None else jnp.where(lane == part, value, made)
                shard[base + 4 + 2 * j, :, block * 128 : block * 128 + 128] = made.astype(BF)

    owns = [
        pltpu.make_async_copy(
            shard.at[unit_id], w_ref.at[unit_id, yx, core, own_rows], own_sems.at[unit_id]
        )
        for unit_id in range(total)
    ]
    mine = small_all.at[y, x, core, z]
    mine[...] = small_ref[...]
    launch(
        "small",
        0,
        [side(step - 1, small_ref, mine, (batch, lax.rem(z + step, 4))) for step in (1, 2, 3)],
    )

    def turn(j, half):
        to = 2 * core + j
        block = lax.rem(to - z + 4, 4)
        src = first_ref.at[j, pl.ds(half * 128, 128)]
        dst = low.at[pl.ds(pl.multiple_of(block * 128, 128), 128)]
        send, recv = turn_send.at[2 * j + half], turn_recv.at[block]
        return (
            lambda: pltpu.make_async_copy(src, dst, local_sems.at[0]),
            lambda: remote(src, dst, send, recv, (column + half, to)),
            jnp.logical_and(to == z, core == half),
        )

    def turned(block):
        spot = low.at[pl.ds(block * 128, 128)]
        return remote(spot, spot, turn_send.at[0], turn_recv.at[block], here["core"])

    for layer in range(layers):
        layout(layer)
        if layer == 0:
            for unit_id in range(1):
                owns[unit_id].start()
                launch("along", unit_id, along(unit_id))
            for unit_id in range(1, LAGS[0]):
                owns[unit_id].start()
                launch("along", unit_id, along(unit_id))
    own_turn = core == z // 2

    def turn_out(j, half):
        local, away, stays = turn(j, half)
        pl.when(stays)(lambda: local().start())
        pl.when(jnp.logical_not(stays))(lambda: away().start())


    def small_hop(number):
        landed("small", number - 1)
        if number == 1:
            line = small_all.at[y, x, core]
            launch("small", 1, [side(3, line, line, here["x"])])
        elif number == 2:
            plane = small_all.at[y, :, core]
            launch("small", 2, [side(4, plane, plane, here["y"])])
        elif number == 3:
            cube = small_all.at[:, :, core]
            launch("small", 3, [side(5, cube, cube, here["core"])])

    def begin():
        small_hop(4)
        for block in range(8):
            four = small_all[block // 4, (block // 2) % 2, block % 2]
            rows_ref[:, block * 128 : block * 128 + 128] = (four[0] + four[1]) + (four[2] + four[3])
        local = turn(0, 0)[0]
        pl.when(own_turn)(lambda: local().wait())
        pl.when(jnp.logical_not(own_turn))(lambda: turned(0).wait_recv())
        for block in range(1, 4):
            turned(block).wait_recv()

        def body(step, carry):
            rows = pl.ds(pl.multiple_of(step * 64, 64), 64)
            cur[rows] = low[rows].astype(F32)
            return carry

        lax.fori_loop(0, 8, body, 0)

    saves = {}

    def save(name, src, dst, slot):
        if name in saves:
            saves[name].wait()
        saves[name] = pltpu.make_async_copy(src, dst, save_sems.at[slot])
        saves[name].start()

    def settle(*names):
        for name in names:
            if name in saves:
                saves.pop(name).wait()

    def norm(layer, which, gain_row, shift_row):
        gain = rows_ref[pl.ds(gain_row, 1)]
        shift_by = rows_ref[pl.ds(shift_row, 1)]

        def body(step, carry):
            rows = pl.ds(step * 64, 64)
            value = acc[rows]
            center = value - jnp.mean(value, -1, keepdims=True)
            spread = jnp.mean(center * center, -1, keepdims=True)
            root = lax.rsqrt(spread + NORM_EPS)
            normal = center * root
            unit[which, rows] = normal
            scale[which, rows] = jnp.broadcast_to(root, (64, 128))
            result = normal * gain + shift_by
            if which == 0:
                acc[rows] = result + rows_ref[pl.ds(layer * 12 + 3, 1)]
                nrm[rows] = result.astype(BF)
            else:
                cur[rows] = result
                low[rows] = result.astype(BF)
            return carry

        lax.fori_loop(0, 8, body, 0)
        save(("unit", which), unit.at[which], unit_ref.at[layer, which], 8 + which)
        save(("scale", which), scale.at[which], scale_ref.at[layer, which], 10 + which)

    def heads(layer, begin, end):
        def body(j, carry):
            lanes = pl.ds(pl.multiple_of(j * 128, 128), 128)
            k_lanes = pl.ds(pl.multiple_of(1024 + j * 128, 128), 128)
            v_lanes = pl.ds(pl.multiple_of(2048 + j * 128, 128), 128)
            q = qkv[:, lanes]
            lane = lax.broadcasted_iota(jnp.int32, q.shape, 1)
            outs = []
            for head in range(2):
                qh = jnp.where((lane // 64) == head, q, jnp.zeros_like(q))
                s_own = dot(qkv[:, k_lanes], qh, NT)
                s_sib = dot(sib[layer, 0, :, lanes], qh, NT)
                top = jnp.maximum(
                    jnp.max(s_own, 0, keepdims=True), jnp.max(s_sib, 0, keepdims=True)
                )
                p_own = jnp.exp(s_own - top)
                p_sib = jnp.exp(s_sib - top)
                mass = jnp.sum(p_own, 0, keepdims=True) + jnp.sum(p_sib, 0, keepdims=True)
                lse_ref[layer, j, pl.ds(head, 1)] = top + jnp.log(mass)
                o = dot(qkv[:, v_lanes], p_own.astype(BF), TN) + dot(
                    sib[layer, 1, :, lanes], p_sib.astype(BF), TN
                )
                outs.append(o[head * 64 : head * 64 + 64] / mass)
            mix[:, lanes] = jnp.transpose(jnp.concatenate(outs, 0)).astype(BF)
            return carry

        lax.fori_loop(begin, end, body, 0)

    fetched = {}

    def fetch(unit_id):
        if unit_id < total and unit_id not in fetched:
            fetched[unit_id] = pltpu.make_async_copy(
                w_ref.at[unit_id], wbuf.at[unit_id % 2], local_sems.at[2 + unit_id % 2]
            )
            fetched[unit_id].start()

    def weight(unit_id, tile):
        return wbuf[unit_id % 2, :, :, :, columns(tile)].reshape(1024, TILE)

    def project(unit_id):
        layer, kind = unit_id // UNITS, unit_id % UNITS
        base = layer * 12
        if kind == 0:
            settle("qkv")
        for copy in flying.pop(("kv", (layer - 1, kind)), ()):
            copy.wait_send()

        def body(tile, carry):
            value = jnp.dot(low[...], weight(unit_id, tile), preferred_element_type=F32)
            cols = columns(tile)
            if kind != 1:
                value = value + rows_ref[pl.ds(base + kind // 2, 1), cols]
            value = value.astype(BF)
            if kind == 0:
                value = (value.astype(F32) * SCORE_SCALE).astype(BF)
            qkv[:, columns(tile + 4 * kind)] = value
            return carry

        lax.fori_loop(0, 4, body, 0)
        if kind:
            spot = 6 + 2 * layer + kind - 1
            src, dst = qkv.at[:, pl.ds(1024 * kind, 1024)], sib.at[layer, kind - 1]
            launch("kv", (layer, kind), [side(spot, src, dst, here["core"])])
        if kind == 2:
            save("qkv", qkv, qkv_ref.at[layer], 1)

    def attention(layer, group):
        if group == 0:
            landed("kv", (layer, 1))
            landed("kv", (layer, 2))
            save("kv", sib.at[layer], kv_ref.at[layer], 2)
            settle("mix")
        heads(layer, 2 * group, 2 * group + 2)
        if group == 3:
            save("mix", mix, mix_ref.at[layer], 3)

    def mixing(unit_id):
        layer = unit_id // UNITS
        base = layer * 12
        settle(("unit", 0), ("scale", 0))

        def body(tile, carry):
            cols = columns(tile)
            value = jnp.dot(mix[...], weight(unit_id, tile), preferred_element_type=F32)
            acc[:, cols] = cur[:, cols] + value + rows_ref[pl.ds(base + 2, 1), cols]
            return carry

        lax.fori_loop(0, 4, body, 0)
        norm(layer, 0, base + 6, base + 4)

    def widen(unit_id):
        layer, j = unit_id // UNITS, unit_id % UNITS // 2 - 2
        base = layer * 12
        settle(("slope", j))

        def body(tile, carry):
            cols = columns(tile)
            value = jnp.dot(nrm[...], weight(unit_id, tile), preferred_element_type=F32)
            value = value + rows_ref[pl.ds(base + 8 + j, 1), cols]
            gate = 0.5 * (1.0 + lax.erf(value * 0.7071067811865476))
            act[j, :, cols] = (value * gate).astype(BF)
            bell = jnp.exp(-0.5 * value * value)
            slope[j, :, cols] = (gate + value * (0.3989422804014327 * bell)).astype(BF)
            return carry

        lax.fori_loop(0, 4, body, 0)
        save(("slope", j), slope.at[j], slope_ref.at[layer, j], 16 + j)

    def narrow(unit_id):
        layer, j = unit_id // UNITS, unit_id % UNITS // 2 - 2
        base = layer * 12

        def body(tile, carry):
            cols = columns(tile)
            acc[:, cols] += jnp.dot(act[j], weight(unit_id, tile), preferred_element_type=F32)
            return carry

        lax.fori_loop(0, 4, body, 0)
        if j == 3:
            settle(("unit", 1), ("scale", 1))
            norm(layer, 1, base + 7, base + 5)
            if layer == layers - 1:
                save("low", low, out_ref, 0)

    turns = [0]

    def flip(source, layer, index):
        slot = turns[0] % 2
        turns[0] += 1
        settle(("flip", slot))

        def body(block, carry):
            for half in range(2):
                lanes = pl.ds(pl.multiple_of(block * 256 + half * 128, 128), 128)
                flipped[slot, half, block] = jnp.transpose(source[:, lanes])
            return carry

        lax.fori_loop(0, 4, body, 0)
        save(("flip", slot), flipped.at[slot], flip_ref.at[layer, index], 4 + slot)

    chunks = []

    def plan_flip(unit_id, source, index):
        part = functools.partial(flip, source, unit_id // UNITS, index)
        chunks.append((unit_id, part, 1.3))

    for unit_id in range(total):
        layer, kind = unit_id // UNITS, unit_id % UNITS
        if kind < 3:
            chunks.append((unit_id, project, 2.0))
            if kind == 0:
                plan_flip(unit_id, low, 0)
        elif kind == 3:
            for group in range(4):
                chunks.append((unit_id - 1, functools.partial(attention, layer, group), 4.5))
            plan_flip(unit_id - 1, mix, 2)
            chunks.append((unit_id, mixing, 4.5))
            plan_flip(unit_id, nrm, 1)
        elif kind % 2 == 0:
            chunks.append((unit_id, widen, 3.5))
            plan_flip(unit_id, act.at[kind // 2 - 2], 3 + kind // 2 - 2)
        else:
            chunks.append((unit_id, narrow, 5.0 if kind == 11 else 1.5))

    def advance(have, budget):
        spent = 0.0
        while chunks and chunks[0][0] <= have and (spent == 0.0 or spent + chunks[0][2] <= budget):
            unit_id, chunk, cost = chunks.pop(0)
            if isinstance(chunk, functools.partial):
                chunk()
            else:
                fetch(unit_id)
                fetched[unit_id].wait()
                chunk(unit_id)
                if unit_id + 2 <= have:
                    fetch(unit_id + 2)
            spent += cost

    ahead, corner_lag, inner_lag, use_lag = LAGS
    step, have = 0, -1
    while step < total + use_lag or chunks:
        if step + ahead < total:
            owns[step + ahead].start()
            launch("along", step + ahead, along(step + ahead))
        if step < total:
            owns[step].wait()
            landed("along", step)
            launch("across", step, across(step))
        if 0 < step < 4:
            small_hop(step)
        if step in TURN_STEPS:
            number = TURN_STEPS.index(step)
            turn_out(number // 2, number % 2)
        if step > BEGIN:
            advance(have, BUDGET)
        if 0 <= step - corner_lag < total:
            landed("across", step - corner_lag)
            launch("corner", step - corner_lag, corner(step - corner_lag))
        if 0 <= step - inner_lag < total:
            landed("corner", step - inner_lag)
            launch("inner", step - inner_lag, inner(step - inner_lag))
        if step == BEGIN:
            begin()
        if 0 <= step - use_lag < total:
            landed("inner", step - use_lag)
            have = step - use_lag
            if have < 2 or have - 2 in fetched and all(item[0] > have - 2 for item in chunks):
                fetch(have)
        if step >= BEGIN:
            advance(have, BUDGET)
        step += 1
    for j in range(2):
        for half in range(2):
            local, away, stays = turn(j, half)
            pl.when(jnp.logical_not(stays))(lambda: away().wait_send())
    for copies in flying.values():
        for copy in copies:
            copy.wait_send()
    settle(*list(saves))


def forward_pass(first, w_qkv, w_out, w_up, w_down, small):
    layers = w_qkv.shape[0]
    width = first.shape[2]
    rows = first.shape[0] * first.shape[1]
    any_spec = pl.BlockSpec(memory_space=pl.ANY)
    vmem = pl.BlockSpec(memory_space=pltpu.VMEM)
    shape = jax.ShapeDtypeStruct
    total = layers * UNITS
    return pl.pallas_call(
        functools.partial(forward_kernel, layers=layers),
        in_specs=[vmem] * 6,
        out_specs=[any_spec, any_spec, vmem, vmem] + [any_spec] * 7,
        out_shape=[
            shape((total, 4, 2, 128, width), BF),
            shape((rows, width), BF),
            shape((layers * 12, width), F32),
            shape((layers, 8, 2, rows), F32),
            shape((layers, rows, 3 * width), BF),
            shape((layers, 2, rows, width), BF),
            shape((layers, rows, width), BF),
            shape((layers, 7, 2, 4, 128, rows), BF),
            shape((layers, 4, rows, width), BF),
            shape((layers, 2, rows, width), F32),
            shape((layers, 2, rows, 128), F32),
        ],
        scratch_shapes=[
            pltpu.VMEM((rows, width), F32),
            pltpu.VMEM((rows, width), BF),
            pltpu.VMEM((rows, 3 * width), BF),
            pltpu.VMEM((layers, 2, rows, width), BF),
            pltpu.VMEM((rows, width), BF),
            pltpu.VMEM((rows, width), BF),
            pltpu.VMEM((rows, width), F32),
            pltpu.VMEM((4, rows, width), BF),
            pltpu.VMEM((4, rows, width), BF),
            pltpu.VMEM((2, rows, width), F32),
            pltpu.VMEM((2, rows, 128), F32),
            pltpu.VMEM((2, 4, 2, 128, width), BF),
            pltpu.VMEM((2, 2, 4, 128, rows), BF),
            pltpu.VMEM((total, 32, width), BF),
            pltpu.VMEM((2, 2, 2, 4, layers * 12, 128), F32),
            pltpu.SemaphoreType.DMA((4,)),
            pltpu.SemaphoreType.DMA((total,)),
            pltpu.SemaphoreType.DMA((20,)),
            pltpu.SemaphoreType.DMA((total, 14)),
            pltpu.SemaphoreType.DMA((total, 14)),
            pltpu.SemaphoreType.DMA((6 + 2 * layers,)),
            pltpu.SemaphoreType.DMA((6 + 2 * layers,)),
            pltpu.SemaphoreType.DMA((4,)),
            pltpu.SemaphoreType.DMA((4,)),
        ],
        compiler_params=pltpu.CompilerParams(
            has_side_effects=True, vmem_limit_bytes=60 << 20
        ),
        name="forward_pass",
    )(first, w_qkv, w_out, w_up, w_down, small)


def backward_kernel(
    top_ref,
    last_ref,
    w_ref,
    rows_ref,
    lse_ref,
    qkv_ref,
    kv_ref,
    mix_ref,
    flip_ref,
    slope_ref,
    unit_ref,
    scale_ref,
    last_out,
    grad_out,
    qkv_out,
    out_out,
    up_out,
    down_out,
    bias_out,
    up_bias_out,
    gain_out,
    grad,
    edge,
    unit,
    scale,
    arena,
    span,
    feat,
    turned,
    wbuf,
    send,
    mine,
    land,
    wide,
    slim,
    ends,
    small_all,
    small_in,
    staged,
    up_all,
    load_sems,
    store_sems,
    send_sems,
    recv_sems,
    side_send,
    side_recv,
    turn_send,
    turn_recv,
    layers,
):
    batch, z, y, x, core = place_of()
    total = layers * UNITS
    here = {"x": (batch ^ 2, z), "y": (batch ^ 4, z), "core": (batch ^ 1, z)}
    slots = 6

    def remote(src, dst, send_sem, recv_sem, device):
        return pltpu.make_async_remote_copy(
            src_ref=src,
            dst_ref=dst,
            send_sem=send_sem,
            recv_sem=recv_sem,
            device_id=device,
            device_id_type=MESH,
        )

    incoming, outgoing = {}, {}

    def launch(kind, number, copies):
        incoming[kind, number] = copies
        outgoing[kind, number] = copies
        for copy in copies:
            copy.start()

    def landed(kind, number):
        for copy in incoming.pop((kind, number)):
            copy.wait_recv()

    def sent(kind, number):
        for copy in outgoing.pop((kind, number), ()):
            copy.wait_send()

    def hop(number, slot, src, dst, device):
        return remote(src, dst, send_sems.at[number, slot], recv_sems.at[number, slot], device)

    def side(slot, src, dst, device):
        return remote(src, dst, side_send.at[slot], side_recv.at[slot], device)

    loads = {}

    def fetch(name, src, dst, slot):
        loads[name] = pltpu.make_async_copy(src, dst, load_sems.at[slot])
        loads[name].start()

    def ready(name):
        loads.pop(name).wait()

    order = []
    for layer in reversed(range(layers)):
        for j in range(4):
            order += [layer * UNITS + 5 + 2 * j, layer * UNITS + 4 + 2 * j]
        order += [layer * UNITS + 3, layer * UNITS, layer * UNITS + 1, layer * UNITS + 2]

    def fetch_weight(number):
        if number < total:
            fetch(("w", number), w_ref.at[order[number]], wbuf.at[number % 2], number % 2)

    def rows_of(number, tile):
        return wbuf[number % 2, tile].reshape(TILE, 1024)

    def fetch_turned(slot, layer, index):
        for half, which in enumerate((core, 1 - core)):
            fetch(
                (slot, half),
                flip_ref.at[layer, index, which],
                turned.at[slot, half],
                10 + 2 * slot + half,
            )

    def ready_turned(slot):
        ready((slot, 0))
        ready((slot, 1))

    def produce(number, slot, upper):
        buffer = number % 2
        sent("core", number - 2)

        def body(tile, carry):
            cols = columns(tile)
            value = jnp.dot(
                turned[slot, 1].reshape(512, 512), upper[:, cols], preferred_element_type=F32
            )
            send[buffer, :, :, cols] = value.astype(BF).reshape(4, 128, TILE)
            return carry

        lax.fori_loop(0, 4, body, 0)
        launch("core", number, [hop(number, 0, send.at[buffer], land.at[number % PLACES], here["core"])])

        def own(tile, carry):
            cols = columns(tile)
            value = jnp.dot(
                turned[slot, 0].reshape(512, 512), upper[:, cols], preferred_element_type=F32
            )
            mine[number % slots, :, :, cols] = value.astype(BF).reshape(4, 128, TILE)
            return carry

        lax.fori_loop(0, 4, own, 0)

    left, right = pl.ds(0, 512), pl.ds(512, 512)

    def chunk_rows(chunk):
        return pl.ds(pl.multiple_of(chunk * 32, 32), 32)

    def stage_core(number):
        part = land.at[number % PLACES]
        landed("core", number)

        def body(block, carry):
            part[block] = part[block] + mine[number % slots, block]
            return carry

        lax.fori_loop(0, 4, body, 0)
        spot = number % slots
        launch(
            "wide",
            number,
            [
                hop(number, 1, part.at[pl.ds(2 - 2 * y, 2), :, left], wide.at[spot, 0], here["y"]),
                hop(number, 2, part.at[pl.ds(1 - x, 1), :, right], wide.at[spot, 1, pl.ds(0, 1)], here["x"]),
                hop(number, 3, part.at[pl.ds(3 - x, 1), :, right], wide.at[spot, 1, pl.ds(1, 1)], here["x"]),
            ],
        )

    def stage_wide(number):
        part, spot = land.at[number % PLACES], number % slots
        landed("wide", number)
        for block in range(2):
            spot_y = 2 * y + block
            part[spot_y, :, left] = part[spot_y, :, left] + wide[spot, 0, block]
            spot_x = 2 * block + x
            part[spot_x, :, right] = part[spot_x, :, right] + wide[spot, 1, block]
        launch(
            "slim",
            number,
            [
                hop(number, 4, part.at[2 * y + 1 - x, :, left], slim.at[spot, 0], here["x"]),
                hop(number, 5, part.at[2 - 2 * y + x, :, right], slim.at[spot, 1], here["y"]),
            ],
        )

    def stage_slim(number):
        part, spot = land.at[number % PLACES, 2 * y + x], number % slots
        landed("slim", number)
        part[:, left] = part[:, left] + slim[spot, 0]
        part[:, right] = part[:, right] + slim[spot, 1]
        copies = []
        for step, chunk in enumerate((z ^ 1, z ^ 3)):
            copies.append(hop(number, 6 + step, part.at[chunk_rows(chunk)], ends.at[spot, step], (batch, z ^ 1)))
        launch("pair", number, copies)

    def stage_pair(number):
        part, spot = land.at[number % PLACES, 2 * y + x], number % slots
        landed("pair", number)
        for step, chunk in enumerate((z, z ^ 2)):
            rows = chunk_rows(chunk)
            part[rows] = part[rows] + ends[spot, step]
        src = part.at[chunk_rows(z ^ 2)]
        launch("ends", number, [hop(number, 8, src, ends.at[spot, 2], (batch, z ^ 2))])

    def stage_ends(number):
        part, spot = land.at[number % PLACES, 2 * y + x], number % slots
        landed("ends", number)
        value = part[chunk_rows(z)].astype(F32) + ends[spot, 2].astype(F32)
        layer, kind = order[number] // UNITS, order[number] % UNITS
        j = kind // 2 - 2
        if kind > 3 and kind % 2 == 0:
            lane = lax.broadcasted_iota(jnp.int32, (32, 128), 1) // 32
            if j == 0 and 4 in stores:
                stores.pop(4).wait()
            for block in range(32):
                spot = pl.ds(block * 128, 128)
                piece = value[:, block // 4 * 128 : block // 4 * 128 + 128]
                if j != block % 4:
                    piece = pltpu.roll(piece, ((j - block % 4) * 32) % 128, 1)
                up_all[:, spot] = piece if j == 0 else jnp.where(lane == j, piece, up_all[:, spot])
            if j == 3:
                stores[4] = pltpu.make_async_copy(up_all, up_out.at[layer], store_sems.at[4])
                stores[4].start()
        else:
            slot = number % 4
            if slot in stores:
                stores.pop(slot).wait()
            staged[slot] = value
            if kind < 3:
                dst = qkv_out.at[layer, :, pl.ds(1024 * kind, 1024)]
            else:
                dst = out_out.at[layer] if kind == 3 else down_out.at[layer, j]
            stores[slot] = pltpu.make_async_copy(staged.at[slot], dst, store_sems.at[slot])
            stores[slot].start()
        for kind in ("wide", "slim", "pair", "ends"):
            sent(kind, number)

    ticks = [0]
    stores = {}
    wide_lag, slim_lag, pair_lag, ends_lag = BACK_LAGS

    def first_half():
        step = ticks[0]
        if step < total:
            stage_core(step)
        if 0 <= step - wide_lag < total:
            stage_wide(step - wide_lag)

    def second_half():
        step = ticks[0]
        ticks[0] += 1
        if 0 <= step - slim_lag < total:
            stage_slim(step - slim_lag)
        if 0 <= step - pair_lag < total:
            stage_pair(step - pair_lag)
        if 0 <= step - ends_lag < total:
            stage_ends(step - ends_lag)

    def tick():
        first_half()
        second_half()

    def norm(base, gain_row, shift_row, sum_row):
        gain = rows_ref[pl.ds(base + gain_row, 1)]

        def body(step, carry):
            gains, shifts, sums = carry
            rows = pl.ds(step * 64, 64)
            value = grad[rows]
            normal = unit[rows]
            scaled = value * gain
            inner = jnp.mean(scaled * normal, -1, keepdims=True)
            centre = jnp.mean(scaled, -1, keepdims=True)
            result = scale[rows][:, :1] * (scaled - centre - normal * inner)
            grad[rows] = result
            rounded = result.astype(BF)
            edge[rows] = rounded
            return (
                gains + jnp.sum(value * normal, 0, keepdims=True),
                shifts + jnp.sum(value, 0, keepdims=True),
                sums + jnp.sum(rounded.astype(F32), 0, keepdims=True),
            )

        zero = jnp.zeros((1, 1024), F32)
        gains, shifts, sums = lax.fori_loop(0, 8, body, (zero, zero, zero))
        put_row(base + gain_row, gains)
        put_row(base + shift_row, shifts)
        put_row(base + sum_row, sums)

    def put_row(row, value):
        for block in range(8):
            small_all[block // 2, block % 2, row : row + 1] = value[:, block * 128 : block * 128 + 128]

    def heads(layer, begin, end):
        def body(j, carry):
            lanes = pl.ds(pl.multiple_of(j * 128, 128), 128)
            q = arena[0, :, lanes]
            do = span[:, lanes]
            lane = lax.broadcasted_iota(jnp.int32, q.shape, 1)
            prod = jnp.transpose(do.astype(F32) * feat[:, lanes].astype(F32))
            dq = []
            sums = [[None, None], [None, None]]
            for head in range(2):
                pick = (lane // 64) == head
                qh = jnp.where(pick, q, jnp.zeros_like(q))
                dh = jnp.where(pick, do, jnp.zeros_like(do))
                delta = jnp.sum(prod[head * 64 : head * 64 + 64], 0, keepdims=True)
                lse = lse_ref[layer, j, pl.ds(head, 1)]
                dqh = None
                for half in range(2):
                    k = arena[1 + 2 * half, :, lanes]
                    v = arena[2 + 2 * half, :, lanes]
                    p = jnp.exp(dot(k, qh, NT) - lse)
                    ds = (p * (dot(v, dh, NT) - delta)).astype(BF)
                    dv = jnp.dot(p.astype(BF), dh, preferred_element_type=F32)
                    dk = jnp.dot(ds, qh, preferred_element_type=F32)
                    part = dot(ds, k, TN)
                    dqh = part if dqh is None else dqh + part
                    sums[half][0] = dk if head == 0 else sums[half][0] + dk
                    sums[half][1] = dv if head == 0 else sums[half][1] + dv
                dq.append(dqh)
            arena[5, :, lanes] = (jnp.where(lane < 64, dq[0], dq[1]) * SCORE_SCALE).astype(BF)
            arena[6, :, lanes] = sums[0][0].astype(BF)
            arena[7, :, lanes] = sums[0][1].astype(BF)
            arena[8, :, lanes] = sums[1][0].astype(BF)
            arena[9, :, lanes] = sums[1][1].astype(BF)
            return carry

        lax.fori_loop(begin, end, body, 0)

    def row_sum(row, slot):
        def body(step, carry):
            rows = pl.ds(pl.multiple_of(step * 64, 64), 64)
            return carry + jnp.sum(arena[slot, rows].astype(F32), 0, keepdims=True)

        put_row(row, lax.fori_loop(0, 8, body, jnp.zeros((1, 1024), F32)))

    def pull(number, upper):
        def body(tile, carry):
            cols = columns(tile)
            grad[:, cols] += dot(upper[...], rows_of(number, tile), NT)
            return carry

        ready(("w", number))
        lax.fori_loop(0, 4, body, 0)
        fetch_weight(number + 2)

    def load_attention(layer):
        for part in range(3):
            fetch(("qkv", part), qkv_ref.at[layer, :, pl.ds(1024 * part, 1024)], arena.at[part], 2 + part)
        for part in range(2):
            fetch(("kv", part), kv_ref.at[layer, part], arena.at[3 + part], 5 + part)

    column = 4 * y + 2 * x
    seat = 2 * lax.rem(z, 2) + core
    stays = core == z // 2

    def homeward(which, block, src, dst):
        rows = src.at[pl.ds(block * 128, 128)]
        spot = dst.at[lax.rem(z, 2), pl.ds(pl.multiple_of(core * 128, 128), 128)]
        to = (column + z // 2, lax.rem(z - block + 4, 4))
        return (
            lambda: pltpu.make_async_copy(rows, spot, load_sems.at[14 + which]),
            lambda: remote(rows, spot, turn_send.at[which, block], turn_recv.at[which, seat], to),
        )

    def turn_start(which, src, dst):
        for block in range(4):
            local, away = homeward(which, block, src, dst)
            if block:
                away().start()
            else:
                pl.when(stays)(lambda: local().start())
                pl.when(jnp.logical_not(stays))(lambda: away().start())

    def turn_end(which, src, dst):
        for block in range(4):
            local, away = homeward(which, block, src, dst)
            if block:
                away().wait_send()
            else:
                pl.when(stays)(lambda: local().wait())
                pl.when(jnp.logical_not(stays))(lambda: away().wait_send())
        for place in range(4):
            spot = dst.at[place // 2, pl.ds(place % 2 * 128, 128)]
            came = remote(spot, spot, turn_send.at[which, 0], turn_recv.at[which, place], here["core"])
            own = jnp.logical_and(2 * core + place // 2 == z, core == place % 2)
            pl.when(jnp.logical_not(own))(came.wait_recv)

    fetch("top", top_ref, grad, 7)
    turn_start(0, last_ref, last_out)
    first = True
    for layer in reversed(range(layers)):
        base = layer * 12
        start = (layers - 1 - layer) * UNITS
        if first:
            fetch("unit", unit_ref.at[layer, 1], unit, 8)
            fetch("scale", scale_ref.at[layer, 1], scale, 9)
            fetch_weight(0)
            fetch_weight(1)
            load_attention(layer)
            ready("top")
            fetch_turned(0, layer, 1)
            fetch_turned(1, layer, 3)
        fetch("slope", slope_ref.at[layer, 0], arena.at[9], 16)
        fetch("mix", mix_ref.at[layer], feat, 17)
        first = False
        ready("unit")
        ready("scale")
        norm(base, 7, 5, 3)
        fetch("unit", unit_ref.at[layer, 0], unit, 8)
        fetch("scale", scale_ref.at[layer, 0], scale, 9)
        ready_turned(0)
        for j in range(4):
            number = start + 2 * j
            ready_turned(1)
            produce(number, 1, edge)
            fetch_turned(1, layer, 4 + j if j < 3 else 2)
            ready(("w", number))
            ready("slope")

            def body(tile, carry):
                cols = columns(tile)
                value = dot(edge[...], rows_of(number, tile), NT)
                value = (arena[9, :, cols].astype(F32) * value).astype(BF)
                span[:, cols] = value
                total_row = jnp.sum(value.astype(F32), 0, keepdims=True)
                for block in range(2):
                    small_all[tile, block, pl.ds(base + 8 + j, 1)] = total_row[
                        :, block * 128 : block * 128 + 128
                    ]
                return carry

            lax.fori_loop(0, 4, body, 0)
            fetch_weight(number + 2)
            if j < 3:
                fetch("slope", slope_ref.at[layer, j + 1], arena.at[9], 16)
            first_half()
            produce(number + 1, 0, span)
            pull(number + 1, span)
            second_half()
        ready("unit")
        ready("scale")
        norm(base, 6, 4, 2)
        if layer:
            fetch("unit", unit_ref.at[layer - 1, 1], unit, 8)
            fetch("scale", scale_ref.at[layer - 1, 1], scale, 9)
        fetch_turned(0, layer, 0)
        ready("mix")
        ready_turned(1)
        number = start + 8
        ready(("w", number))

        def body(tile, carry):
            span[:, columns(tile)] = dot(edge[...], rows_of(number, tile), NT).astype(BF)
            return carry

        lax.fori_loop(0, 4, body, 0)
        fetch_weight(number + 2)
        tick()
        produce(number, 1, edge)
        if layer:
            fetch_turned(1, layer - 1, 3)
        for part in range(3):
            ready(("qkv", part))
        for part in range(2):
            ready(("kv", part))
        for group in range(4):
            heads(layer, 2 * group, 2 * group + 2)
            tick()
        place = layers - 1 - layer
        for part in range(2):
            launch(
                "keys",
                2 * place + part,
                [side(2 * place + part, arena.at[8 + part], arena.at[10 + part], here["core"])],
            )
        if layer:
            load_attention(layer - 1)
        ready_turned(0)
        for part in range(3):
            number = start + 9 + part
            if part:
                landed("keys", 2 * place + part - 1)

                def body(step, carry):
                    rows = pl.ds(pl.multiple_of(step * 64, 64), 64)
                    arena[5 + part, rows] = arena[5 + part, rows] + arena[9 + part, rows]
                    return carry

                lax.fori_loop(0, 8, body, 0)
            produce(number, 0, arena.at[5 + part])
            pull(number, arena.at[5 + part])
            if part == 0:
                row_sum(base, 5)
            if part < 2:
                tick()
            elif layer:
                fetch_turned(0, layer - 1, 1)
        sent("keys", 2 * place)
        sent("keys", 2 * place + 1)
        if layer == 0:

            def body(step, carry):
                rows = pl.ds(pl.multiple_of(step * 64, 64), 64)
                edge[rows] = grad[rows].astype(BF)
                return carry

            lax.fori_loop(0, 8, body, 0)
            turn_start(1, edge, grad_out)
        row_sum(base + 1, 7)
        tick()
    base = 2 * layers

    def small_core():
        launch("small", 0, [side(base, small_all.at[:, 1 - core], small_in.at[pl.ds(0, 4)], here["core"])])

    def small_y():
        landed("small", 0)
        sent("small", 0)
        small_all[:, core] = small_all[:, core] + small_in[0:4]
        launch(
            "small",
            1,
            [side(base + 1, small_all.at[pl.ds(2 - 2 * y, 2), core], small_in.at[pl.ds(4, 2)], here["y"])],
        )

    def small_x():
        landed("small", 1)
        sent("small", 1)
        for block in range(2):
            small_all[2 * y + block, core] = small_all[2 * y + block, core] + small_in[4 + block]
        launch(
            "small",
            2,
            [side(base + 2, small_all.at[2 * y + 1 - x, core], small_in.at[6], here["x"])],
        )

    def small_z():
        landed("small", 2)
        sent("small", 2)
        own = small_all.at[2 * y + x, core]
        own[...] = own[...] + small_in[6]
        launch(
            "small",
            3,
            [
                side(base + 2 + step, own, small_in.at[6 + step], (batch, lax.rem(z + step, 4)))
                for step in (1, 2, 3)
            ],
        )

    def small_end():
        landed("small", 3)
        sent("small", 3)
        value = small_all[2 * y + x, core]
        for step in (1, 2, 3):
            value = value + small_in[6 + step]
        mine_row = value[:, 0:32]
        for place in range(1, 4):
            mine_row = jnp.where(z == place, value[:, place * 32 : place * 32 + 32], mine_row)
        for layer in range(layers):
            top = layer * 12
            bias_out[layer] = mine_row[top : top + 6]
            gain_out[layer] = mine_row[top + 6 : top + 8]
            for j in range(4):
                up_bias_out[layer : layer + 1, j * 32 : j * 32 + 32] = mine_row[top + 8 + j : top + 9 + j]

    small_core()
    queue = [small_y, small_x, small_z, small_end]
    while ticks[0] < total + ends_lag or queue:
        if ticks[0] < total + ends_lag:
            tick()
        if queue:
            queue.pop(0)()
    for kind, number in list(outgoing):
        sent(kind, number)
    for copy in stores.values():
        copy.wait()
    turn_end(0, last_ref, last_out)
    turn_end(1, edge, grad_out)


BACK_LAGS = (2, 4, 5, 6)
PLACES = 13


def backward_pass(top, last, saved):
    w, rows, lse, qkv, kv, mix, flip, slope, unit, scale = saved
    total = w.shape[0]
    layers = total // UNITS
    tokens, width = top.shape
    any_spec = pl.BlockSpec(memory_space=pl.ANY)
    vmem = pl.BlockSpec(memory_space=pltpu.VMEM)
    shape = jax.ShapeDtypeStruct
    return pl.pallas_call(
        functools.partial(backward_kernel, layers=layers),
        in_specs=[any_spec] * 3 + [vmem, vmem] + [any_spec] * 7,
        out_specs=[any_spec] * 6 + [vmem] * 3,
        out_shape=[
            shape((2, tokens // 2, width), BF),
            shape((2, tokens // 2, width), BF),
            shape((layers, 32, 3 * width), F32),
            shape((layers, 32, width), F32),
            shape((layers, 32, 4 * width), F32),
            shape((layers, 4, 32, width), F32),
            shape((layers, 6, 32), F32),
            shape((layers, 128), F32),
            shape((layers, 2, 32), F32),
        ],
        scratch_shapes=[
            pltpu.VMEM((tokens, width), F32),
            pltpu.VMEM((tokens, width), BF),
            pltpu.VMEM((tokens, width), F32),
            pltpu.VMEM((tokens, 128), F32),
            pltpu.VMEM((12, tokens, width), BF),
            pltpu.VMEM((tokens, width), BF),
            pltpu.VMEM((tokens, width), BF),
            pltpu.VMEM((2, 2, 4, 128, tokens), BF),
            pltpu.VMEM((2, 4, 2, 128, width), BF),
            pltpu.VMEM((2, 4, 128, width), BF),
            pltpu.VMEM((6, 4, 128, width), BF),
            pltpu.VMEM((PLACES, 4, 128, width), BF),
            pltpu.VMEM((6, 2, 2, 128, width // 2), BF),
            pltpu.VMEM((6, 2, 128, width // 2), BF),
            pltpu.VMEM((6, 3, 32, width), BF),
            pltpu.VMEM((4, 2, layers * 12, 128), F32),
            pltpu.VMEM((10, layers * 12, 128), F32),
            pltpu.VMEM((4, 32, width), F32),
            pltpu.VMEM((32, 4 * width), F32),
            pltpu.SemaphoreType.DMA((18,)),
            pltpu.SemaphoreType.DMA((5,)),
            pltpu.SemaphoreType.DMA((total, 9)),
            pltpu.SemaphoreType.DMA((total, 9)),
            pltpu.SemaphoreType.DMA((2 * layers + 6,)),
            pltpu.SemaphoreType.DMA((2 * layers + 6,)),
            pltpu.SemaphoreType.DMA((2, 4)),
            pltpu.SemaphoreType.DMA((2, 4)),
        ],
        compiler_params=pltpu.CompilerParams(has_side_effects=True, vmem_limit_bytes=60 << 20),
        name="backward_pass",
    )(top, last, w, rows, lse, qkv, kv, mix, flip, slope, unit, scale)


def swap(value, bit):
    return lax.ppermute(value, "batch", [(place, place ^ bit) for place in range(8)])


def take(value, index, axis):
    return lax.dynamic_index_in_dim(value, index, axis, keepdims=False)


def small_rows(biases, up_bias, gains):
    layers = biases.shape[0]
    rows = jnp.concatenate((biases, gains, up_bias.reshape(layers, 4, 32)), 1).astype(F32)
    wide = jnp.tile(rows.reshape(layers * 12, 32), (1, 4))
    lane = lax.broadcasted_iota(jnp.int32, wide.shape, 1)
    return jnp.where(lane // 32 == lax.axis_index("blk"), wide, 0.0)


def column_shards(
    hidden_in,
    mask_index,
    mask_count,
    replacement,
    out_grad,
    w_qkv,
    w_out,
    w_up,
    w_down,
    biases,
    up_bias,
    gains,
):
    batch = lax.axis_index("batch")
    z = lax.axis_index("blk")
    core = lax.rem(batch, 2)
    seq_count, block_len, width = hidden_in.shape
    layers = w_qkv.shape[0]
    slots = mask_index.shape[1]
    per = width // 32

    slot_ids = jnp.arange(slots, dtype=jnp.int32)
    used = slot_ids[None, :] < mask_count[:, None]
    slot_place = jnp.where(used, mask_index, -1)
    places = z * block_len + jnp.arange(block_len, dtype=jnp.int32)
    hits = slot_place[:, None, :] == places[None, :, None]
    placed = jnp.einsum("sbm,smd->sbd", hits.astype(BF), replacement, preferred_element_type=F32)
    first = jnp.where(jnp.any(hits, -1, keepdims=True), placed.astype(BF), hidden_in)

    mine = lax.rem(z, 2)
    came_grad = swap(take(out_grad, mine, 0), 1)
    came_place = swap(take(slot_place, mine, 0).astype(F32), 1)
    here = (z // 2) == core
    top_grad = jnp.where(here, take(out_grad, mine, 0), came_grad)
    top_place = jnp.where(here, take(slot_place, mine, 0), came_place.astype(jnp.int32))
    blocks = lax.rem(z - jnp.arange(4, dtype=jnp.int32) + 4, 4)
    token_place = (
        blocks[:, None] * block_len
        + core * (block_len // 2)
        + jnp.arange(block_len // 2, dtype=jnp.int32)[None, :]
    ).reshape(-1)
    top_hits = (token_place[:, None] == top_place[None, :]).astype(BF)
    upstream = jnp.dot(top_hits, top_grad, preferred_element_type=F32)

    results = forward_pass(first, w_qkv, w_out, w_up, w_down, small_rows(biases, up_bias, gains))
    last, grad, qkv, out, up, down, bias_rows, up_rows, gain_rows = backward_pass(
        upstream, results[1], (results[0],) + tuple(results[2:])
    )
    return (
        last,
        grad.astype(F32),
        qkv,
        out,
        up,
        down.reshape(layers, 4 * per, width),
        bias_rows,
        up_rows,
        gain_rows,
    )


def solution(mesh):
    fits = mesh.shape["batch"] == 8 and mesh.shape["blk"] == 4
    return jax.shard_map(
        column_shards if fits else general_shards,
        mesh=mesh,
        in_specs=(
            P(*BOTH, None),
            P("batch", None),
            P("batch"),
            P("batch", None, None),
            P("batch", None, None),
            P(None, BOTH, None),
            P(None, BOTH, None),
            P(None, BOTH, None),
            P(None, BOTH, None),
            P(None, None, BOTH),
            P(None, BOTH),
            P(None, None, BOTH),
        ),
        out_specs=(
            P(*BOTH, None),
            P(*BOTH, None),
            P(None, BOTH, None),
            P(None, BOTH, None),
            P(None, BOTH, None),
            P(None, BOTH, None),
            P(None, None, BOTH),
            P(None, BOTH),
            P(None, None, BOTH),
        ),
        check_vma=False,
    )
```
